32 devices in a mesh: rep: 4 (over y, x), shard: 8 (over z, core).
Axes of the slice: x: 2, y: 2, z: 4, core: 2. Of those that a mesh axis runs over, the one named last changes fastest.
Arguments:
- tokens: bfloat16 [4096, 768], P(('rep', 'shard')), may hold values from -6 to 6
- segments: int32 [32, 128], P(('rep', 'shard')), may hold values from 0 to 2, never falling along the last dimension, each value on 1 to 96 neighbouring positions
- cotangent: bfloat16 [4096, 768], P(('rep', 'shard')), may hold values from -6 to 6
- weights: float32 [9216, 768], P('shard'), may hold values from -10 to 10
- vectors: float32 [12, 768], P(None, 'shard'), may hold values from -2 to 2
- first_weights: float32 [9216, 768], P('shard'), may hold values from -40 to 40
- first_vectors: float32 [12, 768], P(None, 'shard'), may hold values from -40 to 40
- second_weights: float32 [9216, 768], P('shard'), may hold values from 2.048 to 8.192
- second_vectors: float32 [12, 768], P(None, 'shard'), may hold values from 2.048 to 8.192
Outputs:
- output: bfloat16 [4096, 768], P(('rep', 'shard'))
- grad_tokens: float32 [4096, 768], P(('rep', 'shard'))
- grad_weights: float32 [9216, 768], P('shard')
- grad_vectors: float32 [12, 768], P(None, 'shard')
- new_weights: float32 [9216, 768], P('shard')
- new_vectors: float32 [12, 768], P(None, 'shard')
- new_first_weights: float32 [9216, 768], P('shard')
- new_first_vectors: float32 [12, 768], P(None, 'shard')
- new_second_weights: float32 [9216, 768], P('shard')
- new_second_vectors: float32 [12, 768], P(None, 'shard')
The draws below stay inside these ranges and needn't reach their ends.
Inputs may be any that keep to these rules, and one draw needn't show every extreme that they name: `segments`: along each sequence the document numbers never fall; a document holds 1 to 96 positions, and one holds exactly that many.
All inputs are finite; a program needn't handle non-finite values.
Results may differ from the reference program's by a relative error of at most 0.024.
Values may be sent and summed in bfloat16 or wider, within the bound.
No kernel may reach another device: no remote copies, remote signals or barrier semaphores. Data moves between devices by JAX's collectives and lax.ppermute only.
A program may use at most 192 MiB of HBM per device.

```python
import math
import jax
import jax.numpy as jnp
import numpy as np
from jax import lax

D = 768
HEADS = 12
HEAD = 64
FF = 3072
SEQ = 128
STEP = 3
VEC = 12
HID = 768
R = 9216
SEQS = 32
TOKENS = 4096


def draw_weights(key, part):
    base = jnp.clip(jax.random.normal(jax.random.fold_in(key, 11), (R, D), jnp.float32), -4.0, 4.0)
    row_ids = lax.broadcasted_iota(jnp.int32, (R, 1), 0)
    fan_in = jnp.where(row_ids < 3 * HID, 1.0 * D, jnp.where(row_ids < 4 * HID, HID / 16.0, jnp.where(row_ids < 4 * HID + FF, 1.0 * D, 1.0 * FF)))
    return jnp.clip(base * lax.rsqrt(fan_in), -10.0, 10.0)


def draw_vectors(key, part):
    row_ids = lax.broadcasted_iota(jnp.int32, (VEC, D), 0)
    is_gain = (row_ids == 0) | (row_ids == 5)
    noise = jnp.clip(jax.random.normal(jax.random.fold_in(key, 22), (VEC, D), jnp.float32), -3.0, 3.0)
    gains = 1.0 + 0.2 * noise
    biases = 0.3 * noise
    return jnp.where(is_gain, gains, biases)


def levels(key, extent, cuts, low, high):
    level, own = 1.0, jax.random.fold_in(key, 6)
    for axis_at, blocks in cuts:
        heights = jnp.exp(jax.random.uniform(jax.random.fold_in(own, axis_at), (blocks,), jnp.float32, low / len(cuts), high / len(cuts)))
        level = level * jnp.repeat(heights, extent[axis_at] // blocks).reshape([-1 if axis == axis_at else 1 for axis in range(len(extent))])
    return level


def split_up(amount, total, most, skew):
    portions = [(1 << 20) // math.isqrt(grade ** skew) + 1 for grade in range(2, amount + 1)]
    rest, holding = total - most - (amount - 1), [1] * (amount - 1)
    while rest > 0:
        free = [i for i in range(amount - 1) if holding[i] < most]
        mass, budget = sum([portions[i] for i in free]), rest
        for i in free:
            addition = min(most - holding[i], max(1, budget * portions[i] // mass), rest)
            holding[i] = holding[i] + addition
            rest = rest - addition
    return np.array([most] + holding)


def ragged_sizes(stream_key, amount, total, most, skew):
    if amount == 2:
        one = jax.random.randint(stream_key, (), max(1, total - most), min(most, total - 1) + 1)
        return jnp.stack([one, total - one])
    sizes = jnp.asarray(split_up(amount, total, most, skew), jnp.int32)
    twos = (amount - 1) // 2
    donor, taker = sizes[1:1 + 2 * twos:2], sizes[2:2 + 2 * twos:2]
    slack = jnp.minimum(donor - 1, most - taker)
    passed = jax.random.randint(jax.random.fold_in(stream_key, 1), (twos,), 0, 1 << 20) % (slack + 1)
    sizes = sizes.at[1:1 + 2 * twos:2].set(donor - passed).at[2:2 + 2 * twos:2].set(taker + passed)
    return sizes[jax.random.permutation(jax.random.fold_in(stream_key, 2), amount)]


def gaussian(stream_key, dims, scale, reach, cuts=(), held_as=jnp.bfloat16):
    entries = jax.random.normal(stream_key, dims, jnp.float32) * scale
    if len(cuts) > 0:
        entries = levels(stream_key, dims, cuts, -0.22, 0.18) * entries
    return jnp.clip(entries, min=-reach, max=reach).astype(held_as)


def setup_inputs(seed: int = 0) -> dict:
    keys = jax.random.split(jax.random.key(seed), 10)
    tokens = gaussian(keys[0], (TOKENS, D), 1.0, 6.0, ((0, 32),))
    segments = jax.vmap(lambda own: jnp.searchsorted(jnp.cumsum(ragged_sizes(own, 3, SEQ, 3 * SEQ // 4, 0)), jnp.arange(SEQ), side="right"))(jax.random.split(keys[1], SEQS)).reshape((SEQS, SEQ)).astype(jnp.int32)
    cotangent = gaussian(keys[2], (TOKENS, D), 1.0, 6.0, ((0, 32),))
    weights = draw_weights(jax.random.fold_in(keys[9], 71), 0)
    vectors = draw_vectors(jax.random.fold_in(keys[9], 71), 0)
    first_weights = gaussian(keys[5], (R, D), (0.1 * TOKENS ** 0.5), 40.0, ((0, 8),), jnp.float32)
    first_vectors = gaussian(keys[6], (VEC, D), (0.1 * TOKENS ** 0.5), 40.0, ((1, 8),), jnp.float32)
    second_weights = jnp.clip(jnp.exp(math.log(8.192) - 1.3862944 * jax.random.uniform(keys[7], (R, D), jnp.float32) ** levels(keys[7], (R, D), ((0, 8),), -0.2, 0.2)), 2.048, 8.192)
    second_vectors = jnp.clip(jnp.exp(math.log(8.192) - 1.3862944 * jax.random.uniform(keys[8], (VEC, D), jnp.float32) ** levels(keys[8], (VEC, D), ((1, 8),), -0.2, 0.2)), 2.048, 8.192)
    return dict(tokens=tokens, segments=segments, cotangent=cotangent, weights=weights, vectors=vectors, first_weights=first_weights, first_vectors=first_vectors, second_weights=second_weights, second_vectors=second_vectors)


norm_eps = 1e-05
beta_one = 0.9
beta_two = 0.999
adam_eps = 1e-08
learn_rate = 0.2
decay_rate = 0.1
masked_score = -1e+30

def normalize(values):
    centred = values - lax.optimization_barrier(jnp.mean(values, axis=-1, keepdims=True))
    return centred * lax.rsqrt(lax.optimization_barrier(jnp.mean(centred * centred, axis=-1, keepdims=True)) + norm_eps)

def affine_norm(values, gain_vec, shift_vec):
    return normalize(values) * gain_vec + shift_vec

def gelu_tanh(values):
    return jax.nn.gelu(values, approximate=True)

def matmul(left_op, right_op):
    return jnp.dot(left_op, right_op, preferred_element_type=jnp.float32)

def matmul_nt(left_op, right_op):
    return jnp.dot(left_op, right_op.T, preferred_element_type=jnp.float32)

def matmul_tn(left_op, right_op):
    return jnp.dot(left_op.T, right_op, preferred_element_type=jnp.float32)

def product(pattern, left_op, right_op):
    return jnp.einsum(pattern, left_op.astype(jnp.float32), right_op.astype(jnp.float32))

def allowed_pairs(segments):
    length = segments.shape[1]
    places = lax.broadcasted_iota(jnp.int32, (length, length), 0)
    others = lax.broadcasted_iota(jnp.int32, (length, length), 1)
    causal = others <= places
    same_doc = segments[:, :, None] == segments[:, None, :]
    return (causal[None] & same_doc)[:, None]

def scores_of(query_rows, key_rows, allowed):
    raw_scores = product('sqhd,skhd->shqk', query_rows, key_rows) * HEAD ** (-0.5)
    return jnp.where(allowed, raw_scores, masked_score)

def forward(tokens, segments, w_bf, v_bf):
    seq_count, length = segments.shape
    tok_count = tokens.shape[0]
    head_shape = (seq_count, length, HEADS, HEAD)
    floats = v_bf.astype(jnp.float32)
    residual = tokens.astype(jnp.float32)
    normed_one = affine_norm(residual, floats[0], floats[1]).astype(jnp.bfloat16)
    projected = matmul_nt(normed_one, w_bf[:3 * HID])
    query_rows = (projected[:, :HID] + floats[2]).astype(jnp.bfloat16)
    key_rows = projected[:, HID:2 * HID].astype(jnp.bfloat16)
    value_rows = (projected[:, 2 * HID:] + floats[3]).astype(jnp.bfloat16)
    allowed = allowed_pairs(segments)
    scores = scores_of(query_rows.reshape(head_shape), key_rows.reshape(head_shape), allowed)
    row_max = lax.optimization_barrier(jnp.max(scores, axis=-1, keepdims=True))
    log_total = row_max + jnp.log(lax.optimization_barrier(jnp.sum(jnp.exp(scores - row_max), axis=-1, keepdims=True)))
    attn_probs = jnp.exp(scores - log_total).astype(jnp.bfloat16)
    mixed_heads = product('shqk,skhd->sqhd', attn_probs, value_rows.reshape(head_shape))
    attended = mixed_heads.reshape(tok_count, HID).astype(jnp.bfloat16)
    hidden_one = residual + matmul(attended, w_bf[3 * HID:4 * HID]) + floats[4]
    normed_two = affine_norm(hidden_one, floats[5], floats[6]).astype(jnp.bfloat16)
    pre_act = matmul_nt(normed_two, w_bf[4 * HID:4 * HID + FF]) + floats[7:11].reshape(FF)
    active = gelu_tanh(pre_act).astype(jnp.bfloat16)
    output = (hidden_one + matmul(active, w_bf[4 * HID + FF:]) + floats[11]).astype(jnp.bfloat16)
    kept_state = (residual, normed_one, query_rows, key_rows, value_rows, log_total, attended, hidden_one, normed_two, pre_act, active, floats)
    return (output, kept_state)

def backward(kept_state, cotangent, segments, w_bf):
    residual, normed_one, query_rows, key_rows, value_rows, log_total, attended, hidden_one, normed_two, pre_act, active, floats = kept_state
    seq_count, length = segments.shape
    tok_count = residual.shape[0]
    head_shape = (seq_count, length, HEADS, HEAD)
    grad_out = cotangent.astype(jnp.float32)
    grad_active = matmul_nt(cotangent, w_bf[4 * HID + FF:])
    grad_pre = jax.vjp(gelu_tanh, pre_act)[1](grad_active)[0]
    grad_pre_bf = grad_pre.astype(jnp.bfloat16)
    grad_normed_two = matmul(grad_pre_bf, w_bf[4 * HID:4 * HID + FF])
    norm_back_two = jax.vjp(affine_norm, hidden_one, floats[5], floats[6])[1]
    grad_h_part, grad_gain_two, grad_shift_two = norm_back_two(grad_normed_two)
    grad_hidden = grad_out + grad_h_part
    grad_hidden_bf = grad_hidden.astype(jnp.bfloat16)
    grad_attended = matmul_nt(grad_hidden_bf, w_bf[3 * HID:4 * HID]).astype(jnp.bfloat16)
    query_four = query_rows.reshape(head_shape)
    key_four = key_rows.reshape(head_shape)
    value_four = value_rows.reshape(head_shape)
    grad_att_four = grad_attended.reshape(head_shape)
    allowed = allowed_pairs(segments)
    scores = scores_of(query_four, key_four, allowed)
    attn_probs = jnp.exp(scores - log_total)
    probs_bf = attn_probs.astype(jnp.bfloat16)
    grad_probs = product('sqhd,skhd->shqk', grad_att_four, value_four)
    inner_sum = lax.optimization_barrier(jnp.sum(attn_probs * grad_probs, axis=-1, keepdims=True))
    grad_scores = (attn_probs * (grad_probs - inner_sum) * HEAD ** (-0.5)).astype(jnp.bfloat16)
    grad_query = product('shqk,skhd->sqhd', grad_scores, key_four).reshape(tok_count, HID)
    grad_keys = product('shqk,sqhd->skhd', grad_scores, query_four).reshape(tok_count, HID)
    grad_values = product('shqk,sqhd->skhd', probs_bf, grad_att_four).reshape(tok_count, HID)
    grad_proj = jnp.concatenate([grad_query, grad_keys, grad_values], axis=1)
    grad_proj_bf = grad_proj.astype(jnp.bfloat16)
    grad_normed_one = matmul(grad_proj_bf, w_bf[:3 * HID])
    norm_back_one = jax.vjp(affine_norm, residual, floats[0], floats[1])[1]
    grad_r_part, grad_gain_one, grad_shift_one = norm_back_one(grad_normed_one)
    grad_tokens = grad_hidden + grad_r_part
    bias_ff = lax.optimization_barrier(jnp.sum(grad_pre, axis=0)).reshape(FF // D, D)
    head_rows = jnp.stack([grad_gain_one, grad_shift_one, lax.optimization_barrier(jnp.sum(grad_query, axis=0)), lax.optimization_barrier(jnp.sum(grad_values, axis=0)), lax.optimization_barrier(jnp.sum(grad_hidden, axis=0)), grad_gain_two, grad_shift_two])
    grad_vec = jnp.concatenate([head_rows, bias_ff, lax.optimization_barrier(jnp.sum(grad_out, axis=0))[None]], axis=0)
    row_terms = jnp.concatenate([grad_proj_bf, attended, grad_pre_bf, active], axis=1)
    col_terms = jnp.stack([normed_one, grad_hidden_bf, normed_two, cotangent])
    return (grad_tokens, grad_vec, row_terms, col_terms)

def weight_grads(row_terms, col_terms):
    row_bounds = (0, 3 * HID, 4 * HID, 4 * HID + FF, R)
    pieces = [matmul_tn(row_terms[:, row_bounds[index]:row_bounds[index + 1]], col_terms[index]) for index in range(4)]
    return jnp.concatenate(pieces, axis=0)

def adam_update(param, first, second, grad, decay):
    new_first = beta_one * first + (1.0 - beta_one) * grad
    new_second = beta_two * second + (1.0 - beta_two) * grad * grad
    first_hat = new_first / (1.0 - beta_one ** STEP)
    second_hat = new_second / (1.0 - beta_two ** STEP)
    new_param = param - learn_rate * (first_hat / (jnp.sqrt(second_hat) + adam_eps) + decay * param)
    return (new_param, new_first, new_second)

def reference(tokens, segments, cotangent, weights, vectors, first_weights, first_vectors, second_weights, second_vectors):
    w_bf = weights.astype(jnp.bfloat16)
    v_bf = vectors.astype(jnp.bfloat16)
    per_block = 32 if SEQS % 32 == 0 else 1
    blocks = SEQS // per_block
    tok_blocks = tokens.reshape(blocks, per_block * SEQ, D)
    seg_blocks = segments.reshape(blocks, per_block, SEQ)
    cot_blocks = cotangent.reshape(blocks, per_block * SEQ, D)

    def block_step(totals, pieces):
        sum_w, sum_v = totals
        tok_piece, seg_piece, cot_piece = pieces
        output, kept_state = forward(tok_piece, seg_piece, w_bf, v_bf)
        grad_tok, grad_vec, row_terms, col_terms = backward(kept_state, cot_piece, seg_piece, w_bf)
        return ((sum_w + weight_grads(row_terms, col_terms), sum_v + grad_vec), (output, grad_tok))
    zero_sums = (jnp.zeros((R, D), jnp.float32), jnp.zeros((VEC, D), jnp.float32))
    (grad_w, grad_v), (outputs, grad_toks) = lax.scan(block_step, zero_sums, (tok_blocks, seg_blocks, cot_blocks))
    new_w, new_fw, new_sw = adam_update(weights, first_weights, second_weights, grad_w, decay_rate)
    new_v, new_fv, new_sv = adam_update(vectors, first_vectors, second_vectors, grad_v, 0.0)
    return (outputs.reshape(TOKENS, D), grad_toks.reshape(TOKENS, D), grad_w, grad_v, new_w, new_v, new_fw, new_fv, new_sw, new_sv)
```

```python
import functools
import math

import jax
import jax.numpy as jnp
from jax import lax
from jax.experimental import pallas as pl
from jax.experimental.pallas import tpu as pltpu
from jax.sharding import PartitionSpec as P

D = 768
HEADS = 12
HEAD = 64
FF = 3072
STEP = 3
HID = 768
R = 9216


norm_eps = 1e-05
beta_one = 0.9
beta_two = 0.999
adam_eps = 1e-08
learn_rate = 0.2
decay_rate = 0.1
masked_score = -1e30


def normalize(values):
    centred = values - jnp.mean(values, axis=-1, keepdims=True)
    return centred * lax.rsqrt(jnp.mean(centred * centred, axis=-1, keepdims=True) + norm_eps)


def affine_norm(values, gain_vec, shift_vec):
    return normalize(values) * gain_vec + shift_vec


def gelu_tanh(values):
    return jax.nn.gelu(values, approximate=True)


def matmul(left_op, right_op):
    return jnp.dot(left_op, right_op, preferred_element_type=jnp.float32)


def matmul_nt(left_op, right_op):
    return lax.dot_general(
        left_op, right_op, (((1,), (1,)), ((), ())), preferred_element_type=jnp.float32
    )


def matmul_tn(left_op, right_op):
    return lax.dot_general(
        left_op, right_op, (((0,), (0,)), ((), ())), preferred_element_type=jnp.float32
    )


def product(pattern, left_op, right_op):
    return jnp.einsum(pattern, left_op, right_op, preferred_element_type=jnp.float32)


def allowed_pairs(segments):
    length = segments.shape[1]
    places = lax.broadcasted_iota(jnp.int32, (length, length), 0)
    others = lax.broadcasted_iota(jnp.int32, (length, length), 1)
    causal = others <= places
    same_doc = segments[:, :, None] == segments[:, None, :]
    return (causal[None] & same_doc)[:, None]


def scores_of(query_rows, key_rows, allowed):
    raw_scores = product("sqhd,skhd->shqk", query_rows, key_rows) * HEAD ** (-0.5)
    return jnp.where(allowed, raw_scores, masked_score)


def forward(tokens, segments, w_bf, v_bf):
    seq_count, length = segments.shape
    tok_count = tokens.shape[0]
    head_shape = (seq_count, length, HEADS, HEAD)
    floats = v_bf.astype(jnp.float32)
    residual = tokens.astype(jnp.float32)
    normed_one = affine_norm(residual, floats[0], floats[1]).astype(jnp.bfloat16)
    projected = matmul_nt(normed_one, w_bf[: 3 * HID])
    query_rows = (projected[:, :HID] + floats[2]).astype(jnp.bfloat16)
    key_rows = projected[:, HID : 2 * HID].astype(jnp.bfloat16)
    value_rows = (projected[:, 2 * HID :] + floats[3]).astype(jnp.bfloat16)
    allowed = allowed_pairs(segments)
    scores = scores_of(query_rows.reshape(head_shape), key_rows.reshape(head_shape), allowed)
    row_max = jnp.max(scores, axis=-1, keepdims=True)
    log_total = row_max + jnp.log(jnp.sum(jnp.exp(scores - row_max), axis=-1, keepdims=True))
    attn_probs = jnp.exp(scores - log_total).astype(jnp.bfloat16)
    mixed_heads = product("shqk,skhd->sqhd", attn_probs, value_rows.reshape(head_shape))
    attended = mixed_heads.reshape(tok_count, HID).astype(jnp.bfloat16)
    hidden_one = residual + matmul(attended, w_bf[3 * HID : 4 * HID]) + floats[4]
    normed_two = affine_norm(hidden_one, floats[5], floats[6]).astype(jnp.bfloat16)
    pre_act = matmul_nt(normed_two, w_bf[4 * HID : 4 * HID + FF]) + floats[7:11].reshape(FF)
    active = gelu_tanh(pre_act).astype(jnp.bfloat16)
    output = (hidden_one + matmul(active, w_bf[4 * HID + FF :]) + floats[11]).astype(jnp.bfloat16)
    kept_state = (
        residual,
        normed_one,
        query_rows,
        key_rows,
        value_rows,
        log_total,
        attended,
        hidden_one,
        normed_two,
        pre_act,
        active,
        floats,
    )
    return (output, kept_state)


def backward(kept_state, cotangent, segments, w_bf):
    (
        residual,
        normed_one,
        query_rows,
        key_rows,
        value_rows,
        log_total,
        attended,
        hidden_one,
        normed_two,
        pre_act,
        active,
        floats,
    ) = kept_state
    seq_count, length = segments.shape
    tok_count = residual.shape[0]
    head_shape = (seq_count, length, HEADS, HEAD)
    grad_out = cotangent.astype(jnp.float32)
    grad_active = matmul_nt(cotangent, w_bf[4 * HID + FF :])
    grad_pre = jax.vjp(gelu_tanh, pre_act)[1](grad_active)[0]
    grad_pre_bf = grad_pre.astype(jnp.bfloat16)
    grad_normed_two = matmul(grad_pre_bf, w_bf[4 * HID : 4 * HID + FF])
    norm_back_two = jax.vjp(affine_norm, hidden_one, floats[5], floats[6])[1]
    grad_h_part, grad_gain_two, grad_shift_two = norm_back_two(grad_normed_two)
    grad_hidden = grad_out + grad_h_part
    grad_hidden_bf = grad_hidden.astype(jnp.bfloat16)
    grad_attended = matmul_nt(grad_hidden_bf, w_bf[3 * HID : 4 * HID]).astype(jnp.bfloat16)
    query_four = query_rows.reshape(head_shape)
    key_four = key_rows.reshape(head_shape)
    value_four = value_rows.reshape(head_shape)
    grad_att_four = grad_attended.reshape(head_shape)
    allowed = allowed_pairs(segments)
    scores = scores_of(query_four, key_four, allowed)
    attn_probs = jnp.exp(scores - log_total)
    probs_bf = attn_probs.astype(jnp.bfloat16)
    grad_probs = product("sqhd,skhd->shqk", grad_att_four, value_four)
    inner_sum = jnp.sum(attn_probs * grad_probs, axis=-1, keepdims=True)
    grad_scores = (attn_probs * (grad_probs - inner_sum) * HEAD ** (-0.5)).astype(jnp.bfloat16)
    grad_query = product("shqk,skhd->sqhd", grad_scores, key_four).reshape(tok_count, HID)
    grad_keys = product("shqk,sqhd->skhd", grad_scores, query_four).reshape(tok_count, HID)
    grad_values = product("shqk,sqhd->skhd", probs_bf, grad_att_four).reshape(tok_count, HID)
    grad_proj = jnp.concatenate([grad_query, grad_keys, grad_values], axis=1)
    grad_proj_bf = grad_proj.astype(jnp.bfloat16)
    grad_normed_one = matmul(grad_proj_bf, w_bf[: 3 * HID])
    norm_back_one = jax.vjp(affine_norm, residual, floats[0], floats[1])[1]
    grad_r_part, grad_gain_one, grad_shift_one = norm_back_one(grad_normed_one)
    grad_tokens = grad_hidden + grad_r_part
    bias_ff = jnp.sum(grad_pre, axis=0).reshape(FF // D, D)
    head_rows = jnp.stack(
        [
            grad_gain_one,
            grad_shift_one,
            jnp.sum(grad_query, axis=0),
            jnp.sum(grad_values, axis=0),
            jnp.sum(grad_hidden, axis=0),
            grad_gain_two,
            grad_shift_two,
        ]
    )
    grad_vec = jnp.concatenate([head_rows, bias_ff, jnp.sum(grad_out, axis=0)[None]], axis=0)
    row_terms = jnp.concatenate([grad_proj_bf, attended, grad_pre_bf, active], axis=1)
    col_terms = jnp.stack([normed_one, grad_hidden_bf, normed_two, cotangent])
    return (grad_tokens, grad_vec, row_terms, col_terms)


def weight_grads(row_terms, col_terms):
    row_bounds = (0, 3 * HID, 4 * HID, 4 * HID + FF, R)
    pieces = [
        matmul_tn(row_terms[:, row_bounds[index] : row_bounds[index + 1]], col_terms[index])
        for index in range(4)
    ]
    return jnp.concatenate(pieces, axis=0)


def adam_update(param, first, second, grad, decay):
    new_first = beta_one * first + (1.0 - beta_one) * grad
    new_second = beta_two * second + (1.0 - beta_two) * grad * grad
    first_hat = new_first / (1.0 - beta_one**STEP)
    second_hat = new_second / (1.0 - beta_two**STEP)
    new_param = param - learn_rate * (first_hat / (jnp.sqrt(second_hat) + adam_eps) + decay * param)
    return (new_param, new_first, new_second)


def bit_reverse(index, bits):
    out = index * 0
    for place in range(bits):
        out = out * 2 + (index >> place) % 2
    return out


class Links:
    def __init__(self, replicas, shards):
        self.replicas = replicas
        self.cores = 2
        self.chips = shards // self.cores
        self.bits = replicas.bit_length() - 1
        self.replica = lax.axis_index("rep")
        shard = lax.axis_index("shard")
        self.chip = shard // self.cores
        self.core = shard % self.cores

    @staticmethod
    def fits(replicas, shards, rows):
        power = replicas > 1 and replicas & (replicas - 1) == 0
        return shards == 8 and power and 2 * rows == 3 * HID

    def send(self, value, target):
        route = []
        for rep in range(self.replicas):
            for chip in range(self.chips):
                for core in range(self.cores):
                    goal = target(rep, chip, core)
                    if goal is None:
                        continue
                    start = (rep * self.chips + chip) * self.cores + core
                    stop = (goal[0] * self.chips + goal[1]) * self.cores + goal[2]
                    route.append((start, stop))
        return lax.ppermute(value, ("rep", "shard"), route)

    def swap_core(self, value):
        return self.send(value, lambda rep, chip, core: (rep, chip, 1 - core))

    def swap_bit(self, value, bit):
        return self.send(value, lambda rep, chip, core: (rep ^ (1 << bit), chip, core))

    def along(self, value, moves):
        table = dict(moves)
        return self.send(
            value, lambda rep, chip, core: (rep, table[chip], core) if chip in table else None
        )

    def bit_of(self, bit):
        return (self.replica >> bit) % 2

    def own_pieces(self, block):
        half = block.shape[0] // 2
        size = half // self.replicas
        first = lax.dynamic_slice_in_dim(block, self.replica * size, size)
        turned = bit_reverse(self.replica, self.bits)
        second = lax.dynamic_slice_in_dim(block, half + turned * size, size)
        return first, second

    def gather_replicas(self, first, second):
        for step in range(self.bits):
            low, high = step, self.bits - 1 - step
            got_first = self.swap_bit(first, low)
            got_second = self.swap_bit(second, high)
            first = jnp.where(
                self.bit_of(low) == 0,
                jnp.concatenate([first, got_first]),
                jnp.concatenate([got_first, first]),
            )
            second = jnp.where(
                self.bit_of(high) == 0,
                jnp.concatenate([second, got_second]),
                jnp.concatenate([got_second, second]),
            )
        return jnp.concatenate([first, second])

    def to_chip(self, piece, goal):
        first = {0: {1: 0, 3: 2}, 3: {0: 1, 2: 3}}.get(goal, {0: 1, 3: 2})
        second = {0: {2: 0}, 1: {2: 1}, 2: {1: 2}, 3: {1: 3}}[goal]
        piece = add_bf(piece, self.along(piece, first))
        return add_bf(piece, self.along(piece, second))

    def sum_all(self, value):
        value = value + self.swap_core(value)
        for bit in range(self.bits):
            value = value + self.swap_bit(value, bit)
        value = value + self.along(value, {0: 1, 1: 0, 2: 3, 3: 2})
        return value + self.along(value, {0: 2, 2: 0, 1: 3, 3: 1})


def add_bf(left, right):
    return (left.astype(jnp.float32) + right.astype(jnp.float32)).astype(jnp.bfloat16)


vector_pad = 16


def dot(left, right, left_dim, right_dim):
    return lax.dot_general(
        left,
        right,
        (((left_dim,), (right_dim,)), ((), ())),
        preferred_element_type=jnp.float32,
    )


def norm_parts(values):
    centred = values - jnp.mean(values, axis=-1, keepdims=True)
    scale = lax.rsqrt(jnp.mean(centred * centred, axis=-1, keepdims=True) + norm_eps)
    return centred * scale, scale


def norm_back(unit, scale, grad):
    inner = jnp.mean(grad, axis=-1, keepdims=True)
    outer = jnp.mean(grad * unit, axis=-1, keepdims=True)
    return scale * (grad - inner - unit * outer)


def row_sum(values):
    return jnp.sum(values, axis=0, keepdims=True)


def left_lanes(value):
    return lax.broadcasted_iota(jnp.int32, value.shape, 1) < HEAD


def head_parts(pair):
    left = left_lanes(pair)
    none = jnp.zeros_like(pair)
    return jnp.where(left, pair, none), jnp.where(left, none, pair)


def forward_kernel(
    rows,
    place,
    tok,
    cot,
    seg_col,
    seg_row,
    *rest,
):
    blocks = rest[:8]
    out, keep, send, dub, hidden, qkv, probs, vec_all, vec_out, w_out = rest[8:18]
    w_all, parts, terms, load_sem, part_sem, store_sem = rest[18:]
    core = place[4]
    loads, extras = [], []
    for slot in range(4):
        for side in range(2):
            number = place[slot] * 2 + (core if side == 0 else 1 - core)
            source = blocks[2 * slot + side]
            extra = pltpu.make_async_copy(
                source.at[pl.ds(rows, vector_pad)],
                parts.at[2 * slot + side],
                part_sem.at[2 * slot + side],
            )
            extra.start()
            extras.append(extra)
            start = pl.multiple_of(number * rows, rows)
            pltpu.make_async_copy(
                source.at[pl.ds(0, rows)], w_all.at[pl.ds(start, rows)], load_sem.at[number]
            ).start()

    def ready(number):
        span = pl.ds(number * rows, rows)
        pltpu.make_async_copy(blocks[0].at[pl.ds(0, rows)], w_all.at[span], load_sem.at[number]).wait()
        store = pltpu.make_async_copy(w_all.at[span], w_out.at[span], store_sem.at[number])
        store.start()
        return store

    for extra in extras:
        extra.wait()
    vec = parts[0].astype(jnp.float32)
    for index in range(1, 8):
        vec = vec + parts[index].astype(jnp.float32)
    vec_all[...] = vec

    def vector(index):
        return vec_all[index : index + 1, :]

    count = tok.shape[0]
    residual = tok[...].astype(jnp.float32)
    unit, _ = norm_parts(residual)
    n_one = (unit * vector(0) + vector(1)).astype(jnp.bfloat16)
    send[:, :D] = n_one
    stores = [ready(0), ready(1)]
    for index, bias in enumerate((vector(2), None, vector(3))):
        value = dot(n_one, w_all[index * HID : (index + 1) * HID], 1, 1)
        if bias is not None:
            value = value + bias
        qkv[:, index * HID : (index + 1) * HID] = value.astype(jnp.bfloat16)
    length = seg_row.shape[1]
    for seq in range(seg_row.shape[0]):
        span = slice(seq * length, (seq + 1) * length)
        order = lax.broadcasted_iota(jnp.int32, (length, length), 0)
        other = lax.broadcasted_iota(jnp.int32, (length, length), 1)
        allowed = (other <= order) & (seg_col[span, :] == seg_row[seq : seq + 1, :])
        for pair in range(HEADS // 2):
            lanes = slice(pair * 2 * HEAD, (pair + 1) * 2 * HEAD)
            key_pair = qkv[span, HID + lanes.start : HID + lanes.stop]
            value_pair = qkv[span, 2 * HID + lanes.start : 2 * HID + lanes.stop]
            mixed = []
            for half, query in enumerate(head_parts(qkv[span, lanes])):
                raw = dot(query, key_pair, 1, 1) * HEAD ** (-0.5)
                raw = jnp.where(allowed, raw, masked_score)
                top = jnp.max(raw, axis=-1, keepdims=True)
                total = jnp.sum(jnp.exp(raw - top), axis=-1, keepdims=True)
                prob = jnp.exp(raw - (top + jnp.log(total)))
                probs[seq * HEADS + 2 * pair + half] = prob
                mixed.append(dot(prob.astype(jnp.bfloat16), value_pair, 1, 0))
            terms[span, lanes] = jnp.where(left_lanes(mixed[0]), mixed[0], mixed[1]).astype(
                jnp.bfloat16
            )
    for number in range(2, 6):
        stores.append(ready(number))
    h_value = residual + dot(terms[:, :HID], w_all[3 * HID : 4 * HID], 1, 0) + vector(4)
    hidden[...] = h_value
    unit, _ = norm_parts(h_value)
    n_two = (unit * vector(5) + vector(6)).astype(jnp.bfloat16)
    send[:, D : 2 * D] = n_two
    send[:, 2 * D : 3 * D] = cot[...]
    for number in range(6, 8):
        stores.append(ready(number))
    result = h_value + vector(11)
    for index in range(FF // D):
        first = 4 * HID + index * D
        second = first + FF
        pre = dot(n_two, w_all[first : first + D], 1, 1) + vector(7 + index)
        squared = pre * pre
        root = math.sqrt(2.0 / math.pi)
        bent = jnp.tanh(root * (pre + 0.044715 * (pre * squared)))
        half = 0.5 * (1.0 + bent)
        active = (pre * half).astype(jnp.bfloat16)
        slope = half + 0.5 * pre * (1.0 - bent * bent) * (root * (1.0 + 3 * 0.044715 * squared))
        change = dot(cot[...], w_all[second : second + D], 1, 1) * slope
        change_bf = change.astype(jnp.bfloat16)
        dub[:, index * D : (index + 1) * D] = change_bf
        terms[:, HID + index * D : HID + (index + 1) * D] = change_bf
        terms[:, HID + FF + index * D : HID + FF + (index + 1) * D] = active
        vec_out[index : index + 1, :] = row_sum(change)
        result = result + dot(active, w_all[second : second + D], 1, 0)
    out[...] = result.astype(jnp.bfloat16)
    vec_out[4:5, :] = row_sum(cot[...].astype(jnp.float32))
    vec_out[5:8, :] = jnp.zeros((3, D), jnp.float32)
    for index in range(3):
        near = pl.multiple_of((2 * index + core) * rows, 128)
        away = pl.multiple_of((2 * index + 1 - core) * rows, 128)
        keep[:, index * rows : (index + 1) * rows] = terms[:, pl.ds(near, rows)]
        send[:, 3 * D + index * rows : 3 * D + (index + 1) * rows] = terms[:, pl.ds(away, rows)]
    for store in stores:
        store.wait()


def hidden_kernel(dub, hidden, cot, vec_all, w_all, dh, dh_bf, da, vec_out, w_one, w_out, sem):
    first = pltpu.make_async_copy(w_all.at[pl.ds(4 * HID, FF)], w_one, sem.at[0])
    second = pltpu.make_async_copy(w_all.at[pl.ds(3 * HID, HID)], w_out, sem.at[1])
    first.start()
    second.start()
    unit, scale = norm_parts(hidden[...])
    first.wait()
    back = dot(dub[...], w_one[...], 1, 0)
    vec_out[0:1, :] = row_sum(back * unit)
    vec_out[1:2, :] = row_sum(back)
    value = cot[...].astype(jnp.float32) + norm_back(unit, scale, back * vec_all[5:6, :])
    dh[...] = value
    vec_out[2:3, :] = row_sum(value)
    vec_out[3:8, :] = jnp.zeros((5, D), jnp.float32)
    rounded = value.astype(jnp.bfloat16)
    dh_bf[...] = rounded
    second.wait()
    da[...] = dot(rounded, w_out[...], 1, 1).astype(jnp.bfloat16)


def attention_kernel(
    rows,
    place,
    da,
    qkv,
    probs,
    dh,
    tok,
    vec_all,
    vec_first,
    vec_second,
    w_all,
    grad_tok,
    keep,
    send,
    vec_out,
    w_in,
    dqkv,
    sem,
):
    core = place[4]
    load = pltpu.make_async_copy(w_all.at[pl.ds(0, 3 * HID)], w_in, sem)
    load.start()
    heads_total = probs.shape[0]
    length = probs.shape[1]
    vec_out[2:4, :] = jnp.zeros((2, D), jnp.float32)
    for seq in range(heads_total // HEADS):
        span = slice(seq * length, (seq + 1) * length)
        for pair in range(HEADS // 2):
            lanes = slice(pair * 2 * HEAD, (pair + 1) * 2 * HEAD)
            query_pair = qkv[span, lanes]
            key_pair = qkv[span, HID + lanes.start : HID + lanes.stop]
            value_pair = qkv[span, 2 * HID + lanes.start : 2 * HID + lanes.stop]
            da_pair = da[span, lanes]
            got = []
            for half, da_head in enumerate(head_parts(da_pair)):
                prob = probs[seq * HEADS + 2 * pair + half]
                grad_prob = dot(da_head, value_pair, 1, 1)
                inner = jnp.sum(prob * grad_prob, axis=-1, keepdims=True)
                grad_score = (prob * (grad_prob - inner) * HEAD ** (-0.5)).astype(jnp.bfloat16)
                got.append(
                    (
                        dot(grad_score, key_pair, 1, 0),
                        dot(grad_score, query_pair, 0, 0),
                        dot(prob.astype(jnp.bfloat16), da_pair, 0, 0),
                    )
                )
            left = left_lanes(got[0][0])
            query_grad, key_grad, value_grad = [
                jnp.where(left, one, two) for one, two in zip(got[0], got[1])
            ]
            dqkv[span, lanes] = query_grad.astype(jnp.bfloat16)
            dqkv[span, HID + lanes.start : HID + lanes.stop] = key_grad.astype(jnp.bfloat16)
            dqkv[span, 2 * HID + lanes.start : 2 * HID + lanes.stop] = value_grad.astype(
                jnp.bfloat16
            )
            vec_out[2:3, lanes] = vec_out[2:3, lanes] + row_sum(query_grad)
            vec_out[3:4, lanes] = vec_out[3:4, lanes] + row_sum(value_grad)
    near = pl.multiple_of(core * rows, 128)
    away = pl.multiple_of((1 - core) * rows, 128)
    keep[...] = dqkv[:, pl.ds(near, rows)]
    send[...] = dqkv[:, pl.ds(away, rows)]
    unit, scale = norm_parts(tok[...].astype(jnp.float32))
    load.wait()
    back = dot(dqkv[...], w_in[...], 1, 0)
    grad_tok[...] = dh[...] + norm_back(unit, scale, back * vec_all[0:1, :])
    vec_out[0:1, :] = row_sum(back * unit)
    vec_out[1:2, :] = row_sum(back)
    vec_out[4:5, :] = vec_second[2:3, :]
    vec_out[5:7, :] = vec_second[0:2, :]
    vec_out[7:12, :] = vec_first[0:5, :]
    vec_out[12:16, :] = jnp.zeros((4, D), jnp.float32)


def product_kernel(split, which, place, keep, got, *rest):
    columns, (away_one, away_two, mine_one, mine_two) = rest[:-7], rest[-7:-3]
    left, right, whole = rest[-3:]
    count = keep.shape[0]
    rows = keep.shape[1]
    left[:count] = keep[...]
    left[count:] = got[...]
    core = place[4]

    def put(span, first, second):
        right[:count] = first
        right[count:] = second
        whole[span, :] = dot(left[:, span], right[...], 0, 0).astype(jnp.bfloat16)

    if split is None:
        put(slice(0, rows), columns[0][...], columns[1][...])
    else:
        plain, mixed = (slice(0, split), slice(split, rows))
        if which == 0:
            plain, mixed = mixed, plain
        put(plain, columns[0][...], columns[1][...])
        fixed = core == which
        put(
            mixed,
            jnp.where(fixed, columns[2][...], columns[0][...]),
            jnp.where(fixed, columns[3][...], columns[1][...]),
        )
    half = rows // 2
    part = half // 2
    high, low = place[5], place[6]
    away_one[...] = whole[pl.ds(pl.multiple_of((1 - high) * part, 16), part), :]
    mine_one[...] = whole[pl.ds(pl.multiple_of(high * part, 16), part), :]
    away_two[...] = whole[pl.ds(pl.multiple_of(half + (1 - low) * part, 16), part), :]
    mine_two[...] = whole[pl.ds(pl.multiple_of(half + low * part, 16), part), :]


any_spec = pl.BlockSpec(memory_space=pl.ANY)
vmem_spec = pl.BlockSpec(memory_space=pltpu.VMEM)
smem_spec = pl.BlockSpec(memory_space=pltpu.SMEM)
bf16, f32 = jnp.bfloat16, jnp.float32


def call(kernel, name, inputs, outputs, scratch, flops, moved):
    return pl.pallas_call(
        kernel,
        name=name,
        grid=(1,),
        in_specs=[spec for _, spec in inputs],
        out_specs=[spec for _, _, spec in outputs],
        out_shape=[jax.ShapeDtypeStruct(shape, kind) for shape, kind, _ in outputs],
        scratch_shapes=scratch,
        compiler_params=pltpu.CompilerParams(vmem_limit_bytes=60 * 1024 * 1024),
        cost_estimate=pl.CostEstimate(flops=flops, bytes_accessed=moved, transcendentals=0),
    )(*[value for value, _ in inputs])


def lane_block(array, width, index):
    return array, pl.BlockSpec((array.shape[0], width), lambda step: (0, index))


def after(kernel, inputs, waits):
    count, extra = len(inputs), len(waits)

    def body(*refs):
        kernel(*refs[:count], *refs[count + extra :])

    return body, inputs + [(value, any_spec) for value in waits]


def parameter_blocks(links, weights, vectors):
    block = weights.astype(bf16)
    shards = links.chips * links.cores
    width = vectors.shape[1]
    number = links.chip * links.cores + links.core
    location = lax.broadcasted_iota(jnp.int32, (vectors.shape[0], width * shards), 1) // width
    spread = jnp.where(location == number, jnp.tile(vectors, (1, shards)), 0.0)
    spread = jnp.pad(spread, ((0, vector_pad - vectors.shape[0]), (0, 0))).astype(bf16)
    first, second = links.own_pieces(block)
    size = first.shape[0]
    mine = jnp.concatenate([first, second, spread])
    inner = (links.chip == 1) | (links.chip == 2)
    near = links.along(mine, {0: 1, 1: 0, 2: 3, 3: 2})
    middle = links.along(mine, {1: 2, 2: 1})
    outward = links.along(middle, {1: 0, 2: 3})
    across = links.along(near, {1: 2, 2: 1})
    far = links.along(across, {1: 0, 2: 3})
    slots = (near, jnp.where(inner, middle, outward), jnp.where(inner, across, far))
    wholes = [jnp.concatenate([block, spread])]
    for slot in slots:
        whole = links.gather_replicas(slot[:size], slot[size : 2 * size])
        wholes.append(jnp.concatenate([whole, slot[2 * size :]]))
    blocks = []
    for whole in wholes:
        blocks += [whole, links.swap_core(whole)]
    return blocks


def scatter_rest(links, mine, got):
    parts = [add_bf(one, two) for one, two in zip(mine, got)]
    for step in range(1, links.bits):
        bits = (links.bits - 1 - step, step)
        size = parts[0].shape[0] // 2
        other = []
        for part, bit in zip(parts, bits):
            away = lax.dynamic_slice_in_dim(part, (1 - links.bit_of(bit)) * size, size)
            other.append(links.swap_bit(away, bit))
        parts = [
            add_bf(lax.dynamic_slice_in_dim(part, links.bit_of(bit) * size, size), add)
            for part, bit, add in zip(parts, bits, other)
        ]
    return jnp.concatenate(parts)


def direct_step(links, tokens, segments, cotangent, weights, vectors):
    count = tokens.shape[0]
    rows = weights.shape[0]
    blocks = parameter_blocks(links, weights, vectors)
    low = links.chip < links.chips // 2
    place = jnp.stack(
        [
            links.chip,
            links.chip ^ 1,
            jnp.where(low, 2, 1),
            jnp.where(low, 3, 0),
            links.core,
            links.bit_of(links.bits - 1),
            links.bit_of(0),
            links.core,
        ]
    ).astype(jnp.int32)
    ends = (place, smem_spec)
    total_rows = rows * links.chips * links.cores
    pairs = segments.shape[0] * HEADS
    length = segments.shape[1]
    matmul_cost = 2 * count * total_rows * D

    def full(*arrays):
        return [(array, vmem_spec) for array in arrays]

    out, keep, send, dub, hidden, qkv, probs, vec_all, vec_first, w_all = call(
        functools.partial(forward_kernel, rows),
        "forward",
        [ends]
        + full(tokens, cotangent, segments.reshape(count, 1), segments)
        + [(block, any_spec) for block in blocks],
        [
            ((count, D), bf16, vmem_spec),
            ((count, 3 * rows), bf16, vmem_spec),
            ((count, 3 * D + 3 * rows), bf16, vmem_spec),
            ((count, FF), bf16, vmem_spec),
            ((count, D), f32, vmem_spec),
            ((count, 3 * HID), bf16, vmem_spec),
            ((pairs, length, length), f32, vmem_spec),
            ((vector_pad, D), f32, vmem_spec),
            ((8, D), f32, vmem_spec),
            ((total_rows, D), bf16, any_spec),
        ],
        [
            pltpu.VMEM((total_rows, D), bf16),
            pltpu.VMEM((8, vector_pad, D), bf16),
            pltpu.VMEM((count, HID + 2 * FF), bf16),
            pltpu.SemaphoreType.DMA((8,)),
            pltpu.SemaphoreType.DMA((8,)),
            pltpu.SemaphoreType.DMA((8,)),
        ],
        matmul_cost * 4 // 3,
        6 * total_rows * D,
    )
    got = links.swap_core(send)

    def product(name, index, sources, split=None, which=0, near=keep, far=got, offset=2, waits=()):
        columns = []
        for own, other, lane in sources:
            columns += [lane_block(own, D, lane[0]), lane_block(other, D, lane[1])]
        far_index = index + offset
        kernel, inputs = after(
            functools.partial(product_kernel, split, which),
            [ends, lane_block(near, rows, index), lane_block(far, rows, far_index)] + columns,
            list(waits),
        )
        return call(
            kernel,
            name,
            inputs,
            [((rows // 4, D), bf16, vmem_spec)] * 4,
            [
                pltpu.VMEM((2 * count, rows), bf16),
                pltpu.VMEM((2 * count, D), bf16),
                pltpu.VMEM((rows, D), bf16),
            ],
            4 * count * rows * D,
            6 * rows * D,
        )

    def first_hop(parts):
        away_one, away_two, mine_one, mine_two = parts
        arrived = (
            links.swap_bit(away_one, links.bits - 1),
            links.swap_bit(away_two, 0),
        )
        return (mine_one, mine_two), arrived

    n_one, n_two, dy = [(send, got, (index, index)) for index in range(3)]
    product_three = product("product_three", 2, [dy])
    tail_rows = 4 * HID + FF - 5 * rows
    product_two = product("product_two", 1, [n_two, dy], tail_rows, 1)
    kernel, inputs = after(
        hidden_kernel,
        full(dub, hidden, cotangent, vec_all) + [(w_all, any_spec)],
        [product_two[0]],
    )
    dh, dh_bf, da, vec_second = call(
        kernel,
        "hidden",
        inputs,
        [
            ((count, D), f32, vmem_spec),
            ((count, D), bf16, vmem_spec),
            ((count, HID), bf16, vmem_spec),
            ((8, D), f32, vmem_spec),
        ],
        [
            pltpu.VMEM((FF, D), bf16),
            pltpu.VMEM((HID, D), bf16),
            pltpu.SemaphoreType.DMA((2,)),
        ],
        matmul_cost * 5 // 12,
        2 * (FF + HID) * D,
    )
    dh_got = links.swap_core(dh_bf)
    out_rows = 4 * HID - 2 * rows
    product_one = product(
        "product_one", 0, [n_two, (dh_bf, dh_got, (0, 0))], out_rows, 0
    )
    kernel, inputs = after(
        functools.partial(attention_kernel, rows),
        [ends]
        + full(da, qkv, probs, dh, tokens, vec_all, vec_first, vec_second)
        + [(w_all, any_spec)],
        [product_one[0]],
    )
    grad_tok, keep_in, send_in, vec_sum = call(
        kernel,
        "attention",
        inputs,
        [
            ((count, D), f32, vmem_spec),
            ((count, rows), bf16, vmem_spec),
            ((count, rows), bf16, vmem_spec),
            ((vector_pad, D), f32, vmem_spec),
        ],
        [
            pltpu.VMEM((3 * HID, D), bf16),
            pltpu.VMEM((count, 3 * HID), bf16),
            pltpu.SemaphoreType.DMA,
        ],
        matmul_cost * 3 // 12,
        2 * 3 * HID * D,
    )
    got_in = links.swap_core(send_in)
    product_zero = product(
        "product_zero", 0, [n_one], near=keep_in, far=got_in, offset=0
    )
    mine = None
    for goal, parts in ((3, product_three), (2, product_two), (1, product_one), (0, product_zero)):
        piece = links.to_chip(scatter_rest(links, *first_hop(parts)), goal)
        mine = piece if mine is None else jnp.where(links.chip == goal, piece, mine)
    half = mine.shape[0] // 2
    grad_w = links.gather_replicas(mine[:half], mine[half:]).astype(f32)
    width = vectors.shape[1]
    all_v = links.sum_all(vec_sum)
    grad_v = lax.dynamic_slice_in_dim(all_v, lax.axis_index("shard") * width, width, 1)
    return out, grad_tok, grad_w, grad_v[: vectors.shape[0]]


def per_device(
    replicas,
    shards,
    tokens,
    segments,
    cotangent,
    weights,
    vectors,
    first_weights,
    first_vectors,
    second_weights,
    second_vectors,
):
    if Links.fits(replicas, shards, weights.shape[0]):
        output, grad_tokens, grad_w, grad_v = direct_step(
            Links(replicas, shards), tokens, segments, cotangent, weights, vectors
        )
    else:
        w_full = lax.all_gather(weights.astype(jnp.bfloat16), "shard", axis=0, tiled=True)
        v_full = lax.all_gather(vectors.astype(jnp.bfloat16), "shard", axis=1, tiled=True)
        output, kept_state = forward(tokens, segments, w_full, v_full)
        grad_tokens, grad_vec, row_terms, col_terms = backward(
            kept_state, cotangent, segments, w_full
        )
        local_grad = weight_grads(row_terms, col_terms).astype(jnp.bfloat16)
        own_w = lax.psum_scatter(local_grad, "shard", scatter_dimension=0, tiled=True)
        own_v = lax.psum_scatter(
            grad_vec.astype(jnp.bfloat16), "shard", scatter_dimension=1, tiled=True
        )
        grad_w = lax.psum(own_w, "rep").astype(jnp.float32)
        grad_v = lax.psum(own_v, "rep").astype(jnp.float32)
    new_w, new_fw, new_sw = adam_update(weights, first_weights, second_weights, grad_w, decay_rate)
    new_v, new_fv, new_sv = adam_update(vectors, first_vectors, second_vectors, grad_v, 0.0)
    return (output, grad_tokens, grad_w, grad_v, new_w, new_v, new_fw, new_fv, new_sw, new_sv)


def solution(mesh):
    placed = (
        P(("rep", "shard"), None),
        P(("rep", "shard"), None),
        P(("rep", "shard"), None),
        P("shard", None),
        P(None, "shard"),
        P("shard", None),
        P(None, "shard"),
        P("shard", None),
        P(None, "shard"),
    )
    return jax.shard_map(
        functools.partial(per_device, mesh.shape["rep"], mesh.shape["shard"]),
        mesh=mesh,
        in_specs=placed,
        out_specs=(
            P(("rep", "shard"), None),
            P(("rep", "shard"), None),
            P("shard", None),
            P(None, "shard"),
            P("shard", None),
            P(None, "shard"),
            P("shard", None),
            P(None, "shard"),
            P("shard", None),
            P(None, "shard"),
        ),
        check_vma=False,
    )
```

```python
import functools
import math

import jax
import jax.numpy as jnp
from jax import lax
from jax.experimental import pallas as pl
from jax.experimental.pallas import tpu as pltpu
from jax.sharding import PartitionSpec as P

D = 768
HEADS = 12
HEAD = 64
FF = 3072
STEP = 3
HID = 768
R = 9216


norm_eps = 1e-05
beta_one = 0.9
beta_two = 0.999
adam_eps = 1e-08
learn_rate = 0.2
decay_rate = 0.1
masked_score = -1e30


def normalize(values):
    centred = values - jnp.mean(values, axis=-1, keepdims=True)
    return centred * lax.rsqrt(jnp.mean(centred * centred, axis=-1, keepdims=True) + norm_eps)


def affine_norm(values, gain_vec, shift_vec):
    return normalize(values) * gain_vec + shift_vec


def gelu_tanh(values):
    return jax.nn.gelu(values, approximate=True)


def matmul(left_op, right_op):
    return jnp.dot(left_op, right_op, preferred_element_type=jnp.float32)


def matmul_nt(left_op, right_op):
    return lax.dot_general(
        left_op, right_op, (((1,), (1,)), ((), ())), preferred_element_type=jnp.float32
    )


def matmul_tn(left_op, right_op):
    return lax.dot_general(
        left_op, right_op, (((0,), (0,)), ((), ())), preferred_element_type=jnp.float32
    )


def product(pattern, left_op, right_op):
    return jnp.einsum(pattern, left_op, right_op, preferred_element_type=jnp.float32)


def allowed_pairs(segments):
    length = segments.shape[1]
    places = lax.broadcasted_iota(jnp.int32, (length, length), 0)
    others = lax.broadcasted_iota(jnp.int32, (length, length), 1)
    causal = others <= places
    same_doc = segments[:, :, None] == segments[:, None, :]
    return (causal[None] & same_doc)[:, None]


def scores_of(query_rows, key_rows, allowed):
    raw_scores = product("sqhd,skhd->shqk", query_rows, key_rows) * HEAD ** (-0.5)
    return jnp.where(allowed, raw_scores, masked_score)


def forward(tokens, segments, w_bf, v_bf):
    seq_count, length = segments.shape
    tok_count = tokens.shape[0]
    head_shape = (seq_count, length, HEADS, HEAD)
    floats = v_bf.astype(jnp.float32)
    residual = tokens.astype(jnp.float32)
    normed_one = affine_norm(residual, floats[0], floats[1]).astype(jnp.bfloat16)
    projected = matmul_nt(normed_one, w_bf[: 3 * HID])
    query_rows = (projected[:, :HID] + floats[2]).astype(jnp.bfloat16)
    key_rows = projected[:, HID : 2 * HID].astype(jnp.bfloat16)
    value_rows = (projected[:, 2 * HID :] + floats[3]).astype(jnp.bfloat16)
    allowed = allowed_pairs(segments)
    scores = scores_of(query_rows.reshape(head_shape), key_rows.reshape(head_shape), allowed)
    row_max = jnp.max(scores, axis=-1, keepdims=True)
    log_total = row_max + jnp.log(jnp.sum(jnp.exp(scores - row_max), axis=-1, keepdims=True))
    attn_probs = jnp.exp(scores - log_total).astype(jnp.bfloat16)
    mixed_heads = product("shqk,skhd->sqhd", attn_probs, value_rows.reshape(head_shape))
    attended = mixed_heads.reshape(tok_count, HID).astype(jnp.bfloat16)
    hidden_one = residual + matmul(attended, w_bf[3 * HID : 4 * HID]) + floats[4]
    normed_two = affine_norm(hidden_one, floats[5], floats[6]).astype(jnp.bfloat16)
    pre_act = matmul_nt(normed_two, w_bf[4 * HID : 4 * HID + FF]) + floats[7:11].reshape(FF)
    active = gelu_tanh(pre_act).astype(jnp.bfloat16)
    output = (hidden_one + matmul(active, w_bf[4 * HID + FF :]) + floats[11]).astype(jnp.bfloat16)
    kept_state = (
        residual,
        normed_one,
        query_rows,
        key_rows,
        value_rows,
        log_total,
        attended,
        hidden_one,
        normed_two,
        pre_act,
        active,
        floats,
    )
    return (output, kept_state)


def backward(kept_state, cotangent, segments, w_bf):
    (
        residual,
        normed_one,
        query_rows,
        key_rows,
        value_rows,
        log_total,
        attended,
        hidden_one,
        normed_two,
        pre_act,
        active,
        floats,
    ) = kept_state
    seq_count, length = segments.shape
    tok_count = residual.shape[0]
    head_shape = (seq_count, length, HEADS, HEAD)
    grad_out = cotangent.astype(jnp.float32)
    grad_active = matmul_nt(cotangent, w_bf[4 * HID + FF :])
    grad_pre = jax.vjp(gelu_tanh, pre_act)[1](grad_active)[0]
    grad_pre_bf = grad_pre.astype(jnp.bfloat16)
    grad_normed_two = matmul(grad_pre_bf, w_bf[4 * HID : 4 * HID + FF])
    norm_back_two = jax.vjp(affine_norm, hidden_one, floats[5], floats[6])[1]
    grad_h_part, grad_gain_two, grad_shift_two = norm_back_two(grad_normed_two)
    grad_hidden = grad_out + grad_h_part
    grad_hidden_bf = grad_hidden.astype(jnp.bfloat16)
    grad_attended = matmul_nt(grad_hidden_bf, w_bf[3 * HID : 4 * HID]).astype(jnp.bfloat16)
    query_four = query_rows.reshape(head_shape)
    key_four = key_rows.reshape(head_shape)
    value_four = value_rows.reshape(head_shape)
    grad_att_four = grad_attended.reshape(head_shape)
    allowed = allowed_pairs(segments)
    scores = scores_of(query_four, key_four, allowed)
    attn_probs = jnp.exp(scores - log_total)
    probs_bf = attn_probs.astype(jnp.bfloat16)
    grad_probs = product("sqhd,skhd->shqk", grad_att_four, value_four)
    inner_sum = jnp.sum(attn_probs * grad_probs, axis=-1, keepdims=True)
    grad_scores = (attn_probs * (grad_probs - inner_sum) * HEAD ** (-0.5)).astype(jnp.bfloat16)
    grad_query = product("shqk,skhd->sqhd", grad_scores, key_four).reshape(tok_count, HID)
    grad_keys = product("shqk,sqhd->skhd", grad_scores, query_four).reshape(tok_count, HID)
    grad_values = product("shqk,sqhd->skhd", probs_bf, grad_att_four).reshape(tok_count, HID)
    grad_proj = jnp.concatenate([grad_query, grad_keys, grad_values], axis=1)
    grad_proj_bf = grad_proj.astype(jnp.bfloat16)
    grad_normed_one = matmul(grad_proj_bf, w_bf[: 3 * HID])
    norm_back_one = jax.vjp(affine_norm, residual, floats[0], floats[1])[1]
    grad_r_part, grad_gain_one, grad_shift_one = norm_back_one(grad_normed_one)
    grad_tokens = grad_hidden + grad_r_part
    bias_ff = jnp.sum(grad_pre, axis=0).reshape(FF // D, D)
    head_rows = jnp.stack(
        [
            grad_gain_one,
            grad_shift_one,
            jnp.sum(grad_query, axis=0),
            jnp.sum(grad_values, axis=0),
            jnp.sum(grad_hidden, axis=0),
            grad_gain_two,
            grad_shift_two,
        ]
    )
    grad_vec = jnp.concatenate([head_rows, bias_ff, jnp.sum(grad_out, axis=0)[None]], axis=0)
    row_terms = jnp.concatenate([grad_proj_bf, attended, grad_pre_bf, active], axis=1)
    col_terms = jnp.stack([normed_one, grad_hidden_bf, normed_two, cotangent])
    return (grad_tokens, grad_vec, row_terms, col_terms)


def weight_grads(row_terms, col_terms):
    row_bounds = (0, 3 * HID, 4 * HID, 4 * HID + FF, R)
    pieces = [
        matmul_tn(row_terms[:, row_bounds[index] : row_bounds[index + 1]], col_terms[index])
        for index in range(4)
    ]
    return jnp.concatenate(pieces, axis=0)


def adam_update(param, first, second, grad, decay):
    new_first = beta_one * first + (1.0 - beta_one) * grad
    new_second = beta_two * second + (1.0 - beta_two) * grad * grad
    first_hat = new_first / (1.0 - beta_one**STEP)
    second_hat = new_second / (1.0 - beta_two**STEP)
    new_param = param - learn_rate * (first_hat / (jnp.sqrt(second_hat) + adam_eps) + decay * param)
    return (new_param, new_first, new_second)


def bit_reverse(index, bits):
    out = index * 0
    for place in range(bits):
        out = out * 2 + (index >> place) % 2
    return out


class Links:
    def __init__(self, replicas, shards):
        self.replicas = replicas
        self.cores = 2
        self.chips = shards // self.cores
        self.bits = replicas.bit_length() - 1
        self.replica = lax.axis_index("rep")
        shard = lax.axis_index("shard")
        self.chip = shard // self.cores
        self.core = shard % self.cores

    @staticmethod
    def fits(replicas, shards, rows):
        power = replicas > 2 and replicas & (replicas - 1) == 0
        return shards == 8 and power and 2 * rows == 3 * HID

    def send(self, value, target):
        route = []
        for rep in range(self.replicas):
            for chip in range(self.chips):
                for core in range(self.cores):
                    goal = target(rep, chip, core)
                    if goal is None:
                        continue
                    start = (rep * self.chips + chip) * self.cores + core
                    stop = (goal[0] * self.chips + goal[1]) * self.cores + goal[2]
                    route.append((start, stop))
        return lax.ppermute(value, ("rep", "shard"), route)

    def swap_core(self, value):
        return self.send(value, lambda rep, chip, core: (rep, chip, 1 - core))

    def swap_both(self, value, bit):
        return self.send(value, lambda rep, chip, core: (rep ^ (1 << bit), chip, 1 - core))

    def swap_bit(self, value, bit):
        return self.send(value, lambda rep, chip, core: (rep ^ (1 << bit), chip, core))

    def along(self, value, moves):
        table = dict(moves)
        return self.send(
            value, lambda rep, chip, core: (rep, table[chip], core) if chip in table else None
        )

    def bit_of(self, bit):
        return (self.replica >> bit) % 2

    def own_pieces(self, block):
        half = block.shape[0] // 2
        size = half // self.replicas
        first = lax.dynamic_slice_in_dim(block, self.replica * size, size)
        turned = bit_reverse(self.replica, self.bits)
        second = lax.dynamic_slice_in_dim(block, half + turned * size, size)
        return first, second

    def gather_replicas(self, first, second):
        for step in range(self.bits):
            low, high = step, self.bits - 1 - step
            got_first = self.swap_bit(first, low)
            got_second = self.swap_bit(second, high)
            first = jnp.where(
                self.bit_of(low) == 0,
                jnp.concatenate([first, got_first]),
                jnp.concatenate([got_first, first]),
            )
            second = jnp.where(
                self.bit_of(high) == 0,
                jnp.concatenate([second, got_second]),
                jnp.concatenate([got_second, second]),
            )
        return jnp.concatenate([first, second])

    def gather_positions(self, piece):
        size = piece.shape[0] // 2
        first, second = piece[:size], piece[size:]
        for step in range(self.bits):
            high, low = self.bits - 1 - step, step
            got_first = self.swap_bit(first, high)
            got_second = self.swap_bit(second, low)
            first = jnp.where(
                self.bit_of(high) == 0,
                jnp.concatenate([first, got_first]),
                jnp.concatenate([got_first, first]),
            )
            second = jnp.where(
                self.bit_of(low) == 0,
                jnp.concatenate([second, got_second]),
                jnp.concatenate([got_second, second]),
            )
        parts = []
        for position in range(self.replicas):
            turned = bit_reverse(position, self.bits)
            parts.append(first[position * size : (position + 1) * size])
            parts.append(second[turned * size : (turned + 1) * size])
        return jnp.concatenate(parts)

    def to_chip(self, piece, goal):
        first = {0: {1: 0, 3: 2}, 3: {0: 1, 2: 3}}.get(goal, {0: 1, 3: 2})
        second = {0: {2: 0}, 1: {2: 1}, 2: {1: 2}, 3: {1: 3}}[goal]
        piece = add_bf(piece, self.along(piece, first))
        return add_bf(piece, self.along(piece, second))

    def sum_all(self, value):
        value = value + self.swap_core(value)
        for bit in range(self.bits):
            value = value + self.swap_bit(value, bit)
        value = value + self.along(value, {0: 1, 1: 0, 2: 3, 3: 2})
        return value + self.along(value, {0: 2, 2: 0, 1: 3, 3: 1})


def add_bf(left, right):
    return (left.astype(jnp.float32) + right.astype(jnp.float32)).astype(jnp.bfloat16)


vector_pad = 16


def dot(left, right, left_dim, right_dim):
    return lax.dot_general(
        left,
        right,
        (((left_dim,), (right_dim,)), ((), ())),
        preferred_element_type=jnp.float32,
    )


def norm_parts(values):
    centred = values - jnp.mean(values, axis=-1, keepdims=True)
    scale = lax.rsqrt(jnp.mean(centred * centred, axis=-1, keepdims=True) + norm_eps)
    return centred * scale, scale


def norm_back(unit, scale, grad):
    inner = jnp.mean(grad, axis=-1, keepdims=True)
    outer = jnp.mean(grad * unit, axis=-1, keepdims=True)
    return scale * (grad - inner - unit * outer)


def row_sum(values):
    return jnp.sum(values, axis=0, keepdims=True)


def left_lanes(value):
    return lax.broadcasted_iota(jnp.int32, value.shape, 1) < HEAD


def head_parts(pair):
    left = left_lanes(pair)
    none = jnp.zeros_like(pair)
    return jnp.where(left, pair, none), jnp.where(left, none, pair)


def load_blocks(place, blocks, rows, target, sem, first, last):
    for slot in range(4):
        chip = place[slot]

        @pl.when((chip >= first) & (chip < last))
        def _():
            for side in range(2):
                core = place[4] if side == 0 else 1 - place[4]
                number = (chip - first) * 2 + core
                start = pl.multiple_of(number * rows, rows)
                pltpu.make_async_copy(
                    blocks[2 * slot + side].at[pl.ds(0, rows)],
                    target.at[pl.ds(start, rows)],
                    sem.at[number],
                ).start()

    def ready(*numbers):
        for number in numbers:
            index = number - 2 * first
            pltpu.make_async_copy(
                blocks[0].at[pl.ds(0, rows)],
                target.at[pl.ds(index * rows, rows)],
                sem.at[index],
            ).wait()

    return ready


def spread_terms(place, terms, rows, first, outs):
    core, across = place[4], place[5]
    wide = outs[0].shape[1]
    for index, out in enumerate(outs):
        block = core if index % 2 == 0 else 1 - core
        side = across if index < 2 else 1 - across
        start = pl.multiple_of(first + block * rows + side * (rows - wide), 128)
        out[...] = terms[:, pl.ds(start, wide)]


def query_kernel(rows, place, tok, seg_col, seg_row, *rest):
    blocks = rest[:8]
    n_out, qkv, probs, att, vec_all, w_in, parts, load_sem, part_sem = rest[8:]
    extras = []
    for index in range(8):
        extra = pltpu.make_async_copy(
            blocks[index].at[pl.ds(rows, vector_pad)], parts.at[index], part_sem.at[index]
        )
        extra.start()
        extras.append(extra)
    ready = load_blocks(place, blocks, rows, w_in, load_sem, 0, 1)
    unit, _ = norm_parts(tok[...].astype(jnp.float32))
    for extra in extras:
        extra.wait()
    vec = parts[0].astype(jnp.float32)
    for index in range(1, 8):
        vec = vec + parts[index].astype(jnp.float32)
    vec_all[...] = vec
    n_one = (unit * vec_all[0:1, :] + vec_all[1:2, :]).astype(jnp.bfloat16)
    n_out[...] = n_one
    ready(0, 1)
    for index, bias in enumerate((vec_all[2:3, :], None, vec_all[3:4, :])):
        value = dot(n_one, w_in[index * HID : (index + 1) * HID], 1, 1)
        if bias is not None:
            value = value + bias
        qkv[:, index * HID : (index + 1) * HID] = value.astype(jnp.bfloat16)
    length = seg_row.shape[1]
    for seq in range(seg_row.shape[0]):
        span = slice(seq * length, (seq + 1) * length)
        order = lax.broadcasted_iota(jnp.int32, (length, length), 0)
        other = lax.broadcasted_iota(jnp.int32, (length, length), 1)
        allowed = (other <= order) & (seg_col[span, :] == seg_row[seq : seq + 1, :])
        for pair in range(HEADS // 2):
            lanes = slice(pair * 2 * HEAD, (pair + 1) * 2 * HEAD)
            key_pair = qkv[span, HID + lanes.start : HID + lanes.stop]
            value_pair = qkv[span, 2 * HID + lanes.start : 2 * HID + lanes.stop]
            mixed = []
            for half, query in enumerate(head_parts(qkv[span, lanes])):
                raw = dot(query, key_pair, 1, 1) * HEAD ** (-0.5)
                raw = jnp.where(allowed, raw, masked_score)
                top = jnp.max(raw, axis=-1, keepdims=True)
                total = jnp.sum(jnp.exp(raw - top), axis=-1, keepdims=True)
                prob = jnp.exp(raw - (top + jnp.log(total)))
                probs[seq * HEADS + 2 * pair + half] = prob
                mixed.append(dot(prob.astype(jnp.bfloat16), value_pair, 1, 0))
            att[span, lanes] = jnp.where(left_lanes(mixed[0]), mixed[0], mixed[1]).astype(
                jnp.bfloat16
            )


def active_kernel(rows, place, tok, att, vec_all, *rest):
    blocks = rest[:8]
    n_out, hidden, act, slope_out = rest[8:12]
    windows = rest[12:16]
    w_mid, load_sem = rest[16:]
    ready = load_blocks(place, blocks, rows, w_mid, load_sem, 1, 3)
    base = 2 * rows

    def weight(first, size):
        return w_mid[first - base : first - base + size]

    ready(2)
    h_value = tok[...].astype(jnp.float32) + dot(att[...], weight(3 * HID, HID), 1, 0)
    h_value = h_value + vec_all[4:5, :]
    hidden[...] = h_value
    unit, _ = norm_parts(h_value)
    n_two = (unit * vec_all[5:6, :] + vec_all[6:7, :]).astype(jnp.bfloat16)
    n_out[...] = n_two
    ready(3, 4, 5)
    root = math.sqrt(2.0 / math.pi)
    for index in range(FF // D):
        span = slice(index * D, (index + 1) * D)
        pre = dot(n_two, weight(4 * HID + index * D, D), 1, 1) + vec_all[7 + index : 8 + index, :]
        squared = pre * pre
        bent = jnp.tanh(root * (pre + 0.044715 * (pre * squared)))
        half = 0.5 * (1.0 + bent)
        act[:, span] = (pre * half).astype(jnp.bfloat16)
        slope_out[:, span] = half + 0.5 * pre * (1.0 - bent * bent) * (
            root * (1.0 + 3 * 0.044715 * squared)
        )
    spread_terms(place, act, rows, 6 * rows - (4 * HID + FF), windows)


def change_kernel(rows, place, cot, att, act, slope, hidden, vec_all, *rest):
    blocks = rest[:8]
    out, dub, vec_out = rest[8:11]
    windows_two, windows_one = rest[11:15], rest[15:19]
    w_top, terms, load_sem = rest[19:]
    ready = load_blocks(place, blocks, rows, w_top, load_sem, 2, 4)
    base = 4 * rows
    terms[:, :HID] = att[...]
    result = hidden[...] + vec_all[11:12, :]
    ready(5, 6, 7)
    for index in range(FF // D):
        span = slice(index * D, (index + 1) * D)
        first = 4 * HID + FF + index * D - base
        weight = w_top[first : first + D]
        active = act[:, span]
        change = dot(cot[...], weight, 1, 1) * slope[:, span]
        change_bf = change.astype(jnp.bfloat16)
        dub[:, span] = change_bf
        terms[:, HID + index * D : HID + (index + 1) * D] = change_bf
        terms[:, HID + FF + index * D : HID + FF + (index + 1) * D] = active
        vec_out[index : index + 1, :] = row_sum(change)
        result = result + dot(active, weight, 1, 0)
    spread_terms(place, terms, rows, 2 * rows, windows_two)
    spread_terms(place, terms, rows, 0, windows_one)
    out[...] = result.astype(jnp.bfloat16)
    vec_out[4:5, :] = row_sum(cot[...].astype(jnp.float32))
    vec_out[5:8, :] = jnp.zeros((3, D), jnp.float32)
    ready(4)


def hidden_kernel(rows, place, dub, hidden, cot, vec_all, *rest):
    blocks = rest[:8]
    dh, dh_bf, da, vec_out, w_mid, load_sem = rest[8:]
    ready = load_blocks(place, blocks, rows, w_mid, load_sem, 1, 3)
    base = 2 * rows
    unit, scale = norm_parts(hidden[...])
    ready(2, 3, 4, 5)
    back = dot(dub[...], w_mid[4 * HID - base : 4 * HID + FF - base], 1, 0)
    vec_out[0:1, :] = row_sum(back * unit)
    vec_out[1:2, :] = row_sum(back)
    value = cot[...].astype(jnp.float32) + norm_back(unit, scale, back * vec_all[5:6, :])
    dh[...] = value
    vec_out[2:3, :] = row_sum(value)
    vec_out[3:8, :] = jnp.zeros((5, D), jnp.float32)
    rounded = value.astype(jnp.bfloat16)
    dh_bf[...] = rounded
    da[...] = dot(rounded, w_mid[3 * HID - base : 4 * HID - base], 1, 1).astype(jnp.bfloat16)


def attention_kernel(rows, place, da, qkv, probs, dh, tok, vec_all, vec_first, vec_second, *rest):
    blocks = rest[:8]
    grad_tok, vec_out = rest[8:10]
    windows = rest[10:14]
    w_in, dqkv, load_sem = rest[14:]
    ready = load_blocks(place, blocks, rows, w_in, load_sem, 0, 1)
    heads_total = probs.shape[0]
    length = probs.shape[1]
    vec_out[2:4, :] = jnp.zeros((2, D), jnp.float32)
    for seq in range(heads_total // HEADS):
        span = slice(seq * length, (seq + 1) * length)
        for pair in range(HEADS // 2):
            lanes = slice(pair * 2 * HEAD, (pair + 1) * 2 * HEAD)
            query_pair = qkv[span, lanes]
            key_pair = qkv[span, HID + lanes.start : HID + lanes.stop]
            value_pair = qkv[span, 2 * HID + lanes.start : 2 * HID + lanes.stop]
            da_pair = da[span, lanes]
            got = []
            for half, da_head in enumerate(head_parts(da_pair)):
                prob = probs[seq * HEADS + 2 * pair + half]
                grad_prob = dot(da_head, value_pair, 1, 1)
                inner = jnp.sum(prob * grad_prob, axis=-1, keepdims=True)
                grad_score = (prob * (grad_prob - inner) * HEAD ** (-0.5)).astype(jnp.bfloat16)
                got.append(
                    (
                        dot(grad_score, key_pair, 1, 0),
                        dot(grad_score, query_pair, 0, 0),
                        dot(prob.astype(jnp.bfloat16), da_pair, 0, 0),
                    )
                )
            left = left_lanes(got[0][0])
            query_grad, key_grad, value_grad = [
                jnp.where(left, one, two) for one, two in zip(got[0], got[1])
            ]
            dqkv[span, lanes] = query_grad.astype(jnp.bfloat16)
            dqkv[span, HID + lanes.start : HID + lanes.stop] = key_grad.astype(jnp.bfloat16)
            dqkv[span, 2 * HID + lanes.start : 2 * HID + lanes.stop] = value_grad.astype(
                jnp.bfloat16
            )
            vec_out[2:3, lanes] = vec_out[2:3, lanes] + row_sum(query_grad)
            vec_out[3:4, lanes] = vec_out[3:4, lanes] + row_sum(value_grad)
    spread_terms(place, dqkv, rows, 0, windows)
    unit, scale = norm_parts(tok[...].astype(jnp.float32))
    ready(0, 1)
    back = dot(dqkv[...], w_in[...], 1, 0)
    grad_tok[...] = dh[...] + norm_back(unit, scale, back * vec_all[0:1, :])
    vec_out[0:1, :] = row_sum(back * unit)
    vec_out[1:2, :] = row_sum(back)
    vec_out[4:5, :] = vec_second[2:3, :]
    vec_out[5:7, :] = vec_second[0:2, :]
    vec_out[7:12, :] = vec_first[0:5, :]
    vec_out[12:16, :] = jnp.zeros((4, D), jnp.float32)


def product_kernel(rows, split, which, place, *rest):
    columns, (away, mine) = rest[4:-5], rest[-5:-3]
    left, right, whole = rest[-3:]
    count, wide = rest[0].shape
    for index in range(4):
        left[index * count : (index + 1) * count] = rest[index][...]
    core, across, high = place[4], place[5], place[6]

    def put(span, other):
        for index in range(4):
            value = columns[index][...]
            if other is not None:
                value = jnp.where(other, columns[4 + index][...], value)
            right[index * count : (index + 1) * count] = value
        whole[span, :] = dot(left[:, span], right[...], 0, 0).astype(jnp.bfloat16)

    if split is None:
        put(slice(0, wide), None)
    else:
        start = rows - wide
        chosen = core == which
        if split <= start:
            put(slice(0, split), chosen & (across == 1))
            put(slice(split, wide), chosen)
        else:
            put(slice(0, split - start), chosen)
            put(slice(split - start, wide), chosen & (across == 0))
    part = rows // 4
    first = across * (wide - rows // 2)
    away[...] = whole[pl.ds(pl.multiple_of(first + (1 - high) * part, 16), part), :]
    mine[...] = whole[pl.ds(pl.multiple_of(first + high * part, 16), part), :]


any_spec = pl.BlockSpec(memory_space=pl.ANY)
vmem_spec = pl.BlockSpec(memory_space=pltpu.VMEM)
smem_spec = pl.BlockSpec(memory_space=pltpu.SMEM)
bf16, f32 = jnp.bfloat16, jnp.float32


def call(kernel, name, inputs, outputs, scratch, flops, moved):
    return pl.pallas_call(
        kernel,
        name=name,
        grid=(1,),
        in_specs=[spec for _, spec in inputs],
        out_specs=[spec for _, _, spec in outputs],
        out_shape=[jax.ShapeDtypeStruct(shape, kind) for shape, kind, _ in outputs],
        scratch_shapes=scratch,
        compiler_params=pltpu.CompilerParams(vmem_limit_bytes=60 * 1024 * 1024),
        cost_estimate=pl.CostEstimate(flops=flops, bytes_accessed=moved, transcendentals=0),
    )(*[value for value, _ in inputs])


def after(kernel, inputs, waits):
    count, extra = len(inputs), len(waits)

    def body(*refs):
        kernel(*refs[:count], *refs[count + extra :])

    return body, inputs + [(value, any_spec) for value in waits]


def parameter_blocks(links, weights, vectors):
    block = weights.astype(bf16)
    shards = links.chips * links.cores
    width = vectors.shape[1]
    number = links.chip * links.cores + links.core
    location = lax.broadcasted_iota(jnp.int32, (vectors.shape[0], width * shards), 1) // width
    spread = jnp.where(location == number, jnp.tile(vectors, (1, shards)), 0.0)
    spread = jnp.pad(spread, ((0, vector_pad - vectors.shape[0]), (0, 0))).astype(bf16)
    first, second = links.own_pieces(block)
    size = first.shape[0]
    mine = jnp.concatenate([first, second, spread])
    inner = (links.chip == 1) | (links.chip == 2)
    near = links.along(mine, {0: 1, 1: 0, 2: 3, 3: 2})
    middle = links.along(mine, {1: 2, 2: 1})
    outward = links.along(middle, {1: 0, 2: 3})
    across = links.along(near, {1: 2, 2: 1})
    far = links.along(across, {1: 0, 2: 3})
    slots = (near, jnp.where(inner, middle, outward), jnp.where(inner, across, far))
    wholes = [jnp.concatenate([block, spread])]
    for slot in slots:
        whole = links.gather_replicas(slot[:size], slot[size : 2 * size])
        wholes.append(jnp.concatenate([whole, slot[2 * size :]]))
    blocks = []
    for whole in wholes:
        blocks += [whole, links.swap_core(whole)]
    return blocks


def direct_step(links, tokens, segments, cotangent, weights, vectors):
    count = tokens.shape[0]
    rows = weights.shape[0]
    wide = -(-rows // 256) * 128
    blocks = parameter_blocks(links, weights, vectors)
    low = links.chip < links.chips // 2
    place = jnp.stack(
        [
            links.chip,
            links.chip ^ 1,
            jnp.where(low, 2, 1),
            jnp.where(low, 3, 0),
            links.core,
            links.bit_of(0),
            links.bit_of(1),
            links.core,
        ]
    ).astype(jnp.int32)
    ends = [(place, smem_spec)]
    pairs = segments.shape[0] * HEADS
    length = segments.shape[1]
    unit_cost = 2 * count * HID * D
    parameters = [(block, any_spec) for block in blocks]

    def full(*arrays):
        return [(array, vmem_spec) for array in arrays]

    def shape(width, kind=bf16, height=count):
        return (height, width), kind, vmem_spec

    def weight_scratch(chips):
        return [pltpu.VMEM((chips * 2 * rows, D), bf16)]

    def weight_sem(chips):
        return [pltpu.SemaphoreType.DMA((chips * 2,))]

    windows = [shape(wide)] * 4

    def share_rows(parts):
        own, to_core, to_side, to_both = parts
        return [own, links.swap_core(to_core), links.swap_bit(to_side, 0), links.swap_both(to_both, 0)]

    def share_columns(value):
        side = links.swap_bit(value, 0)
        return [value, links.swap_core(value), side, links.swap_core(side)]

    dy_all = share_columns(cotangent)
    n_one, qkv, probs, att, vec_all = call(
        functools.partial(query_kernel, rows),
        "query",
        ends + full(tokens, segments.reshape(count, 1), segments) + parameters,
        [
            shape(D),
            shape(3 * HID),
            ((pairs, length, length), f32, vmem_spec),
            shape(HID),
            shape(D, f32, vector_pad),
        ],
        weight_scratch(1)
        + [pltpu.VMEM((8, vector_pad, D), bf16)]
        + weight_sem(1)
        + [pltpu.SemaphoreType.DMA((8,))],
        4 * unit_cost,
        6 * HID * D,
    )
    n_one_all = share_columns(n_one)
    active_out = call(
        functools.partial(active_kernel, rows),
        "active",
        ends + full(tokens, att, vec_all) + parameters,
        [shape(D), shape(D, f32), shape(FF), shape(FF, f32)] + windows,
        weight_scratch(2) + weight_sem(2),
        5 * unit_cost,
        8 * rows * D,
    )
    n_two, hidden, act, slope = active_out[:4]
    rows_three = share_rows(active_out[4:])
    n_two_all = share_columns(n_two)
    change_out = call(
        functools.partial(change_kernel, rows),
        "change",
        ends + full(cotangent, att, act, slope, hidden, vec_all) + parameters,
        [shape(D), shape(FF), shape(D, f32, 8)] + windows + windows,
        weight_scratch(2) + [pltpu.VMEM((count, HID + 2 * FF), bf16)] + weight_sem(2),
        8 * unit_cost,
        8 * rows * D,
    )
    out, dub, vec_first = change_out[:3]
    rows_two = share_rows(change_out[3:7])
    rows_one = share_rows(change_out[7:11])

    def product(name, parts, columns, split=None, which=0, waits=()):
        kernel, inputs = after(
            functools.partial(product_kernel, rows, split, which),
            ends + full(*parts) + full(*columns),
            list(waits),
        )
        return call(
            kernel,
            name,
            inputs,
            [shape(D, bf16, rows // 4)] * 2,
            [
                pltpu.VMEM((4 * count, wide), bf16),
                pltpu.VMEM((4 * count, D), bf16),
                pltpu.VMEM((wide, D), bf16),
            ],
            8 * count * wide * D,
            4 * rows * D,
        )

    def scatter_rest(parts):
        away, mine = parts
        mine = add_bf(mine, links.swap_bit(away, 1))
        for bit in range(2, links.bits):
            size = mine.shape[0] // 2
            away = lax.dynamic_slice_in_dim(mine, (1 - links.bit_of(bit)) * size, size)
            near = lax.dynamic_slice_in_dim(mine, links.bit_of(bit) * size, size)
            mine = add_bf(near, links.swap_bit(away, bit))
        return mine

    three = scatter_rest(product("product_three", rows_three, dy_all))
    kernel, inputs = after(
        functools.partial(hidden_kernel, rows),
        ends + full(dub, hidden, cotangent, vec_all) + parameters,
        [],
    )
    dh, dh_bf, da, vec_second = call(
        kernel,
        "hidden",
        inputs,
        [shape(D, f32), shape(D), shape(HID), shape(D, f32, 8)],
        weight_scratch(2) + weight_sem(2),
        5 * unit_cost,
        8 * rows * D,
    )
    tail_rows = 4 * HID + FF - 5 * rows
    two = scatter_rest(product("product_two", rows_two, n_two_all + dy_all, tail_rows, 1))
    dh_all = share_columns(dh_bf)
    attention_out = call(
        functools.partial(attention_kernel, rows),
        "attention",
        ends + full(da, qkv, probs, dh, tokens, vec_all, vec_first, vec_second) + parameters,
        [shape(D, f32), shape(D, f32, vector_pad)] + windows,
        weight_scratch(1) + [pltpu.VMEM((count, 3 * HID), bf16)] + weight_sem(1),
        4 * unit_cost,
        4 * rows * D,
    )
    grad_tok, vec_sum = attention_out[:2]
    rows_zero = share_rows(attention_out[2:])
    out_rows = 4 * HID - 2 * rows
    one = scatter_rest(product("product_one", rows_one, n_two_all + dh_all, out_rows, 0))
    zero = scatter_rest(product("product_zero", rows_zero, n_one_all))
    mine = None
    for goal, piece in ((3, three), (2, two), (1, one), (0, zero)):
        piece = links.to_chip(piece, goal)
        mine = piece if mine is None else jnp.where(links.chip == goal, piece, mine)
    grad_w = links.gather_positions(mine).astype(f32)
    width = vectors.shape[1]
    all_v = links.sum_all(vec_sum)
    grad_v = lax.dynamic_slice_in_dim(all_v, lax.axis_index("shard") * width, width, 1)
    return out, grad_tok, grad_w, grad_v[: vectors.shape[0]]


def per_device(
    replicas,
    shards,
    tokens,
    segments,
    cotangent,
    weights,
    vectors,
    first_weights,
    first_vectors,
    second_weights,
    second_vectors,
):
    if Links.fits(replicas, shards, weights.shape[0]):
        output, grad_tokens, grad_w, grad_v = direct_step(
            Links(replicas, shards), tokens, segments, cotangent, weights, vectors
        )
    else:
        w_full = lax.all_gather(weights.astype(jnp.bfloat16), "shard", axis=0, tiled=True)
        v_full = lax.all_gather(vectors.astype(jnp.bfloat16), "shard", axis=1, tiled=True)
        output, kept_state = forward(tokens, segments, w_full, v_full)
        grad_tokens, grad_vec, row_terms, col_terms = backward(
            kept_state, cotangent, segments, w_full
        )
        local_grad = weight_grads(row_terms, col_terms).astype(jnp.bfloat16)
        own_w = lax.psum_scatter(local_grad, "shard", scatter_dimension=0, tiled=True)
        own_v = lax.psum_scatter(
            grad_vec.astype(jnp.bfloat16), "shard", scatter_dimension=1, tiled=True
        )
        grad_w = lax.psum(own_w, "rep").astype(jnp.float32)
        grad_v = lax.psum(own_v, "rep").astype(jnp.float32)
    new_w, new_fw, new_sw = adam_update(weights, first_weights, second_weights, grad_w, decay_rate)
    new_v, new_fv, new_sv = adam_update(vectors, first_vectors, second_vectors, grad_v, 0.0)
    return (output, grad_tokens, grad_w, grad_v, new_w, new_v, new_fw, new_fv, new_sw, new_sv)


def solution(mesh):
    placed = (
        P(("rep", "shard"), None),
        P(("rep", "shard"), None),
        P(("rep", "shard"), None),
        P("shard", None),
        P(None, "shard"),
        P("shard", None),
        P(None, "shard"),
        P("shard", None),
        P(None, "shard"),
    )
    return jax.shard_map(
        functools.partial(per_device, mesh.shape["rep"], mesh.shape["shard"]),
        mesh=mesh,
        in_specs=placed,
        out_specs=(
            P(("rep", "shard"), None),
            P(("rep", "shard"), None),
            P("shard", None),
            P(None, "shard"),
            P("shard", None),
            P(None, "shard"),
            P("shard", None),
            P(None, "shard"),
            P("shard", None),
            P(None, "shard"),
        ),
        check_vma=False,
    )
```

```python
import functools
import math

import jax
import jax.numpy as jnp
from jax import lax
from jax.experimental import pallas as pl
from jax.experimental.pallas import tpu as pltpu
from jax.sharding import PartitionSpec as P

D = 768
HEADS = 12
HEAD = 64
FF = 3072
STEP = 3
HID = 768
R = 9216


norm_eps = 1e-05
beta_one = 0.9
beta_two = 0.999
adam_eps = 1e-08
learn_rate = 0.2
decay_rate = 0.1
masked_score = -1e30


def normalize(values):
    centred = values - jnp.mean(values, axis=-1, keepdims=True)
    return centred * lax.rsqrt(jnp.mean(centred * centred, axis=-1, keepdims=True) + norm_eps)


def affine_norm(values, gain_vec, shift_vec):
    return normalize(values) * gain_vec + shift_vec


def gelu_tanh(values):
    return jax.nn.gelu(values, approximate=True)


def matmul(left_op, right_op):
    return jnp.dot(left_op, right_op, preferred_element_type=jnp.float32)


def matmul_nt(left_op, right_op):
    return lax.dot_general(
        left_op, right_op, (((1,), (1,)), ((), ())), preferred_element_type=jnp.float32
    )


def matmul_tn(left_op, right_op):
    return lax.dot_general(
        left_op, right_op, (((0,), (0,)), ((), ())), preferred_element_type=jnp.float32
    )


def product(pattern, left_op, right_op):
    return jnp.einsum(pattern, left_op, right_op, preferred_element_type=jnp.float32)


def allowed_pairs(segments):
    length = segments.shape[1]
    places = lax.broadcasted_iota(jnp.int32, (length, length), 0)
    others = lax.broadcasted_iota(jnp.int32, (length, length), 1)
    causal = others <= places
    same_doc = segments[:, :, None] == segments[:, None, :]
    return (causal[None] & same_doc)[:, None]


def scores_of(query_rows, key_rows, allowed):
    raw_scores = product("sqhd,skhd->shqk", query_rows, key_rows) * HEAD ** (-0.5)
    return jnp.where(allowed, raw_scores, masked_score)


def forward(tokens, segments, w_bf, v_bf):
    seq_count, length = segments.shape
    tok_count = tokens.shape[0]
    head_shape = (seq_count, length, HEADS, HEAD)
    floats = v_bf.astype(jnp.float32)
    residual = tokens.astype(jnp.float32)
    normed_one = affine_norm(residual, floats[0], floats[1]).astype(jnp.bfloat16)
    projected = matmul_nt(normed_one, w_bf[: 3 * HID])
    query_rows = (projected[:, :HID] + floats[2]).astype(jnp.bfloat16)
    key_rows = projected[:, HID : 2 * HID].astype(jnp.bfloat16)
    value_rows = (projected[:, 2 * HID :] + floats[3]).astype(jnp.bfloat16)
    allowed = allowed_pairs(segments)
    scores = scores_of(query_rows.reshape(head_shape), key_rows.reshape(head_shape), allowed)
    row_max = jnp.max(scores, axis=-1, keepdims=True)
    log_total = row_max + jnp.log(jnp.sum(jnp.exp(scores - row_max), axis=-1, keepdims=True))
    attn_probs = jnp.exp(scores - log_total).astype(jnp.bfloat16)
    mixed_heads = product("shqk,skhd->sqhd", attn_probs, value_rows.reshape(head_shape))
    attended = mixed_heads.reshape(tok_count, HID).astype(jnp.bfloat16)
    hidden_one = residual + matmul(attended, w_bf[3 * HID : 4 * HID]) + floats[4]
    normed_two = affine_norm(hidden_one, floats[5], floats[6]).astype(jnp.bfloat16)
    pre_act = matmul_nt(normed_two, w_bf[4 * HID : 4 * HID + FF]) + floats[7:11].reshape(FF)
    active = gelu_tanh(pre_act).astype(jnp.bfloat16)
    output = (hidden_one + matmul(active, w_bf[4 * HID + FF :]) + floats[11]).astype(jnp.bfloat16)
    kept_state = (
        residual,
        normed_one,
        query_rows,
        key_rows,
        value_rows,
        log_total,
        attended,
        hidden_one,
        normed_two,
        pre_act,
        active,
        floats,
    )
    return (output, kept_state)


def backward(kept_state, cotangent, segments, w_bf):
    (
        residual,
        normed_one,
        query_rows,
        key_rows,
        value_rows,
        log_total,
        attended,
        hidden_one,
        normed_two,
        pre_act,
        active,
        floats,
    ) = kept_state
    seq_count, length = segments.shape
    tok_count = residual.shape[0]
    head_shape = (seq_count, length, HEADS, HEAD)
    grad_out = cotangent.astype(jnp.float32)
    grad_active = matmul_nt(cotangent, w_bf[4 * HID + FF :])
    grad_pre = jax.vjp(gelu_tanh, pre_act)[1](grad_active)[0]
    grad_pre_bf = grad_pre.astype(jnp.bfloat16)
    grad_normed_two = matmul(grad_pre_bf, w_bf[4 * HID : 4 * HID + FF])
    norm_back_two = jax.vjp(affine_norm, hidden_one, floats[5], floats[6])[1]
    grad_h_part, grad_gain_two, grad_shift_two = norm_back_two(grad_normed_two)
    grad_hidden = grad_out + grad_h_part
    grad_hidden_bf = grad_hidden.astype(jnp.bfloat16)
    grad_attended = matmul_nt(grad_hidden_bf, w_bf[3 * HID : 4 * HID]).astype(jnp.bfloat16)
    query_four = query_rows.reshape(head_shape)
    key_four = key_rows.reshape(head_shape)
    value_four = value_rows.reshape(head_shape)
    grad_att_four = grad_attended.reshape(head_shape)
    allowed = allowed_pairs(segments)
    scores = scores_of(query_four, key_four, allowed)
    attn_probs = jnp.exp(scores - log_total)
    probs_bf = attn_probs.astype(jnp.bfloat16)
    grad_probs = product("sqhd,skhd->shqk", grad_att_four, value_four)
    inner_sum = jnp.sum(attn_probs * grad_probs, axis=-1, keepdims=True)
    grad_scores = (attn_probs * (grad_probs - inner_sum) * HEAD ** (-0.5)).astype(jnp.bfloat16)
    grad_query = product("shqk,skhd->sqhd", grad_scores, key_four).reshape(tok_count, HID)
    grad_keys = product("shqk,sqhd->skhd", grad_scores, query_four).reshape(tok_count, HID)
    grad_values = product("shqk,sqhd->skhd", probs_bf, grad_att_four).reshape(tok_count, HID)
    grad_proj = jnp.concatenate([grad_query, grad_keys, grad_values], axis=1)
    grad_proj_bf = grad_proj.astype(jnp.bfloat16)
    grad_normed_one = matmul(grad_proj_bf, w_bf[: 3 * HID])
    norm_back_one = jax.vjp(affine_norm, residual, floats[0], floats[1])[1]
    grad_r_part, grad_gain_one, grad_shift_one = norm_back_one(grad_normed_one)
    grad_tokens = grad_hidden + grad_r_part
    bias_ff = jnp.sum(grad_pre, axis=0).reshape(FF // D, D)
    head_rows = jnp.stack(
        [
            grad_gain_one,
            grad_shift_one,
            jnp.sum(grad_query, axis=0),
            jnp.sum(grad_values, axis=0),
            jnp.sum(grad_hidden, axis=0),
            grad_gain_two,
            grad_shift_two,
        ]
    )
    grad_vec = jnp.concatenate([head_rows, bias_ff, jnp.sum(grad_out, axis=0)[None]], axis=0)
    row_terms = jnp.concatenate([grad_proj_bf, attended, grad_pre_bf, active], axis=1)
    col_terms = jnp.stack([normed_one, grad_hidden_bf, normed_two, cotangent])
    return (grad_tokens, grad_vec, row_terms, col_terms)


def weight_grads(row_terms, col_terms):
    row_bounds = (0, 3 * HID, 4 * HID, 4 * HID + FF, R)
    pieces = [
        matmul_tn(row_terms[:, row_bounds[index] : row_bounds[index + 1]], col_terms[index])
        for index in range(4)
    ]
    return jnp.concatenate(pieces, axis=0)


def adam_update(param, first, second, grad, decay):
    new_first = beta_one * first + (1.0 - beta_one) * grad
    new_second = beta_two * second + (1.0 - beta_two) * grad * grad
    first_hat = new_first / (1.0 - beta_one**STEP)
    second_hat = new_second / (1.0 - beta_two**STEP)
    new_param = param - learn_rate * (first_hat / (jnp.sqrt(second_hat) + adam_eps) + decay * param)
    return (new_param, new_first, new_second)


def bit_reverse(index, bits):
    out = index * 0
    for place in range(bits):
        out = out * 2 + (index >> place) % 2
    return out


class Links:
    def __init__(self, replicas, shards):
        self.replicas = replicas
        self.cores = 2
        self.chips = shards // self.cores
        self.bits = replicas.bit_length() - 1
        self.replica = lax.axis_index("rep")
        shard = lax.axis_index("shard")
        self.chip = shard // self.cores
        self.core = shard % self.cores

    @staticmethod
    def fits(replicas, shards, rows):
        power = replicas > 2 and replicas & (replicas - 1) == 0
        return shards == 8 and power and 2 * rows == 3 * HID

    def send(self, value, target):
        route = []
        for rep in range(self.replicas):
            for chip in range(self.chips):
                for core in range(self.cores):
                    goal = target(rep, chip, core)
                    if goal is None:
                        continue
                    start = (rep * self.chips + chip) * self.cores + core
                    stop = (goal[0] * self.chips + goal[1]) * self.cores + goal[2]
                    route.append((start, stop))
        return lax.ppermute(value, ("rep", "shard"), route)

    def swap_core(self, value):
        return self.send(value, lambda rep, chip, core: (rep, chip, 1 - core))

    def swap_both(self, value, bit):
        return self.send(value, lambda rep, chip, core: (rep ^ (1 << bit), chip, 1 - core))

    def swap_bit(self, value, bit):
        return self.send(value, lambda rep, chip, core: (rep ^ (1 << bit), chip, core))

    def along(self, value, moves):
        table = dict(moves)
        return self.send(
            value, lambda rep, chip, core: (rep, table[chip], core) if chip in table else None
        )

    def bit_of(self, bit):
        return (self.replica >> bit) % 2

    def own_pieces(self, block):
        half = block.shape[0] // 2
        size = half // self.replicas
        first = lax.dynamic_slice_in_dim(block, self.replica * size, size)
        turned = bit_reverse(self.replica, self.bits)
        second = lax.dynamic_slice_in_dim(block, half + turned * size, size)
        return first, second

    def gather_pieces(self, first, second):
        for step in range(self.bits):
            low, high = step, self.bits - 1 - step
            got_first = self.swap_bit(first, low)
            got_second = self.swap_bit(second, high)
            if step == self.bits - 1:
                return [first, got_first, second, got_second]
            first = jnp.where(
                self.bit_of(low) == 0,
                jnp.concatenate([first, got_first]),
                jnp.concatenate([got_first, first]),
            )
            second = jnp.where(
                self.bit_of(high) == 0,
                jnp.concatenate([second, got_second]),
                jnp.concatenate([got_second, second]),
            )

    def gather_positions(self, piece):
        size = piece.shape[0] // 2
        first, second = piece[:size], piece[size:]
        for step in range(self.bits):
            high, low = self.bits - 1 - step, step
            got_first = self.swap_bit(first, high)
            got_second = self.swap_bit(second, low)
            first = jnp.where(
                self.bit_of(high) == 0,
                jnp.concatenate([first, got_first]),
                jnp.concatenate([got_first, first]),
            )
            second = jnp.where(
                self.bit_of(low) == 0,
                jnp.concatenate([second, got_second]),
                jnp.concatenate([got_second, second]),
            )
        parts = []
        for position in range(self.replicas):
            turned = bit_reverse(position, self.bits)
            parts.append(first[position * size : (position + 1) * size])
            parts.append(second[turned * size : (turned + 1) * size])
        return jnp.concatenate(parts)

    def to_chip(self, piece, moves):
        got = self.along(piece, moves)
        return add_bf(piece, got)


def add_bf(left, right):
    return (left.astype(jnp.float32) + right.astype(jnp.float32)).astype(jnp.bfloat16)


vector_pad = 16


def dot(left, right, left_dim, right_dim):
    return lax.dot_general(
        left,
        right,
        (((left_dim,), (right_dim,)), ((), ())),
        preferred_element_type=jnp.float32,
    )


def norm_parts(values):
    centred = values - jnp.mean(values, axis=-1, keepdims=True)
    scale = lax.rsqrt(jnp.mean(centred * centred, axis=-1, keepdims=True) + norm_eps)
    return centred * scale, scale


def norm_back(unit, scale, grad):
    inner = jnp.mean(grad, axis=-1, keepdims=True)
    outer = jnp.mean(grad * unit, axis=-1, keepdims=True)
    return scale * (grad - inner - unit * outer)


def row_sum(values):
    return jnp.sum(values, axis=0, keepdims=True)


def left_lanes(value):
    return lax.broadcasted_iota(jnp.int32, value.shape, 1) < HEAD


def head_parts(pair):
    left = left_lanes(pair)
    none = jnp.zeros_like(pair)
    return jnp.where(left, pair, none), jnp.where(left, none, pair)


def load_blocks(place, blocks, rows, target, sem, first, last):
    quarter = rows // 4
    starts = (
        place[7] * quarter,
        (1 - place[7]) * quarter,
        (2 + place[5]) * quarter,
        (3 - place[5]) * quarter,
    )
    for slot in range(4):
        chip = place[slot]

        @pl.when((chip >= first) & (chip < last))
        def _():
            for side in range(2):
                core = place[4] if side == 0 else 1 - place[4]
                number = (chip - first) * 2 + core
                if slot == 0:
                    parts = [(blocks[side], 0, rows)]
                else:
                    at = 2 + (slot - 1) * 8 + side
                    parts = [
                        (blocks[at + 2 * index], starts[index], quarter) for index in range(4)
                    ]
                for ref, shift, size in parts:
                    start = pl.multiple_of(number * rows + shift, 16)
                    pltpu.make_async_copy(ref, target.at[pl.ds(start, size)], sem.at[number]).start()

    done = set()

    def ready(low, high):
        for number in range(low // rows, -(-high // rows)):
            if number in done:
                continue
            done.add(number)
            index = number - 2 * first
            pltpu.make_async_copy(
                blocks[0], target.at[pl.ds(index * rows, rows)], sem.at[index]
            ).wait()

    return ready


block_count = 26


def spread_terms(place, terms, rows, first, outs, wide, lane=0):
    core, across = place[4], place[5]
    count = terms.shape[0]
    for index, out in enumerate(outs):
        block = core if index % 2 == 0 else 1 - core
        side = across if index < 2 else 1 - across
        start = pl.multiple_of(first + block * rows + side * (rows - wide), 128)
        out[:count, lane : lane + wide] = terms[:, pl.ds(start, wide)]


def query_kernel(rows, place, tok, seg_col, seg_row, vec_all, *rest):
    blocks = rest[:block_count]
    n_out, qkv, probs, att, w_in, load_sem = rest[block_count:]
    ready = load_blocks(place, blocks, rows, w_in, load_sem, 0, 1)
    unit, _ = norm_parts(tok[...].astype(jnp.float32))
    n_one = (unit * vec_all[0:1, :] + vec_all[1:2, :]).astype(jnp.bfloat16)
    n_out[...] = n_one
    for index, bias in enumerate((vec_all[2:3, :], None, vec_all[3:4, :])):
        ready(index * HID, (index + 1) * HID)
        value = dot(n_one, w_in[index * HID : (index + 1) * HID], 1, 1)
        if bias is not None:
            value = value + bias
        qkv[:, index * HID : (index + 1) * HID] = value.astype(jnp.bfloat16)
    length = seg_row.shape[1]
    for seq in range(seg_row.shape[0]):
        span = slice(seq * length, (seq + 1) * length)
        order = lax.broadcasted_iota(jnp.int32, (length, length), 0)
        other = lax.broadcasted_iota(jnp.int32, (length, length), 1)
        allowed = (other <= order) & (seg_col[span, :] == seg_row[seq : seq + 1, :])
        for pair in range(HEADS // 2):
            lanes = slice(pair * 2 * HEAD, (pair + 1) * 2 * HEAD)
            key_pair = qkv[span, HID + lanes.start : HID + lanes.stop]
            value_pair = qkv[span, 2 * HID + lanes.start : 2 * HID + lanes.stop]
            mixed = []
            for half, query in enumerate(head_parts(qkv[span, lanes])):
                raw = dot(query, key_pair, 1, 1) * HEAD ** (-0.5)
                raw = jnp.where(allowed, raw, masked_score)
                top = jnp.max(raw, axis=-1, keepdims=True)
                total = jnp.sum(jnp.exp(raw - top), axis=-1, keepdims=True)
                prob = jnp.exp(raw - (top + jnp.log(total)))
                probs[seq * HEADS + 2 * pair + half] = prob
                mixed.append(dot(prob.astype(jnp.bfloat16), value_pair, 1, 0))
            att[span, lanes] = jnp.where(left_lanes(mixed[0]), mixed[0], mixed[1]).astype(
                jnp.bfloat16
            )


def active_kernel(rows, place, tok, att, vec_all, *rest):
    blocks = rest[:block_count]
    n_out, hidden, act, slope_out = rest[block_count : block_count + 4]
    windows = rest[block_count + 4 : block_count + 8]
    w_mid, load_sem = rest[block_count + 8 :]
    ready = load_blocks(place, blocks, rows, w_mid, load_sem, 1, 3)
    base = 2 * rows

    def weight(first, size):
        ready(first, first + size)
        return w_mid[first - base : first - base + size]

    h_value = tok[...].astype(jnp.float32) + dot(att[...], weight(3 * HID, HID), 1, 0)
    h_value = h_value + vec_all[4:5, :]
    hidden[...] = h_value
    unit, _ = norm_parts(h_value)
    n_two = (unit * vec_all[5:6, :] + vec_all[6:7, :]).astype(jnp.bfloat16)
    n_out[...] = n_two
    root = math.sqrt(2.0 / math.pi)
    for index in range(FF // D):
        span = slice(index * D, (index + 1) * D)
        pre = dot(n_two, weight(4 * HID + index * D, D), 1, 1) + vec_all[7 + index : 8 + index, :]
        squared = pre * pre
        bent = jnp.tanh(root * (pre + 0.044715 * (pre * squared)))
        half = 0.5 * (1.0 + bent)
        act[:, span] = (pre * half).astype(jnp.bfloat16)
        slope_out[:, span] = half + 0.5 * pre * (1.0 - bent * bent) * (
            root * (1.0 + 3 * 0.044715 * squared)
        )
    wide = windows[0].shape[1]
    spread_terms(place, act, rows, 6 * rows - (4 * HID + FF), windows, wide)
    windows[1][:, wide:] = n_two
    windows[2][:, wide:] = n_two
    ready(2 * rows, 6 * rows)


def change_kernel(rows, place, cot, att, act, slope, hidden, vec_all, *rest):
    blocks = rest[:block_count]
    rest = rest[block_count:]
    out, dub, vec_out = rest[:3]
    windows = rest[3:7]
    w_top, terms, load_sem = rest[7:]
    ready = load_blocks(place, blocks, rows, w_top, load_sem, 2, 4)
    base = 4 * rows
    terms[:, :HID] = att[...]
    result = hidden[...] + vec_all[11:12, :]
    for index in range(FF // D):
        span = slice(index * D, (index + 1) * D)
        first = 4 * HID + FF + index * D - base
        ready(first + base, first + base + D)
        weight = w_top[first : first + D]
        active = act[:, span]
        change = dot(cot[...], weight, 1, 1) * slope[:, span]
        change_bf = change.astype(jnp.bfloat16)
        dub[:, span] = change_bf
        terms[:, HID + index * D : HID + (index + 1) * D] = change_bf
        terms[:, HID + FF + index * D : HID + FF + (index + 1) * D] = active
        vec_out[index : index + 1, :] = row_sum(change)
        result = result + dot(active, weight, 1, 0)
    wide = windows[0].shape[1] // 2
    spread_terms(place, terms, rows, 2 * rows, windows, wide)
    spread_terms(place, terms, rows, 0, windows, wide, wide)
    out[...] = result.astype(jnp.bfloat16)
    vec_out[4:5, :] = row_sum(cot[...].astype(jnp.float32))
    vec_out[5:8, :] = jnp.zeros((3, D), jnp.float32)
    ready(4 * rows, 8 * rows)


def hidden_kernel(rows, place, dub, hidden, cot, vec_all, *rest):
    blocks = rest[:block_count]
    dh, dh_bf, da, vec_out, w_mid, load_sem = rest[block_count:]
    ready = load_blocks(place, blocks, rows, w_mid, load_sem, 1, 3)
    base = 2 * rows
    unit, scale = norm_parts(hidden[...])
    start = 4 * HID
    back = None
    while start < 4 * HID + FF:
        stop = min((start // rows + 1) * rows, 4 * HID + FF)
        ready(start, stop)
        part = dot(dub[:, start - 4 * HID : stop - 4 * HID], w_mid[start - base : stop - base], 1, 0)
        back = part if back is None else back + part
        start = stop
    vec_out[0:1, :] = row_sum(back * unit)
    vec_out[1:2, :] = row_sum(back)
    value = cot[...].astype(jnp.float32) + norm_back(unit, scale, back * vec_all[5:6, :])
    dh[...] = value
    vec_out[2:3, :] = row_sum(value)
    vec_out[3:8, :] = jnp.zeros((5, D), jnp.float32)
    rounded = value.astype(jnp.bfloat16)
    dh_bf[...] = rounded
    da[...] = dot(rounded, w_mid[3 * HID - base : 4 * HID - base], 1, 1).astype(jnp.bfloat16)


def attention_kernel(rows, place, da, qkv, probs, dh, tok, vec_all, vec_first, vec_second, *rest):
    blocks = rest[:block_count]
    rest = rest[block_count:]
    grad_tok = rest[0]
    windows = rest[1:5]
    w_in, dqkv, vec_out, packed, load_sem = rest[5:]
    ready = load_blocks(place, blocks, rows, w_in, load_sem, 0, 1)
    heads_total = probs.shape[0]
    length = probs.shape[1]
    vec_out[2:4, :] = jnp.zeros((2, D), jnp.float32)
    for seq in range(heads_total // HEADS):
        span = slice(seq * length, (seq + 1) * length)
        for pair in range(HEADS // 2):
            lanes = slice(pair * 2 * HEAD, (pair + 1) * 2 * HEAD)
            query_pair = qkv[span, lanes]
            key_pair = qkv[span, HID + lanes.start : HID + lanes.stop]
            value_pair = qkv[span, 2 * HID + lanes.start : 2 * HID + lanes.stop]
            da_pair = da[span, lanes]
            got = []
            for half, da_head in enumerate(head_parts(da_pair)):
                prob = probs[seq * HEADS + 2 * pair + half]
                grad_prob = dot(da_head, value_pair, 1, 1)
                inner = jnp.sum(prob * grad_prob, axis=-1, keepdims=True)
                grad_score = (prob * (grad_prob - inner) * HEAD ** (-0.5)).astype(jnp.bfloat16)
                got.append(
                    (
                        dot(grad_score, key_pair, 1, 0),
                        dot(grad_score, query_pair, 0, 0),
                        dot(prob.astype(jnp.bfloat16), da_pair, 0, 0),
                    )
                )
            left = left_lanes(got[0][0])
            query_grad, key_grad, value_grad = [
                jnp.where(left, one, two) for one, two in zip(got[0], got[1])
            ]
            dqkv[span, lanes] = query_grad.astype(jnp.bfloat16)
            dqkv[span, HID + lanes.start : HID + lanes.stop] = key_grad.astype(jnp.bfloat16)
            dqkv[span, 2 * HID + lanes.start : 2 * HID + lanes.stop] = value_grad.astype(
                jnp.bfloat16
            )
            vec_out[2:3, lanes] = vec_out[2:3, lanes] + row_sum(query_grad)
            vec_out[3:4, lanes] = vec_out[3:4, lanes] + row_sum(value_grad)
    unit, scale = norm_parts(tok[...].astype(jnp.float32))
    ready(0, 2 * rows)
    back = dot(dqkv[...], w_in[...], 1, 0)
    grad_tok[...] = dh[...] + norm_back(unit, scale, back * vec_all[0:1, :])
    vec_out[0:1, :] = row_sum(back * unit)
    vec_out[1:2, :] = row_sum(back)
    vec_out[4:5, :] = vec_second[2:3, :]
    vec_out[5:7, :] = vec_second[0:2, :]
    vec_out[7:12, :] = vec_first[0:5, :]
    wide = windows[0].shape[1]
    spread_terms(place, dqkv, rows, 0, windows, wide)
    packed[...] = jnp.zeros_like(packed)
    for at, lanes, row, source in vector_tiles(wide):
        packed[at : at + 1, lanes] = vec_out[row : row + 1, source]
    for window in windows:
        window[dqkv.shape[0] :, :] = packed[...].astype(jnp.bfloat16)


def vector_tiles(wide):
    across, packed = D // 128, wide // 128
    for index in range(12 * across):
        at, to = divmod(index, packed)
        row, source = divmod(index, across)
        yield at, slice(to * 128, to * 128 + 128), row, slice(source * 128, source * 128 + 128)


def product_kernel(rows, wide, lane, starts, split, which, place, *rest):
    last = split is None and starts is None
    terms, columns, rest = rest[:4], rest[4:-6], rest[-6:]
    away, mine, left, right, whole, sums = rest
    if last:
        vec_all, columns = columns[0], columns[1:]
    count = columns[0].shape[0]
    for index in range(4):
        left[index * count : (index + 1) * count] = terms[index][:count, lane : lane + wide]
    core, across, high = place[4], place[5], place[6]

    def column(index):
        value = columns[index]
        if last and index > 0:
            unit, _ = norm_parts(value[:, :D].astype(jnp.float32))
            return (unit * vec_all[0:1, :] + vec_all[1:2, :]).astype(jnp.bfloat16)
        start = 0 if last else starts[index]
        return value[:, start : start + D]

    def put(span, other):
        for index in range(4):
            value = column(index)
            if other is not None:
                value = jnp.where(other, column(4 + index), value)
            right[index * count : (index + 1) * count] = value
        whole[span, :] = dot(left[:, span], right[...], 0, 0).astype(jnp.bfloat16)

    if split is None:
        put(slice(0, wide), None)
    else:
        start = rows - wide
        chosen = core == which
        if split <= start:
            put(slice(0, split), chosen & (across == 1))
            put(slice(split, wide), chosen)
        else:
            put(slice(0, split - start), chosen)
            put(slice(split - start, wide), chosen & (across == 0))
    part = rows // 4
    first = across * (wide - rows // 2)
    away[:part] = whole[pl.ds(pl.multiple_of(first + (1 - high) * part, 16), part), :]
    mine[:part] = whole[pl.ds(pl.multiple_of(first + high * part, 16), part), :]
    if last:
        total = terms[0][count:, :].astype(jnp.float32)
        for index in range(1, 4):
            total = total + terms[index][count:, :].astype(jnp.float32)
        sums[...] = jnp.zeros_like(sums)
        for at, lanes, row, source in vector_tiles(wide):
            sums[row : row + 1, source] = total[at : at + 1, lanes]
        away[part:] = sums[...].astype(jnp.bfloat16)
        mine[part:] = sums[...].astype(jnp.bfloat16)


any_spec = pl.BlockSpec(memory_space=pl.ANY)
vmem_spec = pl.BlockSpec(memory_space=pltpu.VMEM)
smem_spec = pl.BlockSpec(memory_space=pltpu.SMEM)
bf16, f32 = jnp.bfloat16, jnp.float32


def call(kernel, inputs, outputs, scratch, flops, moved):
    return pl.pallas_call(
        kernel,
        grid=(1,),
        in_specs=[spec for _, spec in inputs],
        out_specs=[spec for _, _, spec in outputs],
        out_shape=[jax.ShapeDtypeStruct(shape, kind) for shape, kind, _ in outputs],
        scratch_shapes=scratch,
        compiler_params=pltpu.CompilerParams(vmem_limit_bytes=60 * 1024 * 1024),
        cost_estimate=pl.CostEstimate(flops=flops, bytes_accessed=moved, transcendentals=0),
    )(*[value for value, _ in inputs])


def after(kernel, inputs, waits):
    count, extra = len(inputs), len(waits)

    def body(*refs):
        kernel(*refs[:count], *refs[count + extra :])

    return body, inputs + [(value, any_spec) for value in waits]


def parameter_blocks(links, weights, vectors):
    shards = links.chips * links.cores
    width = vectors.shape[1]
    number = links.chip * links.cores + links.core
    location = lax.broadcasted_iota(jnp.int32, (vectors.shape[0], width * shards), 1) // width
    spread = jnp.where(location == number, jnp.tile(vectors, (1, shards)), 0.0)
    spread = jnp.pad(spread, ((0, vector_pad - vectors.shape[0]), (0, 0))).astype(bf16)
    first, second = links.own_pieces(weights)
    size = first.shape[0]
    mine = jnp.concatenate([first.astype(bf16), second.astype(bf16), spread])
    inner = (links.chip == 1) | (links.chip == 2)
    near = links.along(mine, {0: 1, 1: 0, 2: 3, 3: 2})
    middle = links.along(mine, {1: 2, 2: 1})
    across = links.along(near, {1: 2, 2: 1})
    outward = links.along(middle, {1: 0, 2: 3})
    far = links.along(across, {1: 0, 2: 3})
    block = weights.astype(bf16)
    blocks = [block, links.swap_core(block)]
    slots = (near, jnp.where(inner, middle, outward), jnp.where(inner, across, far))
    total = spread
    for slot in slots:
        total = total + slot[2 * size :]
        for piece in links.gather_pieces(slot[:size], slot[size : 2 * size]):
            blocks += [piece, links.swap_core(piece)]
    total = total + links.swap_core(total)
    return blocks, total.astype(f32)


def direct_step(links, tokens, segments, cotangent, weights, vectors):
    count = tokens.shape[0]
    rows = weights.shape[0]
    wide = -(-rows // 256) * 128
    blocks, vec_all = parameter_blocks(links, weights, vectors)
    low = links.chip < links.chips // 2
    place = jnp.stack(
        [
            links.chip,
            links.chip ^ 1,
            jnp.where(low, 2, 1),
            jnp.where(low, 3, 0),
            links.core,
            links.bit_of(0),
            links.bit_of(1),
            links.bit_of(links.bits - 1),
        ]
    ).astype(jnp.int32)
    ends = [(place, smem_spec)]
    pairs = segments.shape[0] * HEADS
    length = segments.shape[1]
    unit_cost = 2 * count * HID * D
    parameters = [(block, any_spec) for block in blocks]

    def full(*arrays):
        return [(array, vmem_spec) for array in arrays]

    def shape(width, kind=bf16, height=count):
        return (height, width), kind, vmem_spec

    def weight_scratch(chips):
        return [pltpu.VMEM((chips * 2 * rows, D), bf16)]

    def weight_sem(chips):
        return [pltpu.SemaphoreType.DMA((chips * 2,))]

    def share_rows(parts):
        own, to_core, to_side, to_both = parts
        side = links.swap_bit(to_side, 0)
        both = links.swap_both(to_both, 0)
        other = links.swap_core(to_core)
        return [own, other, side, both]

    joined = jnp.concatenate([tokens, cotangent], axis=1)
    joined_side = links.swap_bit(joined, 0)
    joined_core = links.swap_core(joined)
    joined_both = links.swap_core(joined_side)
    joined_all = [joined, joined_core, joined_side, joined_both]
    n_one, qkv, probs, att = call(
        functools.partial(query_kernel, rows),
        ends + full(tokens, segments.reshape(count, 1), segments, vec_all) + parameters,
        [
            shape(D),
            shape(3 * HID),
            ((pairs, length, length), f32, vmem_spec),
            shape(HID),
        ],
        weight_scratch(1) + weight_sem(1),
        4 * unit_cost,
        6 * HID * D,
    )
    active_out = call(
        functools.partial(active_kernel, rows),
        ends + full(tokens, att, vec_all) + parameters,
        [shape(D), shape(D, f32), shape(FF), shape(FF, f32)]
        + [shape(wide), shape(wide + D), shape(wide + D), shape(wide)],
        weight_scratch(2) + weight_sem(2),
        5 * unit_cost,
        8 * rows * D,
    )
    n_two, hidden, act, slope = active_out[:4]
    rows_three = share_rows(active_out[4:])
    n_two_both = links.swap_core(rows_three[2])
    n_two_all = [n_two, rows_three[1], rows_three[2], n_two_both]
    n_two_starts = [0, wide, wide, wide]
    change_out = call(
        functools.partial(change_kernel, rows),
        ends + full(cotangent, att, act, slope, hidden, vec_all) + parameters,
        [shape(D), shape(FF), shape(D, f32, 8)] + [shape(2 * wide)] * 4,
        weight_scratch(2) + [pltpu.VMEM((count, HID + 2 * FF), bf16)] + weight_sem(2),
        8 * unit_cost,
        8 * rows * D,
    )
    out, dub, vec_first = change_out[:3]
    rows_middle = share_rows(change_out[3:])

    def product(parts, columns, lane, starts, split=None, which=0, waits=()):
        extra = 0 if starts is not None else vector_pad
        kernel, inputs = after(
            functools.partial(product_kernel, rows, wide, lane, starts, split, which),
            ends + full(*parts) + full(*columns),
            list(waits),
        )
        return call(
            kernel,
            inputs,
            [shape(D, bf16, rows // 4 + extra)] * 2,
            [
                pltpu.VMEM((4 * count, wide), bf16),
                pltpu.VMEM((4 * count, D), bf16),
                pltpu.VMEM((wide, D), bf16),
                pltpu.VMEM((vector_pad, D), f32),
            ],
            8 * count * wide * D,
            4 * rows * D,
        )

    def scatter_rest(parts):
        away, mine = parts
        got = links.swap_bit(away, 1)
        mine = add_bf(mine, got)
        part = rows // 4
        mine, rest = mine[:part], mine[part:]
        for bit in range(2, links.bits):
            size = mine.shape[0] // 2
            away = lax.dynamic_slice_in_dim(mine, (1 - links.bit_of(bit)) * size, size)
            near = lax.dynamic_slice_in_dim(mine, links.bit_of(bit) * size, size)
            mine = add_bf(near, links.swap_bit(away, bit))
            if rest.shape[0]:
                rest = add_bf(rest, links.swap_bit(rest, bit))
        return jnp.concatenate([mine, rest]) if rest.shape[0] else mine

    product_three = product(rows_three, joined_all, 0, [D] * 4)
    three = scatter_rest(product_three)
    kernel, inputs = after(
        functools.partial(hidden_kernel, rows),
        ends + full(dub, hidden, cotangent, vec_all) + parameters,
        product_three[:1],
    )
    dh, dh_bf, da, vec_second = call(
        kernel,
        inputs,
        [shape(D, f32), shape(D), shape(HID), shape(D, f32, 8)],
        weight_scratch(2) + weight_sem(2),
        5 * unit_cost,
        8 * rows * D,
    )
    dh_side = links.swap_bit(dh_bf, 0)
    dh_core = links.swap_core(dh_bf)
    dh_both = links.swap_core(dh_side)
    dh_all = [dh_bf, dh_core, dh_side, dh_both]
    product_two = product(
        rows_middle,
        n_two_all + joined_all,
        0,
        n_two_starts + [D] * 4,
        4 * HID + FF - 5 * rows,
        1,
        waits=[vec_second],
    )
    two = scatter_rest(product_two)
    kernel, inputs = after(
        functools.partial(attention_kernel, rows),
        ends + full(da, qkv, probs, dh, tokens, vec_all, vec_first, vec_second) + parameters,
        product_two[:1],
    )
    attention_out = call(
        kernel,
        inputs,
        [shape(D, f32)] + [shape(wide, bf16, count + vector_pad)] * 4,
        weight_scratch(1)
        + [
            pltpu.VMEM((count, 3 * HID), bf16),
            pltpu.VMEM((vector_pad, D), f32),
            pltpu.VMEM((vector_pad, wide), f32),
        ]
        + weight_sem(1),
        4 * unit_cost,
        4 * rows * D,
    )
    grad_tok = attention_out[0]
    rows_zero = share_rows(attention_out[1:])
    product_one = product(
        rows_middle,
        n_two_all + dh_all,
        wide,
        n_two_starts + [0] * 4,
        4 * HID - 2 * rows,
        0,
        waits=[grad_tok],
    )
    one = scatter_rest(product_one)
    product_zero = product(
        rows_zero, [vec_all, n_one] + joined_all[1:], 0, None, waits=product_one[:1]
    )
    zero = scatter_rest(product_zero)
    three = links.to_chip(three, {0: 1, 2: 3})
    two = links.to_chip(two, {0: 1, 3: 2})
    three = links.to_chip(three, {1: 3})
    two = links.to_chip(two, {1: 2})
    one = links.to_chip(one, {0: 1, 3: 2})
    one = links.to_chip(one, {2: 1})
    zero = links.to_chip(zero, {0: 1, 1: 0, 2: 3, 3: 2})
    mine = jnp.where(links.chip == 1, one, jnp.where(links.chip == 2, two, three))
    zero, mine = lax.optimization_barrier((zero, mine))
    zero = links.to_chip(zero, {0: 2, 2: 0})
    size = mine.shape[0]
    mine = jnp.where(links.chip == 0, zero[:size], mine)
    grad_w = links.gather_positions(mine).astype(f32)
    sums = zero[size:]
    got = links.along(sums, {0: 1, 2: 3})
    sums = jnp.where(links.chip % 2 == 0, sums, got).astype(f32)
    width = vectors.shape[1]
    grad_v = lax.dynamic_slice_in_dim(sums, lax.axis_index("shard") * width, width, 1)
    return out, grad_tok, grad_w, grad_v[: vectors.shape[0]]


def per_device(
    replicas,
    shards,
    tokens,
    segments,
    cotangent,
    weights,
    vectors,
    first_weights,
    first_vectors,
    second_weights,
    second_vectors,
):
    if Links.fits(replicas, shards, weights.shape[0]):
        output, grad_tokens, grad_w, grad_v = direct_step(
            Links(replicas, shards), tokens, segments, cotangent, weights, vectors
        )
    else:
        w_full = lax.all_gather(weights.astype(jnp.bfloat16), "shard", axis=0, tiled=True)
        v_full = lax.all_gather(vectors.astype(jnp.bfloat16), "shard", axis=1, tiled=True)
        output, kept_state = forward(tokens, segments, w_full, v_full)
        grad_tokens, grad_vec, row_terms, col_terms = backward(
            kept_state, cotangent, segments, w_full
        )
        local_grad = weight_grads(row_terms, col_terms).astype(jnp.bfloat16)
        own_w = lax.psum_scatter(local_grad, "shard", scatter_dimension=0, tiled=True)
        own_v = lax.psum_scatter(
            grad_vec.astype(jnp.bfloat16), "shard", scatter_dimension=1, tiled=True
        )
        grad_w = lax.psum(own_w, "rep").astype(jnp.float32)
        grad_v = lax.psum(own_v, "rep").astype(jnp.float32)
    new_w, new_fw, new_sw = adam_update(weights, first_weights, second_weights, grad_w, decay_rate)
    new_v, new_fv, new_sv = adam_update(vectors, first_vectors, second_vectors, grad_v, 0.0)
    return (output, grad_tokens, grad_w, grad_v, new_w, new_v, new_fw, new_fv, new_sw, new_sv)


def solution(mesh):
    placed = (
        P(("rep", "shard"), None),
        P(("rep", "shard"), None),
        P(("rep", "shard"), None),
        P("shard", None),
        P(None, "shard"),
        P("shard", None),
        P(None, "shard"),
        P("shard", None),
        P(None, "shard"),
    )
    return jax.shard_map(
        functools.partial(per_device, mesh.shape["rep"], mesh.shape["shard"]),
        mesh=mesh,
        in_specs=placed,
        out_specs=(
            P(("rep", "shard"), None),
            P(("rep", "shard"), None),
            P("shard", None),
            P(None, "shard"),
            P("shard", None),
            P(None, "shard"),
            P("shard", None),
            P(None, "shard"),
            P("shard", None),
            P(None, "shard"),
        ),
        check_vma=False,
    )
```

```python
import functools
import math

import jax
import jax.numpy as jnp
from jax import lax
from jax.experimental import pallas as pl
from jax.experimental.pallas import tpu as pltpu
from jax.sharding import PartitionSpec as P

D = 768
HEADS = 12
HEAD = 64
FF = 3072
STEP = 3
HID = 768
R = 9216


norm_eps = 1e-05
beta_one = 0.9
beta_two = 0.999
adam_eps = 1e-08
learn_rate = 0.2
decay_rate = 0.1
masked_score = -1e30


def normalize(values):
    centred = values - jnp.mean(values, axis=-1, keepdims=True)
    return centred * lax.rsqrt(jnp.mean(centred * centred, axis=-1, keepdims=True) + norm_eps)


def affine_norm(values, gain_vec, shift_vec):
    return normalize(values) * gain_vec + shift_vec


def gelu_tanh(values):
    return jax.nn.gelu(values, approximate=True)


def matmul(left_op, right_op):
    return jnp.dot(left_op, right_op, preferred_element_type=jnp.float32)


def matmul_nt(left_op, right_op):
    return lax.dot_general(
        left_op, right_op, (((1,), (1,)), ((), ())), preferred_element_type=jnp.float32
    )


def matmul_tn(left_op, right_op):
    return lax.dot_general(
        left_op, right_op, (((0,), (0,)), ((), ())), preferred_element_type=jnp.float32
    )


def product(pattern, left_op, right_op):
    return jnp.einsum(pattern, left_op, right_op, preferred_element_type=jnp.float32)


def allowed_pairs(segments):
    length = segments.shape[1]
    places = lax.broadcasted_iota(jnp.int32, (length, length), 0)
    others = lax.broadcasted_iota(jnp.int32, (length, length), 1)
    causal = others <= places
    same_doc = segments[:, :, None] == segments[:, None, :]
    return (causal[None] & same_doc)[:, None]


def scores_of(query_rows, key_rows, allowed):
    raw_scores = product("sqhd,skhd->shqk", query_rows, key_rows) * HEAD ** (-0.5)
    return jnp.where(allowed, raw_scores, masked_score)


def forward(tokens, segments, w_bf, v_bf):
    seq_count, length = segments.shape
    tok_count = tokens.shape[0]
    head_shape = (seq_count, length, HEADS, HEAD)
    floats = v_bf.astype(jnp.float32)
    residual = tokens.astype(jnp.float32)
    normed_one = affine_norm(residual, floats[0], floats[1]).astype(jnp.bfloat16)
    projected = matmul_nt(normed_one, w_bf[: 3 * HID])
    query_rows = (projected[:, :HID] + floats[2]).astype(jnp.bfloat16)
    key_rows = projected[:, HID : 2 * HID].astype(jnp.bfloat16)
    value_rows = (projected[:, 2 * HID :] + floats[3]).astype(jnp.bfloat16)
    allowed = allowed_pairs(segments)
    scores = scores_of(query_rows.reshape(head_shape), key_rows.reshape(head_shape), allowed)
    row_max = jnp.max(scores, axis=-1, keepdims=True)
    log_total = row_max + jnp.log(jnp.sum(jnp.exp(scores - row_max), axis=-1, keepdims=True))
    attn_probs = jnp.exp(scores - log_total).astype(jnp.bfloat16)
    mixed_heads = product("shqk,skhd->sqhd", attn_probs, value_rows.reshape(head_shape))
    attended = mixed_heads.reshape(tok_count, HID).astype(jnp.bfloat16)
    hidden_one = residual + matmul(attended, w_bf[3 * HID : 4 * HID]) + floats[4]
    normed_two = affine_norm(hidden_one, floats[5], floats[6]).astype(jnp.bfloat16)
    pre_act = matmul_nt(normed_two, w_bf[4 * HID : 4 * HID + FF]) + floats[7:11].reshape(FF)
    active = gelu_tanh(pre_act).astype(jnp.bfloat16)
    output = (hidden_one + matmul(active, w_bf[4 * HID + FF :]) + floats[11]).astype(jnp.bfloat16)
    kept_state = (
        residual,
        normed_one,
        query_rows,
        key_rows,
        value_rows,
        log_total,
        attended,
        hidden_one,
        normed_two,
        pre_act,
        active,
        floats,
    )
    return (output, kept_state)


def backward(kept_state, cotangent, segments, w_bf):
    (
        residual,
        normed_one,
        query_rows,
        key_rows,
        value_rows,
        log_total,
        attended,
        hidden_one,
        normed_two,
        pre_act,
        active,
        floats,
    ) = kept_state
    seq_count, length = segments.shape
    tok_count = residual.shape[0]
    head_shape = (seq_count, length, HEADS, HEAD)
    grad_out = cotangent.astype(jnp.float32)
    grad_active = matmul_nt(cotangent, w_bf[4 * HID + FF :])
    grad_pre = jax.vjp(gelu_tanh, pre_act)[1](grad_active)[0]
    grad_pre_bf = grad_pre.astype(jnp.bfloat16)
    grad_normed_two = matmul(grad_pre_bf, w_bf[4 * HID : 4 * HID + FF])
    norm_back_two = jax.vjp(affine_norm, hidden_one, floats[5], floats[6])[1]
    grad_h_part, grad_gain_two, grad_shift_two = norm_back_two(grad_normed_two)
    grad_hidden = grad_out + grad_h_part
    grad_hidden_bf = grad_hidden.astype(jnp.bfloat16)
    grad_attended = matmul_nt(grad_hidden_bf, w_bf[3 * HID : 4 * HID]).astype(jnp.bfloat16)
    query_four = query_rows.reshape(head_shape)
    key_four = key_rows.reshape(head_shape)
    value_four = value_rows.reshape(head_shape)
    grad_att_four = grad_attended.reshape(head_shape)
    allowed = allowed_pairs(segments)
    scores = scores_of(query_four, key_four, allowed)
    attn_probs = jnp.exp(scores - log_total)
    probs_bf = attn_probs.astype(jnp.bfloat16)
    grad_probs = product("sqhd,skhd->shqk", grad_att_four, value_four)
    inner_sum = jnp.sum(attn_probs * grad_probs, axis=-1, keepdims=True)
    grad_scores = (attn_probs * (grad_probs - inner_sum) * HEAD ** (-0.5)).astype(jnp.bfloat16)
    grad_query = product("shqk,skhd->sqhd", grad_scores, key_four).reshape(tok_count, HID)
    grad_keys = product("shqk,sqhd->skhd", grad_scores, query_four).reshape(tok_count, HID)
    grad_values = product("shqk,sqhd->skhd", probs_bf, grad_att_four).reshape(tok_count, HID)
    grad_proj = jnp.concatenate([grad_query, grad_keys, grad_values], axis=1)
    grad_proj_bf = grad_proj.astype(jnp.bfloat16)
    grad_normed_one = matmul(grad_proj_bf, w_bf[: 3 * HID])
    norm_back_one = jax.vjp(affine_norm, residual, floats[0], floats[1])[1]
    grad_r_part, grad_gain_one, grad_shift_one = norm_back_one(grad_normed_one)
    grad_tokens = grad_hidden + grad_r_part
    bias_ff = jnp.sum(grad_pre, axis=0).reshape(FF // D, D)
    head_rows = jnp.stack(
        [
            grad_gain_one,
            grad_shift_one,
            jnp.sum(grad_query, axis=0),
            jnp.sum(grad_values, axis=0),
            jnp.sum(grad_hidden, axis=0),
            grad_gain_two,
            grad_shift_two,
        ]
    )
    grad_vec = jnp.concatenate([head_rows, bias_ff, jnp.sum(grad_out, axis=0)[None]], axis=0)
    row_terms = jnp.concatenate([grad_proj_bf, attended, grad_pre_bf, active], axis=1)
    col_terms = jnp.stack([normed_one, grad_hidden_bf, normed_two, cotangent])
    return (grad_tokens, grad_vec, row_terms, col_terms)


def weight_grads(row_terms, col_terms):
    row_bounds = (0, 3 * HID, 4 * HID, 4 * HID + FF, R)
    pieces = [
        matmul_tn(row_terms[:, row_bounds[index] : row_bounds[index + 1]], col_terms[index])
        for index in range(4)
    ]
    return jnp.concatenate(pieces, axis=0)


def adam_update(param, first, second, grad, decay):
    new_first = beta_one * first + (1.0 - beta_one) * grad
    new_second = beta_two * second + (1.0 - beta_two) * grad * grad
    first_hat = new_first / (1.0 - beta_one**STEP)
    second_hat = new_second / (1.0 - beta_two**STEP)
    new_param = param - learn_rate * (first_hat / (jnp.sqrt(second_hat) + adam_eps) + decay * param)
    return (new_param, new_first, new_second)


def bit_reverse(index, bits):
    out = index * 0
    for place in range(bits):
        out = out * 2 + (index >> place) % 2
    return out


class Links:
    def __init__(self, replicas, shards):
        self.replicas = replicas
        self.cores = 2
        self.chips = shards // self.cores
        self.bits = replicas.bit_length() - 1
        self.replica = lax.axis_index("rep")
        shard = lax.axis_index("shard")
        self.chip = shard // self.cores
        self.core = shard % self.cores

    @staticmethod
    def fits(replicas, shards, rows):
        power = replicas > 2 and replicas & (replicas - 1) == 0
        return shards == 8 and power and 2 * rows == 3 * HID

    def send(self, value, target):
        route = []
        for rep in range(self.replicas):
            for chip in range(self.chips):
                for core in range(self.cores):
                    goal = target(rep, chip, core)
                    if goal is None:
                        continue
                    start = (rep * self.chips + chip) * self.cores + core
                    stop = (goal[0] * self.chips + goal[1]) * self.cores + goal[2]
                    route.append((start, stop))
        return lax.ppermute(value, ("rep", "shard"), route)

    def swap_core(self, value):
        return self.send(value, lambda rep, chip, core: (rep, chip, 1 - core))

    def swap_both(self, value, bit):
        return self.send(value, lambda rep, chip, core: (rep ^ (1 << bit), chip, 1 - core))

    def swap_bit(self, value, bit):
        return self.send(value, lambda rep, chip, core: (rep ^ (1 << bit), chip, core))

    def along(self, value, moves):
        table = dict(moves)
        return self.send(
            value, lambda rep, chip, core: (rep, table[chip], core) if chip in table else None
        )

    def bit_of(self, bit):
        return (self.replica >> bit) % 2

    def own_pieces(self, block):
        half = block.shape[0] // 2
        size = half // self.replicas
        first = lax.dynamic_slice_in_dim(block, self.replica * size, size)
        turned = bit_reverse(self.replica, self.bits)
        second = lax.dynamic_slice_in_dim(block, half + turned * size, size)
        return first, second

    def gather_pieces(self, first, second):
        for step in range(self.bits):
            low, high = step, self.bits - 1 - step
            got_first = self.swap_bit(first, low)
            got_second = self.swap_bit(second, high)
            if step == self.bits - 1:
                return [first, got_first, second, got_second]
            first = jnp.where(
                self.bit_of(low) == 0,
                jnp.concatenate([first, got_first]),
                jnp.concatenate([got_first, first]),
            )
            second = jnp.where(
                self.bit_of(high) == 0,
                jnp.concatenate([second, got_second]),
                jnp.concatenate([got_second, second]),
            )

    def gather_positions(self, piece):
        size = piece.shape[0] // 2
        first, second = piece[:size], piece[size:]
        for step in range(self.bits):
            high, low = self.bits - 1 - step, step
            got_first = self.swap_bit(first, high)
            got_second = self.swap_bit(second, low)
            if step == self.bits - 1:
                return (first, second), (got_first, got_second)
            first = jnp.where(
                self.bit_of(high) == 0,
                jnp.concatenate([first, got_first]),
                jnp.concatenate([got_first, first]),
            )
            second = jnp.where(
                self.bit_of(low) == 0,
                jnp.concatenate([second, got_second]),
                jnp.concatenate([got_second, second]),
            )

    def position_table(self, other):
        half = self.replicas // 2
        low, high = self.bit_of(0), self.bit_of(self.bits - 1)
        if other:
            low, high = 1 - low, 1 - high
        steps = jnp.arange(half, dtype=jnp.int32)
        firsts = 2 * (low * half + steps)
        seconds = 2 * bit_reverse(high * half + steps, self.bits) + 1
        return jnp.concatenate([firsts, seconds]).astype(jnp.int32)

    def place_pieces(self, own, got):
        half = self.replicas // 2
        size = own[0].shape[0] // half
        whole = jnp.zeros((4 * own[0].shape[0],) + own[0].shape[1:], own[0].dtype)
        for parts, other in ((own, False), (got, True)):
            table = self.position_table(other)
            for index in range(2 * half):
                part = parts[index // half]
                start = (index % half) * size
                whole = lax.dynamic_update_slice_in_dim(
                    whole, part[start : start + size], table[index] * size, 0
                )
        return whole

    def to_chip(self, piece, moves):
        got = self.along(piece, moves)
        return add_bf(piece, got)


def add_bf(left, right):
    return (left.astype(jnp.float32) + right.astype(jnp.float32)).astype(jnp.bfloat16)


vector_pad = 16


def dot(left, right, left_dim, right_dim):
    return lax.dot_general(
        left,
        right,
        (((left_dim,), (right_dim,)), ((), ())),
        preferred_element_type=jnp.float32,
    )


def norm_parts(values):
    centred = values - jnp.mean(values, axis=-1, keepdims=True)
    scale = lax.rsqrt(jnp.mean(centred * centred, axis=-1, keepdims=True) + norm_eps)
    return centred * scale, scale


def norm_back(unit, scale, grad):
    inner = jnp.mean(grad, axis=-1, keepdims=True)
    outer = jnp.mean(grad * unit, axis=-1, keepdims=True)
    return scale * (grad - inner - unit * outer)


def row_sum(values):
    return jnp.sum(values, axis=0, keepdims=True)


def left_lanes(value):
    return lax.broadcasted_iota(jnp.int32, value.shape, 1) < HEAD


def head_parts(pair):
    left = left_lanes(pair)
    none = jnp.zeros_like(pair)
    return jnp.where(left, pair, none), jnp.where(left, none, pair)


def load_blocks(place, blocks, rows, target, sem, first, last):
    quarter = rows // 4
    starts = (
        place[7] * quarter,
        (1 - place[7]) * quarter,
        (2 + place[5]) * quarter,
        (3 - place[5]) * quarter,
    )
    for slot in range(4):
        chip = place[slot]

        @pl.when((chip >= first) & (chip < last))
        def _():
            for side in range(2):
                core = place[4] if side == 0 else 1 - place[4]
                number = (chip - first) * 2 + core
                if slot == 0:
                    parts = [(blocks[side], 0, rows)]
                else:
                    at = 2 + (slot - 1) * 8 + side
                    parts = [
                        (blocks[at + 2 * index], starts[index], quarter) for index in range(4)
                    ]
                for ref, shift, size in parts:
                    start = pl.multiple_of(number * rows + shift, 16)
                    pltpu.make_async_copy(ref, target.at[pl.ds(start, size)], sem.at[number]).start()

    done = set()

    def ready(low, high):
        for number in range(low // rows, -(-high // rows)):
            if number in done:
                continue
            done.add(number)
            index = number - 2 * first
            pltpu.make_async_copy(
                blocks[0], target.at[pl.ds(index * rows, rows)], sem.at[index]
            ).wait()

    return ready


block_count = 26


def spread_terms(place, terms, rows, first, outs, wide, lane=0):
    core, across = place[4], place[5]
    count = terms.shape[0]
    for index, out in enumerate(outs):
        block = core if index % 2 == 0 else 1 - core
        side = across if index < 2 else 1 - across
        start = pl.multiple_of(first + block * rows + side * (rows - wide), 128)
        out[:count, lane : lane + wide] = terms[:, pl.ds(start, wide)]


def query_kernel(rows, place, tok, seg_col, seg_row, vec_all, *rest):
    blocks = rest[:block_count]
    n_out, qkv, probs, att, w_in, load_sem = rest[block_count:]
    ready = load_blocks(place, blocks, rows, w_in, load_sem, 0, 1)
    unit, _ = norm_parts(tok[...].astype(jnp.float32))
    n_one = (unit * vec_all[0:1, :] + vec_all[1:2, :]).astype(jnp.bfloat16)
    n_out[...] = n_one
    for index, bias in enumerate((vec_all[2:3, :], None, vec_all[3:4, :])):
        ready(index * HID, (index + 1) * HID)
        value = dot(n_one, w_in[index * HID : (index + 1) * HID], 1, 1)
        if bias is not None:
            value = value + bias
        qkv[:, index * HID : (index + 1) * HID] = value.astype(jnp.bfloat16)
    length = seg_row.shape[1]
    for seq in range(seg_row.shape[0]):
        span = slice(seq * length, (seq + 1) * length)
        order = lax.broadcasted_iota(jnp.int32, (length, length), 0)
        other = lax.broadcasted_iota(jnp.int32, (length, length), 1)
        allowed = (other <= order) & (seg_col[span, :] == seg_row[seq : seq + 1, :])
        for pair in range(HEADS // 2):
            lanes = slice(pair * 2 * HEAD, (pair + 1) * 2 * HEAD)
            key_pair = qkv[span, HID + lanes.start : HID + lanes.stop]
            value_pair = qkv[span, 2 * HID + lanes.start : 2 * HID + lanes.stop]
            mixed = []
            for half, query in enumerate(head_parts(qkv[span, lanes])):
                raw = dot(query, key_pair, 1, 1) * HEAD ** (-0.5)
                raw = jnp.where(allowed, raw, masked_score)
                top = jnp.max(raw, axis=-1, keepdims=True)
                power = jnp.exp(raw - top)
                prob = power * (1.0 / jnp.sum(power, axis=-1, keepdims=True))
                probs[seq * HEADS + 2 * pair + half] = prob
                mixed.append(dot(prob.astype(jnp.bfloat16), value_pair, 1, 0))
            att[span, lanes] = jnp.where(left_lanes(mixed[0]), mixed[0], mixed[1]).astype(
                jnp.bfloat16
            )


def active_kernel(rows, place, tok, att, vec_all, *rest):
    blocks = rest[:block_count]
    n_out, hidden, act, slope_out = rest[block_count : block_count + 4]
    windows = rest[block_count + 4 : block_count + 8]
    w_mid, load_sem = rest[block_count + 8 :]
    ready = load_blocks(place, blocks, rows, w_mid, load_sem, 1, 3)
    base = 2 * rows

    def weight(first, size):
        ready(first, first + size)
        return w_mid[first - base : first - base + size]

    h_value = tok[...].astype(jnp.float32) + dot(att[...], weight(3 * HID, HID), 1, 0)
    h_value = h_value + vec_all[4:5, :]
    hidden[...] = h_value
    unit, _ = norm_parts(h_value)
    n_two = (unit * vec_all[5:6, :] + vec_all[6:7, :]).astype(jnp.bfloat16)
    n_out[...] = n_two
    root = math.sqrt(2.0 / math.pi)
    for index in range(FF // D):
        span = slice(index * D, (index + 1) * D)
        pre = dot(n_two, weight(4 * HID + index * D, D), 1, 1) + vec_all[7 + index : 8 + index, :]
        squared = pre * pre
        bent = jnp.tanh(root * (pre + 0.044715 * (pre * squared)))
        half = 0.5 * (1.0 + bent)
        act[:, span] = (pre * half).astype(jnp.bfloat16)
        slope_out[:, span] = half + 0.5 * pre * (1.0 - bent * bent) * (
            root * (1.0 + 3 * 0.044715 * squared)
        )
    wide = windows[0].shape[1]
    spread_terms(place, act, rows, 6 * rows - (4 * HID + FF), windows, wide)
    windows[1][:, wide:] = n_two
    windows[2][:, wide:] = n_two
    ready(2 * rows, 6 * rows)


def change_kernel(rows, place, cot, att, act, slope, hidden, vec_all, *rest):
    blocks = rest[:block_count]
    rest = rest[block_count:]
    out, dub, vec_out = rest[:3]
    windows = rest[3:7]
    w_top, terms, load_sem = rest[7:]
    ready = load_blocks(place, blocks, rows, w_top, load_sem, 2, 4)
    base = 4 * rows
    terms[:, :HID] = att[...]
    result = hidden[...] + vec_all[11:12, :]
    for index in range(FF // D):
        span = slice(index * D, (index + 1) * D)
        first = 4 * HID + FF + index * D - base
        ready(first + base, first + base + D)
        weight = w_top[first : first + D]
        active = act[:, span]
        change = dot(cot[...], weight, 1, 1) * slope[:, span]
        change_bf = change.astype(jnp.bfloat16)
        dub[:, span] = change_bf
        terms[:, HID + index * D : HID + (index + 1) * D] = change_bf
        terms[:, HID + FF + index * D : HID + FF + (index + 1) * D] = active
        vec_out[index : index + 1, :] = row_sum(change)
        result = result + dot(active, weight, 1, 0)
    wide = windows[0].shape[1] // 2
    spread_terms(place, terms, rows, 2 * rows, windows, wide)
    spread_terms(place, terms, rows, 0, windows, wide, wide)
    out[...] = result.astype(jnp.bfloat16)
    vec_out[4:5, :] = row_sum(cot[...].astype(jnp.float32))
    vec_out[5:8, :] = jnp.zeros((3, D), jnp.float32)
    ready(4 * rows, 8 * rows)


def hidden_kernel(rows, place, dub, hidden, cot, vec_all, *rest):
    blocks = rest[:block_count]
    dh, dh_bf, da, vec_out, w_mid, load_sem = rest[block_count:]
    ready = load_blocks(place, blocks, rows, w_mid, load_sem, 1, 3)
    base = 2 * rows
    unit, scale = norm_parts(hidden[...])
    start = 4 * HID
    back = None
    while start < 4 * HID + FF:
        stop = min((start // rows + 1) * rows, 4 * HID + FF)
        ready(start, stop)
        part = dot(dub[:, start - 4 * HID : stop - 4 * HID], w_mid[start - base : stop - base], 1, 0)
        back = part if back is None else back + part
        start = stop
    vec_out[0:1, :] = row_sum(back * unit)
    vec_out[1:2, :] = row_sum(back)
    value = cot[...].astype(jnp.float32) + norm_back(unit, scale, back * vec_all[5:6, :])
    dh[...] = value
    vec_out[2:3, :] = row_sum(value)
    vec_out[3:8, :] = jnp.zeros((5, D), jnp.float32)
    rounded = value.astype(jnp.bfloat16)
    dh_bf[...] = rounded
    da[...] = dot(rounded, w_mid[3 * HID - base : 4 * HID - base], 1, 1).astype(jnp.bfloat16)


def attention_kernel(rows, place, da, qkv, probs, dh, tok, vec_all, vec_first, vec_second, *rest):
    blocks = rest[:block_count]
    rest = rest[block_count:]
    grad_tok = rest[0]
    windows = rest[1:5]
    w_in, dqkv, vec_out, packed, load_sem = rest[5:]
    ready = load_blocks(place, blocks, rows, w_in, load_sem, 0, 1)
    heads_total = probs.shape[0]
    length = probs.shape[1]
    vec_out[2:4, :] = jnp.zeros((2, D), jnp.float32)
    for seq in range(heads_total // HEADS):
        span = slice(seq * length, (seq + 1) * length)
        for pair in range(HEADS // 2):
            lanes = slice(pair * 2 * HEAD, (pair + 1) * 2 * HEAD)
            query_pair = qkv[span, lanes]
            key_pair = qkv[span, HID + lanes.start : HID + lanes.stop]
            value_pair = qkv[span, 2 * HID + lanes.start : 2 * HID + lanes.stop]
            da_pair = da[span, lanes]
            got = []
            for half, da_head in enumerate(head_parts(da_pair)):
                prob = probs[seq * HEADS + 2 * pair + half]
                grad_prob = dot(da_head, value_pair, 1, 1)
                inner = jnp.sum(prob * grad_prob, axis=-1, keepdims=True)
                grad_score = (prob * (grad_prob - inner) * HEAD ** (-0.5)).astype(jnp.bfloat16)
                got.append(
                    (
                        dot(grad_score, key_pair, 1, 0),
                        dot(grad_score, query_pair, 0, 0),
                        dot(prob.astype(jnp.bfloat16), da_pair, 0, 0),
                    )
                )
            left = left_lanes(got[0][0])
            query_grad, key_grad, value_grad = [
                jnp.where(left, one, two) for one, two in zip(got[0], got[1])
            ]
            dqkv[span, lanes] = query_grad.astype(jnp.bfloat16)
            dqkv[span, HID + lanes.start : HID + lanes.stop] = key_grad.astype(jnp.bfloat16)
            dqkv[span, 2 * HID + lanes.start : 2 * HID + lanes.stop] = value_grad.astype(
                jnp.bfloat16
            )
            vec_out[2:3, lanes] = vec_out[2:3, lanes] + row_sum(query_grad)
            vec_out[3:4, lanes] = vec_out[3:4, lanes] + row_sum(value_grad)
    unit, scale = norm_parts(tok[...].astype(jnp.float32))
    ready(0, 2 * rows)
    back = dot(dqkv[...], w_in[...], 1, 0)
    grad_tok[...] = dh[...] + norm_back(unit, scale, back * vec_all[0:1, :])
    vec_out[0:1, :] = row_sum(back * unit)
    vec_out[1:2, :] = row_sum(back)
    vec_out[4:5, :] = vec_second[2:3, :]
    vec_out[5:7, :] = vec_second[0:2, :]
    vec_out[7:12, :] = vec_first[0:5, :]
    wide = windows[0].shape[1]
    spread_terms(place, dqkv, rows, 0, windows, wide)
    packed[...] = jnp.zeros_like(packed)
    for at, lanes, row, source in vector_tiles(wide):
        packed[at : at + 1, lanes] = vec_out[row : row + 1, source]
    for window in windows:
        window[dqkv.shape[0] :, :] = packed[...].astype(jnp.bfloat16)


def vector_tiles(wide):
    across, packed = D // 128, wide // 128
    for index in range(12 * across):
        at, to = divmod(index, packed)
        row, source = divmod(index, across)
        yield at, slice(to * 128, to * 128 + 128), row, slice(source * 128, source * 128 + 128)


def product_kernel(rows, wide, lane, starts, split, which, place, *rest):
    last = split is None and starts is None
    terms, columns, rest = rest[:4], rest[4:-6], rest[-6:]
    away, mine, left, right, whole, sums = rest
    if last:
        vec_all, columns = columns[0], columns[1:]
    count = columns[0].shape[0]
    for index in range(4):
        left[index * count : (index + 1) * count] = terms[index][:count, lane : lane + wide]
    core, across, high = place[4], place[5], place[6]

    def column(index):
        value = columns[index]
        if last and index > 0:
            unit, _ = norm_parts(value[:, :D].astype(jnp.float32))
            return (unit * vec_all[0:1, :] + vec_all[1:2, :]).astype(jnp.bfloat16)
        start = 0 if last else starts[index]
        return value[:, start : start + D]

    def put(span, other):
        for index in range(4):
            value = column(index)
            if other is not None:
                value = jnp.where(other, column(4 + index), value)
            right[index * count : (index + 1) * count] = value
        whole[span, :] = dot(left[:, span], right[...], 0, 0).astype(jnp.bfloat16)

    if split is None:
        put(slice(0, wide), None)
    else:
        start = rows - wide
        chosen = core == which
        if split <= start:
            put(slice(0, split), chosen & (across == 1))
            put(slice(split, wide), chosen)
        else:
            put(slice(0, split - start), chosen)
            put(slice(split - start, wide), chosen & (across == 0))
    part = rows // 4
    first = across * (wide - rows // 2)
    away[:part] = whole[pl.ds(pl.multiple_of(first + (1 - high) * part, 16), part), :]
    mine[:part] = whole[pl.ds(pl.multiple_of(first + high * part, 16), part), :]
    if last:
        total = terms[0][count:, :].astype(jnp.float32)
        for index in range(1, 4):
            total = total + terms[index][count:, :].astype(jnp.float32)
        sums[...] = jnp.zeros_like(sums)
        for at, lanes, row, source in vector_tiles(wide):
            sums[row : row + 1, source] = total[at : at + 1, lanes]
        away[part:] = sums[...].astype(jnp.bfloat16)
        mine[part:] = sums[...].astype(jnp.bfloat16)


def adam_kernel(table, first, second, param, one, two, *rest):
    grad_out, param_out, one_out, two_out = rest[-4:]
    early = pl.program_id(0) < pl.num_programs(0) // 2
    grad = jnp.where(early, first[...], second[...]).astype(jnp.float32)
    grad_out[...] = grad
    param_out[...], one_out[...], two_out[...] = adam_update(
        param[...], one[...], two[...], grad, decay_rate
    )


def adam_pieces(table, parts, state, earlier):
    half = table.shape[0] // 2
    size = parts[0].shape[0] // half
    width = parts[0].shape[1]
    piece = pl.BlockSpec((size, width), lambda step, table: (table[step], 0))
    outputs = [jax.ShapeDtypeStruct(state[0].shape, jnp.float32)] * 4
    return pl.pallas_call(
        adam_kernel,
        out_shape=outputs,
        grid_spec=pltpu.PrefetchScalarGridSpec(
            num_scalar_prefetch=1,
            grid=(2 * half,),
            in_specs=[
                pl.BlockSpec((size, width), lambda step, table: (jnp.minimum(step, half - 1), 0)),
                pl.BlockSpec((size, width), lambda step, table: (jnp.maximum(step - half, 0), 0)),
                piece,
                piece,
                piece,
            ]
            + [any_spec] * len(earlier),
            out_specs=[piece] * 4,
        ),
        input_output_aliases={6 + index: index for index in range(len(earlier))},
        cost_estimate=pl.CostEstimate(
            flops=20 * state[0].size, bytes_accessed=14 * state[0].size, transcendentals=0
        ),
    )(table, *parts, *state, *earlier)


any_spec = pl.BlockSpec(memory_space=pl.ANY)
vmem_spec = pl.BlockSpec(memory_space=pltpu.VMEM)
smem_spec = pl.BlockSpec(memory_space=pltpu.SMEM)
bf16, f32 = jnp.bfloat16, jnp.float32


def call(kernel, inputs, outputs, scratch, flops, moved):
    return pl.pallas_call(
        kernel,
        grid=(1,),
        in_specs=[spec for _, spec in inputs],
        out_specs=[spec for _, _, spec in outputs],
        out_shape=[jax.ShapeDtypeStruct(shape, kind) for shape, kind, _ in outputs],
        scratch_shapes=scratch,
        compiler_params=pltpu.CompilerParams(vmem_limit_bytes=60 * 1024 * 1024),
        cost_estimate=pl.CostEstimate(flops=flops, bytes_accessed=moved, transcendentals=0),
    )(*[value for value, _ in inputs])


def after(kernel, inputs, waits):
    count, extra = len(inputs), len(waits)

    def body(*refs):
        kernel(*refs[:count], *refs[count + extra :])

    return body, inputs + [(value, any_spec) for value in waits]


def parameter_blocks(links, weights, vectors):
    shards = links.chips * links.cores
    width = vectors.shape[1]
    number = links.chip * links.cores + links.core
    location = lax.broadcasted_iota(jnp.int32, (vectors.shape[0], width * shards), 1) // width
    spread = jnp.where(location == number, jnp.tile(vectors, (1, shards)), 0.0)
    spread = jnp.pad(spread, ((0, vector_pad - vectors.shape[0]), (0, 0))).astype(bf16)
    first, second = links.own_pieces(weights)
    size = first.shape[0]
    mine = jnp.concatenate([first.astype(bf16), second.astype(bf16), spread])
    inner = (links.chip == 1) | (links.chip == 2)
    near = links.along(mine, {0: 1, 1: 0, 2: 3, 3: 2})
    middle = links.along(mine, {1: 2, 2: 1})
    across = links.along(near, {1: 2, 2: 1})
    outward = links.along(middle, {1: 0, 2: 3})
    far = links.along(across, {1: 0, 2: 3})
    block = weights.astype(bf16)
    blocks = [block, links.swap_core(block)]
    slots = (near, jnp.where(inner, middle, outward), jnp.where(inner, across, far))
    total = spread
    for slot in slots:
        total = total + slot[2 * size :]
        for piece in links.gather_pieces(slot[:size], slot[size : 2 * size]):
            blocks += [piece, links.swap_core(piece)]
    total = total + links.swap_core(total)
    return blocks, total.astype(f32)


def direct_step(links, tokens, segments, cotangent, state, vectors):
    count = tokens.shape[0]
    weights = state[0]
    rows = weights.shape[0]
    wide = -(-rows // 256) * 128
    blocks, vec_all = parameter_blocks(links, weights, vectors)
    low = links.chip < links.chips // 2
    place = jnp.stack(
        [
            links.chip,
            links.chip ^ 1,
            jnp.where(low, 2, 1),
            jnp.where(low, 3, 0),
            links.core,
            links.bit_of(0),
            links.bit_of(1),
            links.bit_of(links.bits - 1),
        ]
    ).astype(jnp.int32)
    ends = [(place, smem_spec)]
    pairs = segments.shape[0] * HEADS
    length = segments.shape[1]
    unit_cost = 2 * count * HID * D
    parameters = [(block, any_spec) for block in blocks]

    def full(*arrays):
        return [(array, vmem_spec) for array in arrays]

    def shape(width, kind=bf16, height=count):
        return (height, width), kind, vmem_spec

    def weight_scratch(chips):
        return [pltpu.VMEM((chips * 2 * rows, D), bf16)]

    def weight_sem(chips):
        return [pltpu.SemaphoreType.DMA((chips * 2,))]

    def share_rows(parts):
        own, to_core, to_side, to_both = parts
        side = links.swap_bit(to_side, 0)
        both = links.swap_both(to_both, 0)
        other = links.swap_core(to_core)
        return [own, other, side, both]

    joined = jnp.concatenate([tokens, cotangent], axis=1)
    joined_side = links.swap_bit(joined, 0)
    joined_core = links.swap_core(joined)
    joined_both = links.swap_core(joined_side)
    joined_all = [joined, joined_core, joined_side, joined_both]
    n_one, qkv, probs, att = call(
        functools.partial(query_kernel, rows),
        ends + full(tokens, segments.reshape(count, 1), segments, vec_all) + parameters,
        [
            shape(D),
            shape(3 * HID),
            ((pairs, length, length), f32, vmem_spec),
            shape(HID),
        ],
        weight_scratch(1) + weight_sem(1),
        4 * unit_cost,
        6 * HID * D,
    )
    active_out = call(
        functools.partial(active_kernel, rows),
        ends + full(tokens, att, vec_all) + parameters,
        [shape(D), shape(D, f32), shape(FF), shape(FF, f32)]
        + [shape(wide), shape(wide + D), shape(wide + D), shape(wide)],
        weight_scratch(2) + weight_sem(2),
        5 * unit_cost,
        8 * rows * D,
    )
    n_two, hidden, act, slope = active_out[:4]
    rows_three = share_rows(active_out[4:])
    n_two_both = links.swap_core(rows_three[2])
    n_two_all = [n_two, rows_three[1], rows_three[2], n_two_both]
    n_two_starts = [0, wide, wide, wide]
    change_out = call(
        functools.partial(change_kernel, rows),
        ends + full(cotangent, att, act, slope, hidden, vec_all) + parameters,
        [shape(D), shape(FF), shape(D, f32, 8)] + [shape(2 * wide)] * 4,
        weight_scratch(2) + [pltpu.VMEM((count, HID + 2 * FF), bf16)] + weight_sem(2),
        8 * unit_cost,
        8 * rows * D,
    )
    out, dub, vec_first = change_out[:3]
    rows_middle = share_rows(change_out[3:])

    def product(parts, columns, lane, starts, split=None, which=0, waits=()):
        extra = 0 if starts is not None else vector_pad
        kernel, inputs = after(
            functools.partial(product_kernel, rows, wide, lane, starts, split, which),
            ends + full(*parts) + full(*columns),
            list(waits),
        )
        return call(
            kernel,
            inputs,
            [shape(D, bf16, rows // 4 + extra)] * 2,
            [
                pltpu.VMEM((4 * count, wide), bf16),
                pltpu.VMEM((4 * count, D), bf16),
                pltpu.VMEM((wide, D), bf16),
                pltpu.VMEM((vector_pad, D), f32),
            ],
            8 * count * wide * D,
            4 * rows * D,
        )

    def scatter_rest(parts):
        away, mine = parts
        got = links.swap_bit(away, 1)
        mine = add_bf(mine, got)
        part = rows // 4
        mine, rest = mine[:part], mine[part:]
        for bit in range(2, links.bits):
            size = mine.shape[0] // 2
            away = lax.dynamic_slice_in_dim(mine, (1 - links.bit_of(bit)) * size, size)
            near = lax.dynamic_slice_in_dim(mine, links.bit_of(bit) * size, size)
            mine = add_bf(near, links.swap_bit(away, bit))
            if rest.shape[0]:
                rest = add_bf(rest, links.swap_bit(rest, bit))
        return jnp.concatenate([mine, rest]) if rest.shape[0] else mine

    product_three = product(rows_three, joined_all, 0, [D] * 4)
    three = scatter_rest(product_three)
    kernel, inputs = after(
        functools.partial(hidden_kernel, rows),
        ends + full(dub, hidden, cotangent, vec_all) + parameters,
        product_three[:1],
    )
    dh, dh_bf, da, vec_second = call(
        kernel,
        inputs,
        [shape(D, f32), shape(D), shape(HID), shape(D, f32, 8)],
        weight_scratch(2) + weight_sem(2),
        5 * unit_cost,
        8 * rows * D,
    )
    dh_side = links.swap_bit(dh_bf, 0)
    dh_core = links.swap_core(dh_bf)
    dh_both = links.swap_core(dh_side)
    dh_all = [dh_bf, dh_core, dh_side, dh_both]
    product_two = product(
        rows_middle,
        n_two_all + joined_all,
        0,
        n_two_starts + [D] * 4,
        4 * HID + FF - 5 * rows,
        1,
        waits=[vec_second],
    )
    two = scatter_rest(product_two)
    product_one = product(
        rows_middle,
        n_two_all + dh_all,
        wide,
        n_two_starts + [0] * 4,
        4 * HID - 2 * rows,
        0,
        waits=product_two[:1],
    )
    one = scatter_rest(product_one)
    kernel, inputs = after(
        functools.partial(attention_kernel, rows),
        ends + full(da, qkv, probs, dh, tokens, vec_all, vec_first, vec_second) + parameters,
        product_one[:1],
    )
    attention_out = call(
        kernel,
        inputs,
        [shape(D, f32)] + [shape(wide, bf16, count + vector_pad)] * 4,
        weight_scratch(1)
        + [
            pltpu.VMEM((count, 3 * HID), bf16),
            pltpu.VMEM((vector_pad, D), f32),
            pltpu.VMEM((vector_pad, wide), f32),
        ]
        + weight_sem(1),
        4 * unit_cost,
        4 * rows * D,
    )
    grad_tok = attention_out[0]
    rows_zero = share_rows(attention_out[1:])
    product_zero = product(rows_zero, [vec_all, n_one] + joined_all[1:], 0, None)
    zero = scatter_rest(product_zero)
    three = links.to_chip(three, {0: 1, 2: 3})
    two, grad_tok = lax.optimization_barrier((two, grad_tok))
    two = links.to_chip(two, {0: 1, 3: 2})
    three = links.to_chip(three, {1: 3})
    two = links.to_chip(two, {1: 2})
    one = links.to_chip(one, {0: 1, 3: 2})
    one = links.to_chip(one, {2: 1})
    zero = links.to_chip(zero, {0: 1, 1: 0, 2: 3, 3: 2})
    mine = jnp.where(links.chip == 1, one, jnp.where(links.chip == 2, two, three))
    zero, mine = lax.optimization_barrier((zero, mine))
    zero = links.to_chip(zero, {0: 2, 2: 0})
    size = mine.shape[0]
    mine = jnp.where(links.chip == 0, zero[:size], mine)
    own, late = links.gather_positions(mine)
    sums = zero[size:]
    got = links.along(sums, {0: 1, 2: 3})
    sums = jnp.where(links.chip % 2 == 0, sums, got).astype(f32)
    width = vectors.shape[1]
    grad_v = lax.dynamic_slice_in_dim(sums, lax.axis_index("shard") * width, width, 1)
    if own[0].shape[0] % (8 * links.replicas):
        grad_w = links.place_pieces(own, late).astype(f32)
        new = [grad_w] + list(adam_update(*state, grad_w, decay_rate))
    else:
        new = adam_pieces(links.position_table(False), own, state, [])
        new = adam_pieces(links.position_table(True), late, state, new)
    return out, grad_tok, grad_v[: vectors.shape[0]], new


def per_device(
    replicas,
    shards,
    tokens,
    segments,
    cotangent,
    weights,
    vectors,
    first_weights,
    first_vectors,
    second_weights,
    second_vectors,
):
    if Links.fits(replicas, shards, weights.shape[0]):
        output, grad_tokens, grad_v, new = direct_step(
            Links(replicas, shards),
            tokens,
            segments,
            cotangent,
            (weights, first_weights, second_weights),
            vectors,
        )
    else:
        w_full = lax.all_gather(weights.astype(jnp.bfloat16), "shard", axis=0, tiled=True)
        v_full = lax.all_gather(vectors.astype(jnp.bfloat16), "shard", axis=1, tiled=True)
        output, kept_state = forward(tokens, segments, w_full, v_full)
        grad_tokens, grad_vec, row_terms, col_terms = backward(
            kept_state, cotangent, segments, w_full
        )
        local_grad = weight_grads(row_terms, col_terms).astype(jnp.bfloat16)
        own_w = lax.psum_scatter(local_grad, "shard", scatter_dimension=0, tiled=True)
        own_v = lax.psum_scatter(
            grad_vec.astype(jnp.bfloat16), "shard", scatter_dimension=1, tiled=True
        )
        grad_w = lax.psum(own_w, "rep").astype(jnp.float32)
        grad_v = lax.psum(own_v, "rep").astype(jnp.float32)
        new = [grad_w]
        new += adam_update(weights, first_weights, second_weights, grad_w, decay_rate)
    grad_w, new_w, new_fw, new_sw = new
    new_v, new_fv, new_sv = adam_update(vectors, first_vectors, second_vectors, grad_v, 0.0)
    return (output, grad_tokens, grad_w, grad_v, new_w, new_v, new_fw, new_fv, new_sw, new_sv)


def solution(mesh):
    placed = (
        P(("rep", "shard"), None),
        P(("rep", "shard"), None),
        P(("rep", "shard"), None),
        P("shard", None),
        P(None, "shard"),
        P("shard", None),
        P(None, "shard"),
        P("shard", None),
        P(None, "shard"),
    )
    return jax.shard_map(
        functools.partial(per_device, mesh.shape["rep"], mesh.shape["shard"]),
        mesh=mesh,
        in_specs=placed,
        out_specs=(
            P(("rep", "shard"), None),
            P(("rep", "shard"), None),
            P("shard", None),
            P(None, "shard"),
            P("shard", None),
            P(None, "shard"),
            P("shard", None),
            P(None, "shard"),
            P("shard", None),
            P(None, "shard"),
        ),
        check_vma=False,
    )
```

```python
import functools
import math

import jax
import jax.numpy as jnp
from jax import lax
from jax.experimental import pallas as pl
from jax.experimental.pallas import tpu as pltpu
from jax.sharding import PartitionSpec as P

D = 768
HEADS = 12
HEAD = 64
FF = 3072
STEP = 3
HID = 768
R = 9216


norm_eps = 1e-05
beta_one = 0.9
beta_two = 0.999
adam_eps = 1e-08
learn_rate = 0.2
decay_rate = 0.1
masked_score = -1e30


def normalize(values):
    centred = values - jnp.mean(values, axis=-1, keepdims=True)
    return centred * lax.rsqrt(jnp.mean(centred * centred, axis=-1, keepdims=True) + norm_eps)


def affine_norm(values, gain_vec, shift_vec):
    return normalize(values) * gain_vec + shift_vec


def gelu_tanh(values):
    return jax.nn.gelu(values, approximate=True)


def matmul(left_op, right_op):
    return jnp.dot(left_op, right_op, preferred_element_type=jnp.float32)


def matmul_nt(left_op, right_op):
    return lax.dot_general(
        left_op, right_op, (((1,), (1,)), ((), ())), preferred_element_type=jnp.float32
    )


def matmul_tn(left_op, right_op):
    return lax.dot_general(
        left_op, right_op, (((0,), (0,)), ((), ())), preferred_element_type=jnp.float32
    )


def product(pattern, left_op, right_op):
    return jnp.einsum(pattern, left_op, right_op, preferred_element_type=jnp.float32)


def allowed_pairs(segments):
    length = segments.shape[1]
    places = lax.broadcasted_iota(jnp.int32, (length, length), 0)
    others = lax.broadcasted_iota(jnp.int32, (length, length), 1)
    causal = others <= places
    same_doc = segments[:, :, None] == segments[:, None, :]
    return (causal[None] & same_doc)[:, None]


def scores_of(query_rows, key_rows, allowed):
    raw_scores = product("sqhd,skhd->shqk", query_rows, key_rows) * HEAD ** (-0.5)
    return jnp.where(allowed, raw_scores, masked_score)


def forward(tokens, segments, w_bf, v_bf):
    seq_count, length = segments.shape
    tok_count = tokens.shape[0]
    head_shape = (seq_count, length, HEADS, HEAD)
    floats = v_bf.astype(jnp.float32)
    residual = tokens.astype(jnp.float32)
    normed_one = affine_norm(residual, floats[0], floats[1]).astype(jnp.bfloat16)
    projected = matmul_nt(normed_one, w_bf[: 3 * HID])
    query_rows = (projected[:, :HID] + floats[2]).astype(jnp.bfloat16)
    key_rows = projected[:, HID : 2 * HID].astype(jnp.bfloat16)
    value_rows = (projected[:, 2 * HID :] + floats[3]).astype(jnp.bfloat16)
    allowed = allowed_pairs(segments)
    scores = scores_of(query_rows.reshape(head_shape), key_rows.reshape(head_shape), allowed)
    row_max = jnp.max(scores, axis=-1, keepdims=True)
    log_total = row_max + jnp.log(jnp.sum(jnp.exp(scores - row_max), axis=-1, keepdims=True))
    attn_probs = jnp.exp(scores - log_total).astype(jnp.bfloat16)
    mixed_heads = product("shqk,skhd->sqhd", attn_probs, value_rows.reshape(head_shape))
    attended = mixed_heads.reshape(tok_count, HID).astype(jnp.bfloat16)
    hidden_one = residual + matmul(attended, w_bf[3 * HID : 4 * HID]) + floats[4]
    normed_two = affine_norm(hidden_one, floats[5], floats[6]).astype(jnp.bfloat16)
    pre_act = matmul_nt(normed_two, w_bf[4 * HID : 4 * HID + FF]) + floats[7:11].reshape(FF)
    active = gelu_tanh(pre_act).astype(jnp.bfloat16)
    output = (hidden_one + matmul(active, w_bf[4 * HID + FF :]) + floats[11]).astype(jnp.bfloat16)
    kept_state = (
        residual,
        normed_one,
        query_rows,
        key_rows,
        value_rows,
        log_total,
        attended,
        hidden_one,
        normed_two,
        pre_act,
        active,
        floats,
    )
    return (output, kept_state)


def backward(kept_state, cotangent, segments, w_bf):
    (
        residual,
        normed_one,
        query_rows,
        key_rows,
        value_rows,
        log_total,
        attended,
        hidden_one,
        normed_two,
        pre_act,
        active,
        floats,
    ) = kept_state
    seq_count, length = segments.shape
    tok_count = residual.shape[0]
    head_shape = (seq_count, length, HEADS, HEAD)
    grad_out = cotangent.astype(jnp.float32)
    grad_active = matmul_nt(cotangent, w_bf[4 * HID + FF :])
    grad_pre = jax.vjp(gelu_tanh, pre_act)[1](grad_active)[0]
    grad_pre_bf = grad_pre.astype(jnp.bfloat16)
    grad_normed_two = matmul(grad_pre_bf, w_bf[4 * HID : 4 * HID + FF])
    norm_back_two = jax.vjp(affine_norm, hidden_one, floats[5], floats[6])[1]
    grad_h_part, grad_gain_two, grad_shift_two = norm_back_two(grad_normed_two)
    grad_hidden = grad_out + grad_h_part
    grad_hidden_bf = grad_hidden.astype(jnp.bfloat16)
    grad_attended = matmul_nt(grad_hidden_bf, w_bf[3 * HID : 4 * HID]).astype(jnp.bfloat16)
    query_four = query_rows.reshape(head_shape)
    key_four = key_rows.reshape(head_shape)
    value_four = value_rows.reshape(head_shape)
    grad_att_four = grad_attended.reshape(head_shape)
    allowed = allowed_pairs(segments)
    scores = scores_of(query_four, key_four, allowed)
    attn_probs = jnp.exp(scores - log_total)
    probs_bf = attn_probs.astype(jnp.bfloat16)
    grad_probs = product("sqhd,skhd->shqk", grad_att_four, value_four)
    inner_sum = jnp.sum(attn_probs * grad_probs, axis=-1, keepdims=True)
    grad_scores = (attn_probs * (grad_probs - inner_sum) * HEAD ** (-0.5)).astype(jnp.bfloat16)
    grad_query = product("shqk,skhd->sqhd", grad_scores, key_four).reshape(tok_count, HID)
    grad_keys = product("shqk,sqhd->skhd", grad_scores, query_four).reshape(tok_count, HID)
    grad_values = product("shqk,sqhd->skhd", probs_bf, grad_att_four).reshape(tok_count, HID)
    grad_proj = jnp.concatenate([grad_query, grad_keys, grad_values], axis=1)
    grad_proj_bf = grad_proj.astype(jnp.bfloat16)
    grad_normed_one = matmul(grad_proj_bf, w_bf[: 3 * HID])
    norm_back_one = jax.vjp(affine_norm, residual, floats[0], floats[1])[1]
    grad_r_part, grad_gain_one, grad_shift_one = norm_back_one(grad_normed_one)
    grad_tokens = grad_hidden + grad_r_part
    bias_ff = jnp.sum(grad_pre, axis=0).reshape(FF // D, D)
    head_rows = jnp.stack(
        [
            grad_gain_one,
            grad_shift_one,
            jnp.sum(grad_query, axis=0),
            jnp.sum(grad_values, axis=0),
            jnp.sum(grad_hidden, axis=0),
            grad_gain_two,
            grad_shift_two,
        ]
    )
    grad_vec = jnp.concatenate([head_rows, bias_ff, jnp.sum(grad_out, axis=0)[None]], axis=0)
    row_terms = jnp.concatenate([grad_proj_bf, attended, grad_pre_bf, active], axis=1)
    col_terms = jnp.stack([normed_one, grad_hidden_bf, normed_two, cotangent])
    return (grad_tokens, grad_vec, row_terms, col_terms)


def weight_grads(row_terms, col_terms):
    row_bounds = (0, 3 * HID, 4 * HID, 4 * HID + FF, R)
    pieces = [
        matmul_tn(row_terms[:, row_bounds[index] : row_bounds[index + 1]], col_terms[index])
        for index in range(4)
    ]
    return jnp.concatenate(pieces, axis=0)


def adam_update(param, first, second, grad, decay):
    new_first = beta_one * first + (1.0 - beta_one) * grad
    new_second = beta_two * second + (1.0 - beta_two) * grad * grad
    first_hat = new_first / (1.0 - beta_one**STEP)
    second_hat = new_second / (1.0 - beta_two**STEP)
    new_param = param - learn_rate * (first_hat / (jnp.sqrt(second_hat) + adam_eps) + decay * param)
    return (new_param, new_first, new_second)


def bit_reverse(index, bits):
    out = index * 0
    for place in range(bits):
        out = out * 2 + (index >> place) % 2
    return out


class Links:
    def __init__(self, replicas, shards):
        self.replicas = replicas
        self.cores = 2
        self.chips = shards // self.cores
        self.bits = replicas.bit_length() - 1
        self.replica = lax.axis_index("rep")
        shard = lax.axis_index("shard")
        self.chip = shard // self.cores
        self.core = shard % self.cores

    @staticmethod
    def fits(replicas, shards, rows):
        power = replicas > 2 and replicas & (replicas - 1) == 0
        return shards == 8 and power and 2 * rows == 3 * HID

    def send(self, value, target):
        route = []
        for rep in range(self.replicas):
            for chip in range(self.chips):
                for core in range(self.cores):
                    goal = target(rep, chip, core)
                    if goal is None:
                        continue
                    start = (rep * self.chips + chip) * self.cores + core
                    stop = (goal[0] * self.chips + goal[1]) * self.cores + goal[2]
                    route.append((start, stop))
        return lax.ppermute(value, ("rep", "shard"), route)

    def swap_core(self, value):
        return self.send(value, lambda rep, chip, core: (rep, chip, 1 - core))

    def swap_both(self, value, bit):
        return self.send(value, lambda rep, chip, core: (rep ^ (1 << bit), chip, 1 - core))

    def swap_bit(self, value, bit):
        return self.send(value, lambda rep, chip, core: (rep ^ (1 << bit), chip, core))

    def along(self, value, moves):
        table = dict(moves)
        return self.send(
            value, lambda rep, chip, core: (rep, table[chip], core) if chip in table else None
        )

    def bit_of(self, bit):
        return (self.replica >> bit) % 2

    def own_pieces(self, block):
        half = block.shape[0] // 2
        size = half // self.replicas
        first = lax.dynamic_slice_in_dim(block, self.replica * size, size)
        turned = bit_reverse(self.replica, self.bits)
        second = lax.dynamic_slice_in_dim(block, half + turned * size, size)
        return first, second

    def gather_pieces(self, first, second):
        for step in range(self.bits):
            low, high = step, self.bits - 1 - step
            got_first = self.swap_bit(first, low)
            got_second = self.swap_bit(second, high)
            if step == self.bits - 1:
                return [first, got_first, second, got_second]
            first = jnp.where(
                self.bit_of(low) == 0,
                jnp.concatenate([first, got_first]),
                jnp.concatenate([got_first, first]),
            )
            second = jnp.where(
                self.bit_of(high) == 0,
                jnp.concatenate([second, got_second]),
                jnp.concatenate([got_second, second]),
            )

    def gather_positions(self, piece):
        size = piece.shape[0] // 2
        first, second = piece[:size], piece[size:]
        for step in range(self.bits):
            high, low = self.bits - 1 - step, step
            got_first = self.swap_bit(first, high)
            got_second = self.swap_bit(second, low)
            first = jnp.where(
                self.bit_of(high) == 0,
                jnp.concatenate([first, got_first]),
                jnp.concatenate([got_first, first]),
            )
            second = jnp.where(
                self.bit_of(low) == 0,
                jnp.concatenate([second, got_second]),
                jnp.concatenate([got_second, second]),
            )
        parts = []
        for position in range(self.replicas):
            turned = bit_reverse(position, self.bits)
            parts.append(first[position * size : (position + 1) * size])
            parts.append(second[turned * size : (turned + 1) * size])
        return jnp.concatenate(parts)

    def to_chip(self, piece, moves):
        got = self.along(piece, moves)
        return add_bf(piece, got)


def add_bf(left, right):
    return (left.astype(jnp.float32) + right.astype(jnp.float32)).astype(jnp.bfloat16)


vector_pad = 16


def dot(left, right, left_dim, right_dim):
    return lax.dot_general(
        left,
        right,
        (((left_dim,), (right_dim,)), ((), ())),
        preferred_element_type=jnp.float32,
    )


def norm_parts(values):
    centred = values - jnp.mean(values, axis=-1, keepdims=True)
    scale = lax.rsqrt(jnp.mean(centred * centred, axis=-1, keepdims=True) + norm_eps)
    return centred * scale, scale


def norm_back(unit, scale, grad):
    inner = jnp.mean(grad, axis=-1, keepdims=True)
    outer = jnp.mean(grad * unit, axis=-1, keepdims=True)
    return scale * (grad - inner - unit * outer)


def row_sum(values):
    return jnp.sum(values, axis=0, keepdims=True)


def left_lanes(value):
    return lax.broadcasted_iota(jnp.int32, value.shape, 1) < HEAD


def head_parts(pair):
    left = left_lanes(pair)
    none = jnp.zeros_like(pair)
    return jnp.where(left, pair, none), jnp.where(left, none, pair)


def load_blocks(place, blocks, rows, target, sem, first, last):
    quarter = rows // 4
    starts = (
        place[7] * quarter,
        (1 - place[7]) * quarter,
        (2 + place[5]) * quarter,
        (3 - place[5]) * quarter,
    )
    for slot in range(4):
        chip = place[slot]

        @pl.when((chip >= first) & (chip < last))
        def _():
            for side in range(2):
                core = place[4] if side == 0 else 1 - place[4]
                number = (chip - first) * 2 + core
                if slot == 0:
                    parts = [(blocks[side], 0, rows)]
                else:
                    at = 2 + (slot - 1) * 8 + side
                    parts = [
                        (blocks[at + 2 * index], starts[index], quarter) for index in range(4)
                    ]
                for ref, shift, size in parts:
                    start = pl.multiple_of(number * rows + shift, 16)
                    pltpu.make_async_copy(ref, target.at[pl.ds(start, size)], sem.at[number]).start()

    done = set()

    def ready(low, high):
        for number in range(low // rows, -(-high // rows)):
            if number in done:
                continue
            done.add(number)
            index = number - 2 * first
            pltpu.make_async_copy(
                blocks[0], target.at[pl.ds(index * rows, rows)], sem.at[index]
            ).wait()

    return ready


block_count = 26


def spread_terms(place, terms, rows, first, outs, wide, lane=0):
    core, across = place[4], place[5]
    count = terms.shape[0]
    for index, out in enumerate(outs):
        block = core if index % 2 == 0 else 1 - core
        side = across if index < 2 else 1 - across
        start = pl.multiple_of(first + block * rows + side * (rows - wide), 128)
        out[:count, lane : lane + wide] = terms[:, pl.ds(start, wide)]


def query_kernel(rows, place, tok, seg_col, seg_row, vec_all, *rest):
    blocks = rest[:block_count]
    n_out, qkv, probs, att, w_in, load_sem = rest[block_count:]
    ready = load_blocks(place, blocks, rows, w_in, load_sem, 0, 1)
    unit, _ = norm_parts(tok[...].astype(jnp.float32))
    n_one = (unit * vec_all[0:1, :] + vec_all[1:2, :]).astype(jnp.bfloat16)
    n_out[...] = n_one
    for index, bias in enumerate((vec_all[2:3, :], None, vec_all[3:4, :])):
        ready(index * HID, (index + 1) * HID)
        value = dot(n_one, w_in[index * HID : (index + 1) * HID], 1, 1)
        if bias is not None:
            value = value + bias
        qkv[:, index * HID : (index + 1) * HID] = value.astype(jnp.bfloat16)
    length = seg_row.shape[1]
    for seq in range(seg_row.shape[0]):
        span = slice(seq * length, (seq + 1) * length)
        order = lax.broadcasted_iota(jnp.int32, (length, length), 0)
        other = lax.broadcasted_iota(jnp.int32, (length, length), 1)
        allowed = (other <= order) & (seg_col[span, :] == seg_row[seq : seq + 1, :])
        for pair in range(HEADS // 2):
            lanes = slice(pair * 2 * HEAD, (pair + 1) * 2 * HEAD)
            key_pair = qkv[span, HID + lanes.start : HID + lanes.stop]
            value_pair = qkv[span, 2 * HID + lanes.start : 2 * HID + lanes.stop]
            mixed = []
            for half, query in enumerate(head_parts(qkv[span, lanes])):
                raw = dot(query, key_pair, 1, 1) * HEAD ** (-0.5)
                raw = jnp.where(allowed, raw, masked_score)
                top = jnp.max(raw, axis=-1, keepdims=True)
                power = jnp.exp(raw - top)
                prob = power * (1.0 / jnp.sum(power, axis=-1, keepdims=True))
                probs[seq * HEADS + 2 * pair + half] = prob
                mixed.append(dot(prob.astype(jnp.bfloat16), value_pair, 1, 0))
            att[span, lanes] = jnp.where(left_lanes(mixed[0]), mixed[0], mixed[1]).astype(
                jnp.bfloat16
            )


def active_kernel(rows, place, tok, att, vec_all, *rest):
    blocks = rest[:block_count]
    n_out, hidden, act, slope_out = rest[block_count : block_count + 4]
    windows = rest[block_count + 4 : block_count + 8]
    w_mid, load_sem = rest[block_count + 8 :]
    ready = load_blocks(place, blocks, rows, w_mid, load_sem, 1, 3)
    base = 2 * rows

    def weight(first, size):
        ready(first, first + size)
        return w_mid[first - base : first - base + size]

    h_value = tok[...].astype(jnp.float32) + dot(att[...], weight(3 * HID, HID), 1, 0)
    h_value = h_value + vec_all[4:5, :]
    hidden[...] = h_value
    unit, _ = norm_parts(h_value)
    n_two = (unit * vec_all[5:6, :] + vec_all[6:7, :]).astype(jnp.bfloat16)
    n_out[...] = n_two
    root = math.sqrt(2.0 / math.pi)
    for index in range(FF // D):
        span = slice(index * D, (index + 1) * D)
        pre = dot(n_two, weight(4 * HID + index * D, D), 1, 1) + vec_all[7 + index : 8 + index, :]
        squared = pre * pre
        bent = jnp.tanh(root * (pre + 0.044715 * (pre * squared)))
        half = 0.5 * (1.0 + bent)
        act[:, span] = (pre * half).astype(jnp.bfloat16)
        slope_out[:, span] = half + 0.5 * pre * (1.0 - bent * bent) * (
            root * (1.0 + 3 * 0.044715 * squared)
        )
    wide = windows[0].shape[1]
    spread_terms(place, act, rows, 6 * rows - (4 * HID + FF), windows, wide)
    windows[1][:, wide:] = n_two
    windows[2][:, wide:] = n_two
    ready(2 * rows, 6 * rows)


def change_kernel(rows, place, cot, att, act, slope, hidden, vec_all, *rest):
    blocks = rest[:block_count]
    rest = rest[block_count:]
    out, dub, vec_out = rest[:3]
    windows = rest[3:7]
    w_top, terms, load_sem = rest[7:]
    ready = load_blocks(place, blocks, rows, w_top, load_sem, 2, 4)
    base = 4 * rows
    terms[:, :HID] = att[...]
    result = hidden[...] + vec_all[11:12, :]
    for index in range(FF // D):
        span = slice(index * D, (index + 1) * D)
        first = 4 * HID + FF + index * D - base
        ready(first + base, first + base + D)
        weight = w_top[first : first + D]
        active = act[:, span]
        change = dot(cot[...], weight, 1, 1) * slope[:, span]
        change_bf = change.astype(jnp.bfloat16)
        dub[:, span] = change_bf
        terms[:, HID + index * D : HID + (index + 1) * D] = change_bf
        terms[:, HID + FF + index * D : HID + FF + (index + 1) * D] = active
        vec_out[index : index + 1, :] = row_sum(change)
        result = result + dot(active, weight, 1, 0)
    wide = windows[0].shape[1] // 2
    spread_terms(place, terms, rows, 2 * rows, windows, wide)
    spread_terms(place, terms, rows, 0, windows, wide, wide)
    out[...] = result.astype(jnp.bfloat16)
    vec_out[4:5, :] = row_sum(cot[...].astype(jnp.float32))
    vec_out[5:8, :] = jnp.zeros((3, D), jnp.float32)
    ready(4 * rows, 8 * rows)


def hidden_kernel(rows, place, dub, hidden, cot, vec_all, *rest):
    blocks = rest[:block_count]
    dh, dh_bf, da, vec_out, w_mid, load_sem = rest[block_count:]
    ready = load_blocks(place, blocks, rows, w_mid, load_sem, 1, 3)
    base = 2 * rows
    unit, scale = norm_parts(hidden[...])
    start = 4 * HID
    back = None
    while start < 4 * HID + FF:
        stop = min((start // rows + 1) * rows, 4 * HID + FF)
        ready(start, stop)
        part = dot(dub[:, start - 4 * HID : stop - 4 * HID], w_mid[start - base : stop - base], 1, 0)
        back = part if back is None else back + part
        start = stop
    vec_out[0:1, :] = row_sum(back * unit)
    vec_out[1:2, :] = row_sum(back)
    value = cot[...].astype(jnp.float32) + norm_back(unit, scale, back * vec_all[5:6, :])
    dh[...] = value
    vec_out[2:3, :] = row_sum(value)
    vec_out[3:8, :] = jnp.zeros((5, D), jnp.float32)
    rounded = value.astype(jnp.bfloat16)
    dh_bf[...] = rounded
    da[...] = dot(rounded, w_mid[3 * HID - base : 4 * HID - base], 1, 1).astype(jnp.bfloat16)


def attention_kernel(rows, place, da, qkv, probs, dh, tok, vec_all, vec_first, vec_second, *rest):
    blocks = rest[:block_count]
    rest = rest[block_count:]
    grad_tok = rest[0]
    windows = rest[1:5]
    w_in, dqkv, vec_out, packed, load_sem = rest[5:]
    ready = load_blocks(place, blocks, rows, w_in, load_sem, 0, 1)
    heads_total = probs.shape[0]
    length = probs.shape[1]
    vec_out[2:4, :] = jnp.zeros((2, D), jnp.float32)
    for seq in range(heads_total // HEADS):
        span = slice(seq * length, (seq + 1) * length)
        for pair in range(HEADS // 2):
            lanes = slice(pair * 2 * HEAD, (pair + 1) * 2 * HEAD)
            query_pair = qkv[span, lanes]
            key_pair = qkv[span, HID + lanes.start : HID + lanes.stop]
            value_pair = qkv[span, 2 * HID + lanes.start : 2 * HID + lanes.stop]
            da_pair = da[span, lanes]
            got = []
            for half, da_head in enumerate(head_parts(da_pair)):
                prob = probs[seq * HEADS + 2 * pair + half]
                grad_prob = dot(da_head, value_pair, 1, 1)
                inner = jnp.sum(prob * grad_prob, axis=-1, keepdims=True)
                grad_score = (prob * (grad_prob - inner) * HEAD ** (-0.5)).astype(jnp.bfloat16)
                got.append(
                    (
                        dot(grad_score, key_pair, 1, 0),
                        dot(grad_score, query_pair, 0, 0),
                        dot(prob.astype(jnp.bfloat16), da_pair, 0, 0),
                    )
                )
            left = left_lanes(got[0][0])
            query_grad, key_grad, value_grad = [
                jnp.where(left, one, two) for one, two in zip(got[0], got[1])
            ]
            dqkv[span, lanes] = query_grad.astype(jnp.bfloat16)
            dqkv[span, HID + lanes.start : HID + lanes.stop] = key_grad.astype(jnp.bfloat16)
            dqkv[span, 2 * HID + lanes.start : 2 * HID + lanes.stop] = value_grad.astype(
                jnp.bfloat16
            )
            vec_out[2:3, lanes] = vec_out[2:3, lanes] + row_sum(query_grad)
            vec_out[3:4, lanes] = vec_out[3:4, lanes] + row_sum(value_grad)
    unit, scale = norm_parts(tok[...].astype(jnp.float32))
    ready(0, 2 * rows)
    back = dot(dqkv[...], w_in[...], 1, 0)
    grad_tok[...] = dh[...] + norm_back(unit, scale, back * vec_all[0:1, :])
    vec_out[0:1, :] = row_sum(back * unit)
    vec_out[1:2, :] = row_sum(back)
    vec_out[4:5, :] = vec_second[2:3, :]
    vec_out[5:7, :] = vec_second[0:2, :]
    vec_out[7:12, :] = vec_first[0:5, :]
    wide = windows[0].shape[1]
    spread_terms(place, dqkv, rows, 0, windows, wide)
    packed[...] = jnp.zeros_like(packed)
    for at, lanes, row, source in vector_tiles(wide):
        packed[at : at + 1, lanes] = vec_out[row : row + 1, source]
    for window in windows:
        window[dqkv.shape[0] :, :] = packed[...].astype(jnp.bfloat16)


def vector_tiles(wide):
    across, packed = D // 128, wide // 128
    for index in range(12 * across):
        at, to = divmod(index, packed)
        row, source = divmod(index, across)
        yield at, slice(to * 128, to * 128 + 128), row, slice(source * 128, source * 128 + 128)


def product_kernel(rows, wide, lane, starts, split, which, place, *rest):
    last = split is None and starts is None
    terms, columns, rest = rest[:4], rest[4:-6], rest[-6:]
    away, mine, left, right, whole, sums = rest
    if last:
        vec_all, columns = columns[0], columns[1:]
    count = columns[0].shape[0]
    for index in range(4):
        left[index * count : (index + 1) * count] = terms[index][:count, lane : lane + wide]
    core, across, high = place[4], place[5], place[6]

    def column(index):
        value = columns[index]
        if last and index > 0:
            unit, _ = norm_parts(value[:, :D].astype(jnp.float32))
            return (unit * vec_all[0:1, :] + vec_all[1:2, :]).astype(jnp.bfloat16)
        start = 0 if last else starts[index]
        return value[:, start : start + D]

    def put(span, other):
        for index in range(4):
            value = column(index)
            if other is not None:
                value = jnp.where(other, column(4 + index), value)
            right[index * count : (index + 1) * count] = value
        whole[span, :] = dot(left[:, span], right[...], 0, 0).astype(jnp.bfloat16)

    if split is None:
        put(slice(0, wide), None)
    else:
        start = rows - wide
        chosen = core == which
        if split <= start:
            put(slice(0, split), chosen & (across == 1))
            put(slice(split, wide), chosen)
        else:
            put(slice(0, split - start), chosen)
            put(slice(split - start, wide), chosen & (across == 0))
    part = rows // 4
    first = across * (wide - rows // 2)
    away[:part] = whole[pl.ds(pl.multiple_of(first + (1 - high) * part, 16), part), :]
    mine[:part] = whole[pl.ds(pl.multiple_of(first + high * part, 16), part), :]
    if last:
        total = terms[0][count:, :].astype(jnp.float32)
        for index in range(1, 4):
            total = total + terms[index][count:, :].astype(jnp.float32)
        sums[...] = jnp.zeros_like(sums)
        for at, lanes, row, source in vector_tiles(wide):
            sums[row : row + 1, source] = total[at : at + 1, lanes]
        away[part:] = sums[...].astype(jnp.bfloat16)
        mine[part:] = sums[...].astype(jnp.bfloat16)


any_spec = pl.BlockSpec(memory_space=pl.ANY)
vmem_spec = pl.BlockSpec(memory_space=pltpu.VMEM)
smem_spec = pl.BlockSpec(memory_space=pltpu.SMEM)
bf16, f32 = jnp.bfloat16, jnp.float32


def grant(inputs, outputs, scratch):
    arrays = [value for value, spec in inputs if spec is vmem_spec]
    arrays += [jax.ShapeDtypeStruct(shape, kind) for shape, kind, spec in outputs]
    need = 2 * sum(value.size * value.dtype.itemsize for value in arrays)
    for item in scratch:
        if hasattr(item, "shape") and item.dtype in (bf16, f32):
            need += math.prod(item.shape) * jnp.dtype(item.dtype).itemsize
    return need + 6 * 1024 * 1024


def call(kernel, inputs, outputs, scratch, flops, moved):
    return pl.pallas_call(
        kernel,
        grid=(1,),
        in_specs=[spec for _, spec in inputs],
        out_specs=[spec for _, _, spec in outputs],
        out_shape=[jax.ShapeDtypeStruct(shape, kind) for shape, kind, _ in outputs],
        scratch_shapes=scratch,
        compiler_params=pltpu.CompilerParams(vmem_limit_bytes=grant(inputs, outputs, scratch)),
        cost_estimate=pl.CostEstimate(flops=flops, bytes_accessed=moved, transcendentals=0),
    )(*[value for value, _ in inputs])


def after(kernel, inputs, waits):
    count, extra = len(inputs), len(waits)

    def body(*refs):
        kernel(*refs[:count], *refs[count + extra :])

    return body, inputs + [(value, any_spec) for value in waits]


def parameter_blocks(links, weights, vectors):
    shards = links.chips * links.cores
    width = vectors.shape[1]
    number = links.chip * links.cores + links.core
    location = lax.broadcasted_iota(jnp.int32, (vectors.shape[0], width * shards), 1) // width
    spread = jnp.where(location == number, jnp.tile(vectors, (1, shards)), 0.0)
    spread = jnp.pad(spread, ((0, vector_pad - vectors.shape[0]), (0, 0))).astype(bf16)
    first, second = links.own_pieces(weights)
    size = first.shape[0]
    mine = jnp.concatenate([first.astype(bf16), second.astype(bf16), spread])
    inner = (links.chip == 1) | (links.chip == 2)
    near = links.along(mine, {0: 1, 1: 0, 2: 3, 3: 2})
    middle = links.along(mine, {1: 2, 2: 1})
    across = links.along(near, {1: 2, 2: 1})
    outward = links.along(middle, {1: 0, 2: 3})
    far = links.along(across, {1: 0, 2: 3})
    block = weights.astype(bf16)
    blocks = [block, links.swap_core(block)]
    slots = (near, jnp.where(inner, middle, outward), jnp.where(inner, across, far))
    total = spread
    for slot in slots:
        total = total + slot[2 * size :]
        for piece in links.gather_pieces(slot[:size], slot[size : 2 * size]):
            blocks += [piece, links.swap_core(piece)]
    total = total + links.swap_core(total)
    return blocks, total.astype(f32)


def direct_step(links, tokens, segments, cotangent, state, vectors):
    count = tokens.shape[0]
    weights = state[0]
    rows = weights.shape[0]
    wide = -(-rows // 256) * 128
    blocks, vec_all = parameter_blocks(links, weights, vectors)
    low = links.chip < links.chips // 2
    place = jnp.stack(
        [
            links.chip,
            links.chip ^ 1,
            jnp.where(low, 2, 1),
            jnp.where(low, 3, 0),
            links.core,
            links.bit_of(0),
            links.bit_of(1),
            links.bit_of(links.bits - 1),
        ]
    ).astype(jnp.int32)
    ends = [(place, smem_spec)]
    pairs = segments.shape[0] * HEADS
    length = segments.shape[1]
    unit_cost = 2 * count * HID * D
    parameters = [(block, any_spec) for block in blocks]

    def full(*arrays):
        return [(array, vmem_spec) for array in arrays]

    def shape(width, kind=bf16, height=count):
        return (height, width), kind, vmem_spec

    def weight_scratch(chips):
        return [pltpu.VMEM((chips * 2 * rows, D), bf16)]

    def weight_sem(chips):
        return [pltpu.SemaphoreType.DMA((chips * 2,))]

    def share_rows(parts):
        own, to_core, to_side, to_both = parts
        side = links.swap_bit(to_side, 0)
        both = links.swap_both(to_both, 0)
        other = links.swap_core(to_core)
        return [own, other, side, both]

    joined = jnp.concatenate([tokens, cotangent], axis=1)
    joined_side = links.swap_bit(joined, 0)
    joined_core = links.swap_core(joined)
    joined_both = links.swap_core(joined_side)
    joined_all = [joined, joined_core, joined_side, joined_both]
    n_one, qkv, probs, att = call(
        functools.partial(query_kernel, rows),
        ends + full(tokens, segments.reshape(count, 1), segments, vec_all) + parameters,
        [
            shape(D),
            shape(3 * HID),
            ((pairs, length, length), f32, vmem_spec),
            shape(HID),
        ],
        weight_scratch(1) + weight_sem(1),
        4 * unit_cost,
        6 * HID * D,
    )
    active_out = call(
        functools.partial(active_kernel, rows),
        ends + full(tokens, att, vec_all) + parameters,
        [shape(D), shape(D, f32), shape(FF), shape(FF, f32)]
        + [shape(wide), shape(wide + D), shape(wide + D), shape(wide)],
        weight_scratch(2) + weight_sem(2),
        5 * unit_cost,
        8 * rows * D,
    )
    n_two, hidden, act, slope = active_out[:4]
    rows_three = share_rows(active_out[4:])
    n_two_both = links.swap_core(rows_three[2])
    n_two_all = [n_two, rows_three[1], rows_three[2], n_two_both]
    n_two_starts = [0, wide, wide, wide]
    change_out = call(
        functools.partial(change_kernel, rows),
        ends + full(cotangent, att, act, slope, hidden, vec_all) + parameters,
        [shape(D), shape(FF), shape(D, f32, 8)] + [shape(2 * wide)] * 4,
        weight_scratch(2) + [pltpu.VMEM((count, HID + 2 * FF), bf16)] + weight_sem(2),
        8 * unit_cost,
        8 * rows * D,
    )
    out, dub, vec_first = change_out[:3]
    rows_middle = share_rows(change_out[3:])

    def product(parts, columns, lane, starts, split=None, which=0, waits=()):
        extra = 0 if starts is not None else vector_pad
        kernel, inputs = after(
            functools.partial(product_kernel, rows, wide, lane, starts, split, which),
            ends + full(*parts) + full(*columns),
            list(waits),
        )
        return call(
            kernel,
            inputs,
            [shape(D, bf16, rows // 4 + extra)] * 2,
            [
                pltpu.VMEM((4 * count, wide), bf16),
                pltpu.VMEM((4 * count, D), bf16),
                pltpu.VMEM((wide, D), bf16),
                pltpu.VMEM((vector_pad, D), f32),
            ],
            8 * count * wide * D,
            4 * rows * D,
        )

    def scatter_rest(parts):
        away, mine = parts
        got = links.swap_bit(away, 1)
        mine = add_bf(mine, got)
        part = rows // 4
        mine, rest = mine[:part], mine[part:]
        for bit in range(2, links.bits):
            size = mine.shape[0] // 2
            away = lax.dynamic_slice_in_dim(mine, (1 - links.bit_of(bit)) * size, size)
            near = lax.dynamic_slice_in_dim(mine, links.bit_of(bit) * size, size)
            mine = add_bf(near, links.swap_bit(away, bit))
            if rest.shape[0]:
                rest = add_bf(rest, links.swap_bit(rest, bit))
        return jnp.concatenate([mine, rest]) if rest.shape[0] else mine

    product_three = product(rows_three, joined_all, 0, [D] * 4)
    three = scatter_rest(product_three)
    kernel, inputs = after(
        functools.partial(hidden_kernel, rows),
        ends + full(dub, hidden, cotangent, vec_all) + parameters,
        product_three[:1],
    )
    dh, dh_bf, da, vec_second = call(
        kernel,
        inputs,
        [shape(D, f32), shape(D), shape(HID), shape(D, f32, 8)],
        weight_scratch(2) + weight_sem(2),
        5 * unit_cost,
        8 * rows * D,
    )
    dh_side = links.swap_bit(dh_bf, 0)
    dh_core = links.swap_core(dh_bf)
    dh_both = links.swap_core(dh_side)
    dh_all = [dh_bf, dh_core, dh_side, dh_both]
    product_two = product(
        rows_middle,
        n_two_all + joined_all,
        0,
        n_two_starts + [D] * 4,
        4 * HID + FF - 5 * rows,
        1,
        waits=[vec_second],
    )
    two = scatter_rest(product_two)
    product_one = product(
        rows_middle,
        n_two_all + dh_all,
        wide,
        n_two_starts + [0] * 4,
        4 * HID - 2 * rows,
        0,
        waits=product_two[:1],
    )
    one = scatter_rest(product_one)
    kernel, inputs = after(
        functools.partial(attention_kernel, rows),
        ends + full(da, qkv, probs, dh, tokens, vec_all, vec_first, vec_second) + parameters,
        product_one[:1],
    )
    attention_out = call(
        kernel,
        inputs,
        [shape(D, f32)] + [shape(wide, bf16, count + vector_pad)] * 4,
        weight_scratch(1)
        + [
            pltpu.VMEM((count, 3 * HID), bf16),
            pltpu.VMEM((vector_pad, D), f32),
            pltpu.VMEM((vector_pad, wide), f32),
        ]
        + weight_sem(1),
        4 * unit_cost,
        4 * rows * D,
    )
    grad_tok = attention_out[0]
    rows_zero = share_rows(attention_out[1:])
    product_zero = product(rows_zero, [vec_all, n_one] + joined_all[1:], 0, None)
    zero = scatter_rest(product_zero)
    three = links.to_chip(three, {0: 1, 2: 3})
    two, grad_tok = lax.optimization_barrier((two, grad_tok))
    two = links.to_chip(two, {0: 1, 3: 2})
    three = links.to_chip(three, {1: 3})
    two = links.to_chip(two, {1: 2})
    one = links.to_chip(one, {0: 1, 3: 2})
    one = links.to_chip(one, {2: 1})
    zero = links.to_chip(zero, {0: 1, 1: 0, 2: 3, 3: 2})
    mine = jnp.where(links.chip == 1, one, jnp.where(links.chip == 2, two, three))
    zero, mine = lax.optimization_barrier((zero, mine))
    zero = links.to_chip(zero, {0: 2, 2: 0})
    size = mine.shape[0]
    mine = jnp.where(links.chip == 0, zero[:size], mine)
    grad_w = links.gather_positions(mine).astype(f32)
    sums = zero[size:]
    got = links.along(sums, {0: 1, 2: 3})
    sums = jnp.where(links.chip % 2 == 0, sums, got).astype(f32)
    width = vectors.shape[1]
    grad_v = lax.dynamic_slice_in_dim(sums, lax.axis_index("shard") * width, width, 1)
    new = [grad_w] + list(adam_update(*state, grad_w, decay_rate))
    return out, grad_tok, grad_v[: vectors.shape[0]], new


def per_device(
    replicas,
    shards,
    tokens,
    segments,
    cotangent,
    weights,
    vectors,
    first_weights,
    first_vectors,
    second_weights,
    second_vectors,
):
    if Links.fits(replicas, shards, weights.shape[0]):
        output, grad_tokens, grad_v, new = direct_step(
            Links(replicas, shards),
            tokens,
            segments,
            cotangent,
            (weights, first_weights, second_weights),
            vectors,
        )
    else:
        w_full = lax.all_gather(weights.astype(jnp.bfloat16), "shard", axis=0, tiled=True)
        v_full = lax.all_gather(vectors.astype(jnp.bfloat16), "shard", axis=1, tiled=True)
        output, kept_state = forward(tokens, segments, w_full, v_full)
        grad_tokens, grad_vec, row_terms, col_terms = backward(
            kept_state, cotangent, segments, w_full
        )
        local_grad = weight_grads(row_terms, col_terms).astype(jnp.bfloat16)
        own_w = lax.psum_scatter(local_grad, "shard", scatter_dimension=0, tiled=True)
        own_v = lax.psum_scatter(
            grad_vec.astype(jnp.bfloat16), "shard", scatter_dimension=1, tiled=True
        )
        grad_w = lax.psum(own_w, "rep").astype(jnp.float32)
        grad_v = lax.psum(own_v, "rep").astype(jnp.float32)
        new = [grad_w]
        new += adam_update(weights, first_weights, second_weights, grad_w, decay_rate)
    grad_w, new_w, new_fw, new_sw = new
    new_v, new_fv, new_sv = adam_update(vectors, first_vectors, second_vectors, grad_v, 0.0)
    return (output, grad_tokens, grad_w, grad_v, new_w, new_v, new_fw, new_fv, new_sw, new_sv)


def solution(mesh):
    placed = (
        P(("rep", "shard"), None),
        P(("rep", "shard"), None),
        P(("rep", "shard"), None),
        P("shard", None),
        P(None, "shard"),
        P("shard", None),
        P(None, "shard"),
        P("shard", None),
        P(None, "shard"),
    )
    return jax.shard_map(
        functools.partial(per_device, mesh.shape["rep"], mesh.shape["shard"]),
        mesh=mesh,
        in_specs=placed,
        out_specs=(
            P(("rep", "shard"), None),
            P(("rep", "shard"), None),
            P("shard", None),
            P(None, "shard"),
            P("shard", None),
            P(None, "shard"),
            P("shard", None),
            P(None, "shard"),
            P("shard", None),
            P(None, "shard"),
        ),
        check_vma=False,
    )
```

```python
import functools
import math

import jax
import jax.numpy as jnp
from jax import lax
from jax.experimental import pallas as pl
from jax.experimental.pallas import tpu as pltpu
from jax.sharding import PartitionSpec as P

D = 768
HEADS = 12
HEAD = 64
FF = 3072
STEP = 3
HID = 768
R = 9216


norm_eps = 1e-05
beta_one = 0.9
beta_two = 0.999
adam_eps = 1e-08
learn_rate = 0.2
decay_rate = 0.1
masked_score = -1e30


def normalize(values):
    centred = values - jnp.mean(values, axis=-1, keepdims=True)
    return centred * lax.rsqrt(jnp.mean(centred * centred, axis=-1, keepdims=True) + norm_eps)


def affine_norm(values, gain_vec, shift_vec):
    return normalize(values) * gain_vec + shift_vec


def gelu_tanh(values):
    return jax.nn.gelu(values, approximate=True)


def matmul(left_op, right_op):
    return jnp.dot(left_op, right_op, preferred_element_type=jnp.float32)


def matmul_nt(left_op, right_op):
    return lax.dot_general(
        left_op, right_op, (((1,), (1,)), ((), ())), preferred_element_type=jnp.float32
    )


def matmul_tn(left_op, right_op):
    return lax.dot_general(
        left_op, right_op, (((0,), (0,)), ((), ())), preferred_element_type=jnp.float32
    )


def product(pattern, left_op, right_op):
    return jnp.einsum(pattern, left_op, right_op, preferred_element_type=jnp.float32)


def allowed_pairs(segments):
    length = segments.shape[1]
    places = lax.broadcasted_iota(jnp.int32, (length, length), 0)
    others = lax.broadcasted_iota(jnp.int32, (length, length), 1)
    causal = others <= places
    same_doc = segments[:, :, None] == segments[:, None, :]
    return (causal[None] & same_doc)[:, None]


def scores_of(query_rows, key_rows, allowed):
    raw_scores = product("sqhd,skhd->shqk", query_rows, key_rows) * HEAD ** (-0.5)
    return jnp.where(allowed, raw_scores, masked_score)


def forward(tokens, segments, w_bf, v_bf):
    seq_count, length = segments.shape
    tok_count = tokens.shape[0]
    head_shape = (seq_count, length, HEADS, HEAD)
    floats = v_bf.astype(jnp.float32)
    residual = tokens.astype(jnp.float32)
    normed_one = affine_norm(residual, floats[0], floats[1]).astype(jnp.bfloat16)
    projected = matmul_nt(normed_one, w_bf[: 3 * HID])
    query_rows = (projected[:, :HID] + floats[2]).astype(jnp.bfloat16)
    key_rows = projected[:, HID : 2 * HID].astype(jnp.bfloat16)
    value_rows = (projected[:, 2 * HID :] + floats[3]).astype(jnp.bfloat16)
    allowed = allowed_pairs(segments)
    scores = scores_of(query_rows.reshape(head_shape), key_rows.reshape(head_shape), allowed)
    row_max = jnp.max(scores, axis=-1, keepdims=True)
    log_total = row_max + jnp.log(jnp.sum(jnp.exp(scores - row_max), axis=-1, keepdims=True))
    attn_probs = jnp.exp(scores - log_total).astype(jnp.bfloat16)
    mixed_heads = product("shqk,skhd->sqhd", attn_probs, value_rows.reshape(head_shape))
    attended = mixed_heads.reshape(tok_count, HID).astype(jnp.bfloat16)
    hidden_one = residual + matmul(attended, w_bf[3 * HID : 4 * HID]) + floats[4]
    normed_two = affine_norm(hidden_one, floats[5], floats[6]).astype(jnp.bfloat16)
    pre_act = matmul_nt(normed_two, w_bf[4 * HID : 4 * HID + FF]) + floats[7:11].reshape(FF)
    active = gelu_tanh(pre_act).astype(jnp.bfloat16)
    output = (hidden_one + matmul(active, w_bf[4 * HID + FF :]) + floats[11]).astype(jnp.bfloat16)
    kept_state = (
        residual,
        normed_one,
        query_rows,
        key_rows,
        value_rows,
        log_total,
        attended,
        hidden_one,
        normed_two,
        pre_act,
        active,
        floats,
    )
    return (output, kept_state)


def backward(kept_state, cotangent, segments, w_bf):
    (
        residual,
        normed_one,
        query_rows,
        key_rows,
        value_rows,
        log_total,
        attended,
        hidden_one,
        normed_two,
        pre_act,
        active,
        floats,
    ) = kept_state
    seq_count, length = segments.shape
    tok_count = residual.shape[0]
    head_shape = (seq_count, length, HEADS, HEAD)
    grad_out = cotangent.astype(jnp.float32)
    grad_active = matmul_nt(cotangent, w_bf[4 * HID + FF :])
    grad_pre = jax.vjp(gelu_tanh, pre_act)[1](grad_active)[0]
    grad_pre_bf = grad_pre.astype(jnp.bfloat16)
    grad_normed_two = matmul(grad_pre_bf, w_bf[4 * HID : 4 * HID + FF])
    norm_back_two = jax.vjp(affine_norm, hidden_one, floats[5], floats[6])[1]
    grad_h_part, grad_gain_two, grad_shift_two = norm_back_two(grad_normed_two)
    grad_hidden = grad_out + grad_h_part
    grad_hidden_bf = grad_hidden.astype(jnp.bfloat16)
    grad_attended = matmul_nt(grad_hidden_bf, w_bf[3 * HID : 4 * HID]).astype(jnp.bfloat16)
    query_four = query_rows.reshape(head_shape)
    key_four = key_rows.reshape(head_shape)
    value_four = value_rows.reshape(head_shape)
    grad_att_four = grad_attended.reshape(head_shape)
    allowed = allowed_pairs(segments)
    scores = scores_of(query_four, key_four, allowed)
    attn_probs = jnp.exp(scores - log_total)
    probs_bf = attn_probs.astype(jnp.bfloat16)
    grad_probs = product("sqhd,skhd->shqk", grad_att_four, value_four)
    inner_sum = jnp.sum(attn_probs * grad_probs, axis=-1, keepdims=True)
    grad_scores = (attn_probs * (grad_probs - inner_sum) * HEAD ** (-0.5)).astype(jnp.bfloat16)
    grad_query = product("shqk,skhd->sqhd", grad_scores, key_four).reshape(tok_count, HID)
    grad_keys = product("shqk,sqhd->skhd", grad_scores, query_four).reshape(tok_count, HID)
    grad_values = product("shqk,sqhd->skhd", probs_bf, grad_att_four).reshape(tok_count, HID)
    grad_proj = jnp.concatenate([grad_query, grad_keys, grad_values], axis=1)
    grad_proj_bf = grad_proj.astype(jnp.bfloat16)
    grad_normed_one = matmul(grad_proj_bf, w_bf[: 3 * HID])
    norm_back_one = jax.vjp(affine_norm, residual, floats[0], floats[1])[1]
    grad_r_part, grad_gain_one, grad_shift_one = norm_back_one(grad_normed_one)
    grad_tokens = grad_hidden + grad_r_part
    bias_ff = jnp.sum(grad_pre, axis=0).reshape(FF // D, D)
    head_rows = jnp.stack(
        [
            grad_gain_one,
            grad_shift_one,
            jnp.sum(grad_query, axis=0),
            jnp.sum(grad_values, axis=0),
            jnp.sum(grad_hidden, axis=0),
            grad_gain_two,
            grad_shift_two,
        ]
    )
    grad_vec = jnp.concatenate([head_rows, bias_ff, jnp.sum(grad_out, axis=0)[None]], axis=0)
    row_terms = jnp.concatenate([grad_proj_bf, attended, grad_pre_bf, active], axis=1)
    col_terms = jnp.stack([normed_one, grad_hidden_bf, normed_two, cotangent])
    return (grad_tokens, grad_vec, row_terms, col_terms)


def weight_grads(row_terms, col_terms):
    row_bounds = (0, 3 * HID, 4 * HID, 4 * HID + FF, R)
    pieces = [
        matmul_tn(row_terms[:, row_bounds[index] : row_bounds[index + 1]], col_terms[index])
        for index in range(4)
    ]
    return jnp.concatenate(pieces, axis=0)


def adam_update(param, first, second, grad, decay):
    new_first = beta_one * first + (1.0 - beta_one) * grad
    new_second = beta_two * second + (1.0 - beta_two) * grad * grad
    first_hat = new_first / (1.0 - beta_one**STEP)
    second_hat = new_second / (1.0 - beta_two**STEP)
    new_param = param - learn_rate * (first_hat / (jnp.sqrt(second_hat) + adam_eps) + decay * param)
    return (new_param, new_first, new_second)


def bit_reverse(index, bits):
    out = index * 0
    for place in range(bits):
        out = out * 2 + (index >> place) % 2
    return out


class Links:
    def __init__(self, replicas, shards):
        self.replicas = replicas
        self.cores = 2
        self.chips = shards // self.cores
        self.bits = replicas.bit_length() - 1
        self.replica = lax.axis_index("rep")
        shard = lax.axis_index("shard")
        self.chip = shard // self.cores
        self.core = shard % self.cores

    @staticmethod
    def fits(replicas, shards, rows):
        power = replicas > 2 and replicas & (replicas - 1) == 0
        return shards == 8 and power and 2 * rows == 3 * HID

    def send(self, value, target):
        route = []
        for rep in range(self.replicas):
            for chip in range(self.chips):
                for core in range(self.cores):
                    goal = target(rep, chip, core)
                    if goal is None:
                        continue
                    start = (rep * self.chips + chip) * self.cores + core
                    stop = (goal[0] * self.chips + goal[1]) * self.cores + goal[2]
                    route.append((start, stop))
        return lax.ppermute(value, ("rep", "shard"), route)

    def swap_core(self, value):
        return self.send(value, lambda rep, chip, core: (rep, chip, 1 - core))

    def swap_both(self, value, bit):
        return self.send(value, lambda rep, chip, core: (rep ^ (1 << bit), chip, 1 - core))

    def swap_bit(self, value, bit):
        return self.send(value, lambda rep, chip, core: (rep ^ (1 << bit), chip, core))

    def along(self, value, moves):
        table = dict(moves)
        return self.send(
            value, lambda rep, chip, core: (rep, table[chip], core) if chip in table else None
        )

    def bit_of(self, bit):
        return (self.replica >> bit) % 2

    def own_pieces(self, block):
        half = block.shape[0] // 2
        size = half // self.replicas
        first = lax.dynamic_slice_in_dim(block, self.replica * size, size)
        turned = bit_reverse(self.replica, self.bits)
        second = lax.dynamic_slice_in_dim(block, half + turned * size, size)
        return first, second

    def gather_pieces(self, first, second):
        for step in range(self.bits):
            low, high = step, self.bits - 1 - step
            got_first = self.swap_bit(first, low)
            got_second = self.swap_bit(second, high)
            if step == self.bits - 1:
                return [first, got_first, second, got_second]
            first = jnp.where(
                self.bit_of(low) == 0,
                jnp.concatenate([first, got_first]),
                jnp.concatenate([got_first, first]),
            )
            second = jnp.where(
                self.bit_of(high) == 0,
                jnp.concatenate([second, got_second]),
                jnp.concatenate([got_second, second]),
            )

    def gather_positions(self, piece):
        size = piece.shape[0] // 2
        first, second = piece[:size], piece[size:]
        for step in range(self.bits):
            high, low = self.bits - 1 - step, step
            got_first = self.swap_bit(first, high)
            got_second = self.swap_bit(second, low)
            first = jnp.where(
                self.bit_of(high) == 0,
                jnp.concatenate([first, got_first]),
                jnp.concatenate([got_first, first]),
            )
            second = jnp.where(
                self.bit_of(low) == 0,
                jnp.concatenate([second, got_second]),
                jnp.concatenate([got_second, second]),
            )
        parts = []
        for position in range(self.replicas):
            turned = bit_reverse(position, self.bits)
            parts.append(first[position * size : (position + 1) * size])
            parts.append(second[turned * size : (turned + 1) * size])
        return jnp.concatenate(parts)

    def to_chip(self, piece, moves):
        got = self.along(piece, moves)
        return add_bf(piece, got)


def add_bf(left, right):
    return (left.astype(jnp.float32) + right.astype(jnp.float32)).astype(jnp.bfloat16)


vector_pad = 16


def dot(left, right, left_dim, right_dim):
    return lax.dot_general(
        left,
        right,
        (((left_dim,), (right_dim,)), ((), ())),
        preferred_element_type=jnp.float32,
    )


def norm_parts(values):
    centred = values - jnp.mean(values, axis=-1, keepdims=True)
    scale = lax.rsqrt(jnp.mean(centred * centred, axis=-1, keepdims=True) + norm_eps)
    return centred * scale, scale


def norm_back(unit, scale, grad):
    inner = jnp.mean(grad, axis=-1, keepdims=True)
    outer = jnp.mean(grad * unit, axis=-1, keepdims=True)
    return scale * (grad - inner - unit * outer)


def row_sum(values):
    return jnp.sum(values, axis=0, keepdims=True)


def left_lanes(value):
    return lax.broadcasted_iota(jnp.int32, value.shape, 1) < HEAD


def head_parts(pair):
    left = left_lanes(pair)
    none = jnp.zeros_like(pair)
    return jnp.where(left, pair, none), jnp.where(left, none, pair)


def load_blocks(place, blocks, rows, target, sem, first, last):
    quarter = rows // 4
    starts = (
        place[7] * quarter,
        (1 - place[7]) * quarter,
        (2 + place[5]) * quarter,
        (3 - place[5]) * quarter,
    )
    for slot in range(4):
        chip = place[slot]

        @pl.when((chip >= first) & (chip < last))
        def _():
            for side in range(2):
                core = place[4] if side == 0 else 1 - place[4]
                number = (chip - first) * 2 + core
                if slot == 0:
                    parts = [(blocks[side], 0, rows)]
                else:
                    at = 2 + (slot - 1) * 8 + side
                    parts = [
                        (blocks[at + 2 * index], starts[index], quarter) for index in range(4)
                    ]
                for ref, shift, size in parts:
                    start = pl.multiple_of(number * rows + shift, 16)
                    pltpu.make_async_copy(ref, target.at[pl.ds(start, size)], sem.at[number]).start()

    done = set()

    def ready(low, high):
        for number in range(low // rows, -(-high // rows)):
            if number in done:
                continue
            done.add(number)
            index = number - 2 * first
            pltpu.make_async_copy(
                blocks[0], target.at[pl.ds(index * rows, rows)], sem.at[index]
            ).wait()

    return ready


block_count = 26


def spread_terms(place, terms, rows, first, outs, wide, lane=0):
    core, across = place[4], place[5]
    count = terms.shape[0]
    for index, out in enumerate(outs):
        block = core if index % 2 == 0 else 1 - core
        side = across if index < 2 else 1 - across
        start = pl.multiple_of(first + block * rows + side * (rows - wide), 128)
        out[:count, lane : lane + wide] = terms[:, pl.ds(start, wide)]


def query_kernel(rows, place, tok, seg_col, seg_row, vec_all, *rest):
    blocks = rest[:block_count]
    n_out, qkv, probs, att, w_in, load_sem = rest[block_count:]
    ready = load_blocks(place, blocks, rows, w_in, load_sem, 0, 1)
    unit, _ = norm_parts(tok[...].astype(jnp.float32))
    n_one = (unit * vec_all[0:1, :] + vec_all[1:2, :]).astype(jnp.bfloat16)
    n_out[...] = n_one
    for index, bias in enumerate((vec_all[2:3, :], None, vec_all[3:4, :])):
        ready(index * HID, (index + 1) * HID)
        value = dot(n_one, w_in[index * HID : (index + 1) * HID], 1, 1)
        if bias is not None:
            value = value + bias
        qkv[:, index * HID : (index + 1) * HID] = value.astype(jnp.bfloat16)
    length = seg_row.shape[1]
    for seq in range(seg_row.shape[0]):
        span = slice(seq * length, (seq + 1) * length)
        order = lax.broadcasted_iota(jnp.int32, (length, length), 0)
        other = lax.broadcasted_iota(jnp.int32, (length, length), 1)
        allowed = (other <= order) & (seg_col[span, :] == seg_row[seq : seq + 1, :])
        for pair in range(HEADS // 2):
            lanes = slice(pair * 2 * HEAD, (pair + 1) * 2 * HEAD)
            key_pair = qkv[span, HID + lanes.start : HID + lanes.stop]
            value_pair = qkv[span, 2 * HID + lanes.start : 2 * HID + lanes.stop]
            mixed = []
            for half, query in enumerate(head_parts(qkv[span, lanes])):
                raw = dot(query, key_pair, 1, 1) * HEAD ** (-0.5)
                raw = jnp.where(allowed, raw, masked_score)
                top = jnp.max(raw, axis=-1, keepdims=True)
                power = jnp.exp(raw - top)
                prob = power * (1.0 / jnp.sum(power, axis=-1, keepdims=True))
                probs[seq * HEADS + 2 * pair + half] = prob
                mixed.append(dot(prob.astype(jnp.bfloat16), value_pair, 1, 0))
            att[span, lanes] = jnp.where(left_lanes(mixed[0]), mixed[0], mixed[1]).astype(
                jnp.bfloat16
            )


def active_kernel(rows, place, tok, att, vec_all, *rest):
    blocks = rest[:block_count]
    n_out, hidden, act, slope_out = rest[block_count : block_count + 4]
    windows = rest[block_count + 4 : block_count + 8]
    w_mid, load_sem = rest[block_count + 8 :]
    ready = load_blocks(place, blocks, rows, w_mid, load_sem, 1, 3)
    base = 2 * rows

    def weight(first, size):
        ready(first, first + size)
        return w_mid[first - base : first - base + size]

    h_value = tok[...].astype(jnp.float32) + dot(att[...], weight(3 * HID, HID), 1, 0)
    h_value = h_value + vec_all[4:5, :]
    hidden[...] = h_value
    unit, _ = norm_parts(h_value)
    n_two = (unit * vec_all[5:6, :] + vec_all[6:7, :]).astype(jnp.bfloat16)
    n_out[...] = n_two
    root = math.sqrt(2.0 / math.pi)
    for index in range(FF // D):
        span = slice(index * D, (index + 1) * D)
        pre = dot(n_two, weight(4 * HID + index * D, D), 1, 1) + vec_all[7 + index : 8 + index, :]
        squared = pre * pre
        bent = jnp.tanh(root * (pre + 0.044715 * (pre * squared)))
        half = 0.5 * (1.0 + bent)
        act[:, span] = (pre * half).astype(jnp.bfloat16)
        slope_out[:, span] = half + 0.5 * pre * (1.0 - bent * bent) * (
            root * (1.0 + 3 * 0.044715 * squared)
        )
    wide = windows[0].shape[1]
    spread_terms(place, act, rows, 6 * rows - (4 * HID + FF), windows, wide)
    windows[1][:, wide:] = n_two
    windows[2][:, wide:] = n_two
    ready(2 * rows, 6 * rows)


def change_kernel(rows, place, cot, att, act, slope, hidden, vec_all, *rest):
    blocks = rest[:block_count]
    rest = rest[block_count:]
    out, dub, vec_out = rest[:3]
    windows = rest[3:7]
    w_top, terms, load_sem = rest[7:]
    ready = load_blocks(place, blocks, rows, w_top, load_sem, 2, 4)
    base = 4 * rows
    terms[:, :HID] = att[...]
    result = hidden[...] + vec_all[11:12, :]
    for index in range(FF // D):
        span = slice(index * D, (index + 1) * D)
        first = 4 * HID + FF + index * D - base
        ready(first + base, first + base + D)
        weight = w_top[first : first + D]
        active = act[:, span]
        change = dot(cot[...], weight, 1, 1) * slope[:, span]
        change_bf = change.astype(jnp.bfloat16)
        dub[:, span] = change_bf
        terms[:, HID + index * D : HID + (index + 1) * D] = change_bf
        terms[:, HID + FF + index * D : HID + FF + (index + 1) * D] = active
        vec_out[index : index + 1, :] = row_sum(change)
        result = result + dot(active, weight, 1, 0)
    wide = windows[0].shape[1] // 2
    spread_terms(place, terms, rows, 2 * rows, windows, wide)
    spread_terms(place, terms, rows, 0, windows, wide, wide)
    out[...] = result.astype(jnp.bfloat16)
    vec_out[4:5, :] = row_sum(cot[...].astype(jnp.float32))
    vec_out[5:8, :] = jnp.zeros((3, D), jnp.float32)
    ready(4 * rows, 8 * rows)


def hidden_kernel(rows, place, dub, hidden, cot, vec_all, *rest):
    blocks = rest[:block_count]
    dh, dh_bf, da, vec_out, w_mid, load_sem = rest[block_count:]
    ready = load_blocks(place, blocks, rows, w_mid, load_sem, 1, 3)
    base = 2 * rows
    unit, scale = norm_parts(hidden[...])
    start = 4 * HID
    back = None
    while start < 4 * HID + FF:
        stop = min((start // rows + 1) * rows, 4 * HID + FF)
        ready(start, stop)
        part = dot(dub[:, start - 4 * HID : stop - 4 * HID], w_mid[start - base : stop - base], 1, 0)
        back = part if back is None else back + part
        start = stop
    vec_out[0:1, :] = row_sum(back * unit)
    vec_out[1:2, :] = row_sum(back)
    value = cot[...].astype(jnp.float32) + norm_back(unit, scale, back * vec_all[5:6, :])
    dh[...] = value
    vec_out[2:3, :] = row_sum(value)
    vec_out[3:8, :] = jnp.zeros((5, D), jnp.float32)
    rounded = value.astype(jnp.bfloat16)
    dh_bf[...] = rounded
    da[...] = dot(rounded, w_mid[3 * HID - base : 4 * HID - base], 1, 1).astype(jnp.bfloat16)


def attention_kernel(rows, place, da, qkv, probs, dh, tok, vec_all, vec_first, vec_second, *rest):
    blocks = rest[:block_count]
    rest = rest[block_count:]
    grad_tok = rest[0]
    windows = rest[1:5]
    w_in, dqkv, vec_out, packed, load_sem = rest[5:]
    ready = load_blocks(place, blocks, rows, w_in, load_sem, 0, 1)
    heads_total = probs.shape[0]
    length = probs.shape[1]
    vec_out[2:4, :] = jnp.zeros((2, D), jnp.float32)
    for seq in range(heads_total // HEADS):
        span = slice(seq * length, (seq + 1) * length)
        for pair in range(HEADS // 2):
            lanes = slice(pair * 2 * HEAD, (pair + 1) * 2 * HEAD)
            query_pair = qkv[span, lanes]
            key_pair = qkv[span, HID + lanes.start : HID + lanes.stop]
            value_pair = qkv[span, 2 * HID + lanes.start : 2 * HID + lanes.stop]
            da_pair = da[span, lanes]
            got = []
            for half, da_head in enumerate(head_parts(da_pair)):
                prob = probs[seq * HEADS + 2 * pair + half]
                grad_prob = dot(da_head, value_pair, 1, 1)
                inner = jnp.sum(prob * grad_prob, axis=-1, keepdims=True)
                grad_score = (prob * (grad_prob - inner) * HEAD ** (-0.5)).astype(jnp.bfloat16)
                got.append(
                    (
                        dot(grad_score, key_pair, 1, 0),
                        dot(grad_score, query_pair, 0, 0),
                        dot(prob.astype(jnp.bfloat16), da_pair, 0, 0),
                    )
                )
            left = left_lanes(got[0][0])
            query_grad, key_grad, value_grad = [
                jnp.where(left, one, two) for one, two in zip(got[0], got[1])
            ]
            dqkv[span, lanes] = query_grad.astype(jnp.bfloat16)
            dqkv[span, HID + lanes.start : HID + lanes.stop] = key_grad.astype(jnp.bfloat16)
            dqkv[span, 2 * HID + lanes.start : 2 * HID + lanes.stop] = value_grad.astype(
                jnp.bfloat16
            )
            vec_out[2:3, lanes] = vec_out[2:3, lanes] + row_sum(query_grad)
            vec_out[3:4, lanes] = vec_out[3:4, lanes] + row_sum(value_grad)
    unit, scale = norm_parts(tok[...].astype(jnp.float32))
    ready(0, 2 * rows)
    back = dot(dqkv[...], w_in[...], 1, 0)
    grad_tok[...] = dh[...] + norm_back(unit, scale, back * vec_all[0:1, :])
    vec_out[0:1, :] = row_sum(back * unit)
    vec_out[1:2, :] = row_sum(back)
    vec_out[4:5, :] = vec_second[2:3, :]
    vec_out[5:7, :] = vec_second[0:2, :]
    vec_out[7:12, :] = vec_first[0:5, :]
    wide = windows[0].shape[1]
    spread_terms(place, dqkv, rows, 0, windows, wide)
    packed[...] = jnp.zeros_like(packed)
    for at, lanes, row, source in vector_tiles(wide):
        packed[at : at + 1, lanes] = vec_out[row : row + 1, source]
    for window in windows:
        window[dqkv.shape[0] :, :] = packed[...].astype(jnp.bfloat16)


def vector_tiles(wide):
    across, packed = D // 128, wide // 128
    for index in range(12 * across):
        at, to = divmod(index, packed)
        row, source = divmod(index, across)
        yield at, slice(to * 128, to * 128 + 128), row, slice(source * 128, source * 128 + 128)


def product_kernel(rows, wide, lane, starts, split, which, place, *rest):
    last = split is None and starts is None
    terms, columns, rest = rest[:4], rest[4:-6], rest[-6:]
    away, mine, left, right, whole, sums = rest
    if last:
        vec_all, columns = columns[0], columns[1:]
    count = columns[0].shape[0]
    for index in range(4):
        left[index * count : (index + 1) * count] = terms[index][:count, lane : lane + wide]
    core, across, high = place[4], place[5], place[6]

    def column(index):
        value = columns[index]
        if last and index > 0:
            unit, _ = norm_parts(value[:, :D].astype(jnp.float32))
            return (unit * vec_all[0:1, :] + vec_all[1:2, :]).astype(jnp.bfloat16)
        start = 0 if last else starts[index]
        return value[:, start : start + D]

    def put(span, other):
        for index in range(4):
            value = column(index)
            if other is not None:
                value = jnp.where(other, column(4 + index), value)
            right[index * count : (index + 1) * count] = value
        whole[span, :] = dot(left[:, span], right[...], 0, 0).astype(jnp.bfloat16)

    if split is None:
        put(slice(0, wide), None)
    else:
        start = rows - wide
        chosen = core == which
        if split <= start:
            put(slice(0, split), chosen & (across == 1))
            put(slice(split, wide), chosen)
        else:
            put(slice(0, split - start), chosen)
            put(slice(split - start, wide), chosen & (across == 0))
    part = rows // 4
    first = across * (wide - rows // 2)
    away[:part] = whole[pl.ds(pl.multiple_of(first + (1 - high) * part, 16), part), :]
    mine[:part] = whole[pl.ds(pl.multiple_of(first + high * part, 16), part), :]
    if last:
        total = terms[0][count:, :].astype(jnp.float32)
        for index in range(1, 4):
            total = total + terms[index][count:, :].astype(jnp.float32)
        sums[...] = jnp.zeros_like(sums)
        for at, lanes, row, source in vector_tiles(wide):
            sums[row : row + 1, source] = total[at : at + 1, lanes]
        away[part:] = sums[...].astype(jnp.bfloat16)
        mine[part:] = sums[...].astype(jnp.bfloat16)


any_spec = pl.BlockSpec(memory_space=pl.ANY)
vmem_spec = pl.BlockSpec(memory_space=pltpu.VMEM)
smem_spec = pl.BlockSpec(memory_space=pltpu.SMEM)
bf16, f32 = jnp.bfloat16, jnp.float32


def grant(inputs, outputs, scratch):
    arrays = [value for value, spec in inputs if spec is vmem_spec]
    arrays += [jax.ShapeDtypeStruct(shape, kind) for shape, kind, spec in outputs]
    need = 2 * sum(value.size * value.dtype.itemsize for value in arrays)
    for item in scratch:
        if hasattr(item, "shape") and item.dtype in (bf16, f32):
            need += math.prod(item.shape) * jnp.dtype(item.dtype).itemsize
    return need + 6 * 1024 * 1024


def call(kernel, inputs, outputs, scratch, flops, moved):
    return pl.pallas_call(
        kernel,
        grid=(1,),
        in_specs=[spec for _, spec in inputs],
        out_specs=[spec for _, _, spec in outputs],
        out_shape=[jax.ShapeDtypeStruct(shape, kind) for shape, kind, _ in outputs],
        scratch_shapes=scratch,
        compiler_params=pltpu.CompilerParams(vmem_limit_bytes=grant(inputs, outputs, scratch)),
        cost_estimate=pl.CostEstimate(flops=flops, bytes_accessed=moved, transcendentals=0),
    )(*[value for value, _ in inputs])


def after(kernel, inputs, waits):
    count, extra = len(inputs), len(waits)

    def body(*refs):
        kernel(*refs[:count], *refs[count + extra :])

    return body, inputs + [(value, any_spec) for value in waits]


def parameter_blocks(links, weights, vectors):
    shards = links.chips * links.cores
    width = vectors.shape[1]
    number = links.chip * links.cores + links.core
    location = lax.broadcasted_iota(jnp.int32, (vectors.shape[0], width * shards), 1) // width
    spread = jnp.where(location == number, jnp.tile(vectors, (1, shards)), 0.0)
    spread = jnp.pad(spread, ((0, vector_pad - vectors.shape[0]), (0, 0))).astype(bf16)
    first, second = links.own_pieces(weights)
    size = first.shape[0]
    mine = jnp.concatenate([first.astype(bf16), second.astype(bf16), spread])
    inner = (links.chip == 1) | (links.chip == 2)
    near = links.along(mine, {0: 1, 1: 0, 2: 3, 3: 2})
    middle = links.along(mine, {1: 2, 2: 1})
    across = links.along(near, {1: 2, 2: 1})
    outward = links.along(middle, {1: 0, 2: 3})
    far = links.along(across, {1: 0, 2: 3})
    block = weights.astype(bf16)
    blocks = [block, links.swap_core(block)]
    slots = (near, jnp.where(inner, middle, outward), jnp.where(inner, across, far))
    total = spread
    for slot in slots:
        total = total + slot[2 * size :]
        for piece in links.gather_pieces(slot[:size], slot[size : 2 * size]):
            blocks += [piece, links.swap_core(piece)]
    total = total + links.swap_core(total)
    return blocks, total.astype(f32)


def direct_step(links, tokens, segments, cotangent, state, vectors):
    count = tokens.shape[0]
    weights = state[0]
    rows = weights.shape[0]
    wide = -(-rows // 256) * 128
    blocks, vec_all = parameter_blocks(links, weights, vectors)
    low = links.chip < links.chips // 2
    place = jnp.stack(
        [
            links.chip,
            links.chip ^ 1,
            jnp.where(low, 2, 1),
            jnp.where(low, 3, 0),
            links.core,
            links.bit_of(0),
            links.bit_of(1),
            links.bit_of(links.bits - 1),
        ]
    ).astype(jnp.int32)
    ends = [(place, smem_spec)]
    pairs = segments.shape[0] * HEADS
    length = segments.shape[1]
    unit_cost = 2 * count * HID * D
    parameters = [(block, any_spec) for block in blocks]

    def full(*arrays):
        return [(array, vmem_spec) for array in arrays]

    def shape(width, kind=bf16, height=count):
        return (height, width), kind, vmem_spec

    def weight_scratch(chips):
        return [pltpu.VMEM((chips * 2 * rows, D), bf16)]

    def weight_sem(chips):
        return [pltpu.SemaphoreType.DMA((chips * 2,))]

    def share_rows(parts):
        own, to_core, to_side, to_both = parts
        side = links.swap_bit(to_side, 0)
        both = links.swap_both(to_both, 0)
        other = links.swap_core(to_core)
        return [own, other, side, both]

    joined = jnp.concatenate([tokens, cotangent], axis=1)
    joined_side = links.swap_bit(joined, 0)
    joined_core = links.swap_core(joined)
    joined_both = links.swap_core(joined_side)
    joined_all = [joined, joined_core, joined_side, joined_both]
    column = segments.reshape(count, 1)
    n_one, qkv, probs, att = call(
        functools.partial(query_kernel, rows),
        ends + full(tokens, column, segments, vec_all) + parameters,
        [
            shape(D),
            shape(3 * HID),
            ((pairs, length, length), f32, vmem_spec),
            shape(HID),
        ],
        weight_scratch(1) + weight_sem(1),
        4 * unit_cost,
        6 * HID * D,
    )
    active_out = call(
        functools.partial(active_kernel, rows),
        ends + full(tokens, att, vec_all) + parameters,
        [shape(D), shape(D, f32), shape(FF), shape(FF, f32)]
        + [shape(wide), shape(wide + D), shape(wide + D), shape(wide)],
        weight_scratch(2) + weight_sem(2),
        5 * unit_cost,
        8 * rows * D,
    )
    n_two, hidden, act, slope = active_out[:4]
    rows_three = share_rows(active_out[4:])
    n_two_both = links.swap_core(rows_three[2])
    n_two_all = [n_two, rows_three[1], rows_three[2], n_two_both]
    n_two_starts = [0, wide, wide, wide]
    change_out = call(
        functools.partial(change_kernel, rows),
        ends + full(cotangent, att, act, slope, hidden, vec_all) + parameters,
        [shape(D), shape(FF), shape(D, f32, 8)] + [shape(2 * wide)] * 4,
        weight_scratch(2) + [pltpu.VMEM((count, HID + 2 * FF), bf16)] + weight_sem(2),
        8 * unit_cost,
        8 * rows * D,
    )
    out, dub, vec_first = change_out[:3]
    rows_middle = share_rows(change_out[3:])

    def product(parts, columns, lane, starts, split=None, which=0, waits=()):
        extra = 0 if starts is not None else vector_pad
        kernel, inputs = after(
            functools.partial(product_kernel, rows, wide, lane, starts, split, which),
            ends + full(*parts) + full(*columns),
            list(waits),
        )
        return call(
            kernel,
            inputs,
            [shape(D, bf16, rows // 4 + extra)] * 2,
            [
                pltpu.VMEM((4 * count, wide), bf16),
                pltpu.VMEM((4 * count, D), bf16),
                pltpu.VMEM((wide, D), bf16),
                pltpu.VMEM((vector_pad, D), f32),
            ],
            8 * count * wide * D,
            4 * rows * D,
        )

    def scatter_rest(parts):
        away, mine = parts
        got = links.swap_bit(away, 1)
        mine = add_bf(mine, got)
        part = rows // 4
        mine, rest = mine[:part], mine[part:]
        for bit in range(2, links.bits):
            size = mine.shape[0] // 2
            away = lax.dynamic_slice_in_dim(mine, (1 - links.bit_of(bit)) * size, size)
            near = lax.dynamic_slice_in_dim(mine, links.bit_of(bit) * size, size)
            mine = add_bf(near, links.swap_bit(away, bit))
            if rest.shape[0]:
                rest = add_bf(rest, links.swap_bit(rest, bit))
        return jnp.concatenate([mine, rest]) if rest.shape[0] else mine

    product_three = product(rows_three, joined_all, 0, [D] * 4)
    three = scatter_rest(product_three)
    kernel, inputs = after(
        functools.partial(hidden_kernel, rows),
        ends + full(dub, hidden, cotangent, vec_all) + parameters,
        product_three[:1],
    )
    dh, dh_bf, da, vec_second = call(
        kernel,
        inputs,
        [shape(D, f32), shape(D), shape(HID), shape(D, f32, 8)],
        weight_scratch(2) + weight_sem(2),
        5 * unit_cost,
        8 * rows * D,
    )
    dh_side = links.swap_bit(dh_bf, 0)
    dh_core = links.swap_core(dh_bf)
    dh_both = links.swap_core(dh_side)
    dh_all = [dh_bf, dh_core, dh_side, dh_both]
    kernel, inputs = after(
        functools.partial(attention_kernel, rows),
        ends + full(da, qkv, probs, dh, tokens, vec_all, vec_first, vec_second) + parameters,
        [vec_second],
    )
    attention_out = call(
        kernel,
        inputs,
        [shape(D, f32)] + [shape(wide, bf16, count + vector_pad)] * 4,
        weight_scratch(1)
        + [
            pltpu.VMEM((count, 3 * HID), bf16),
            pltpu.VMEM((vector_pad, D), f32),
            pltpu.VMEM((vector_pad, wide), f32),
        ]
        + weight_sem(1),
        4 * unit_cost,
        4 * rows * D,
    )
    grad_tok = attention_out[0]
    rows_zero = share_rows(attention_out[1:])
    product_two = product(
        rows_middle,
        n_two_all + joined_all,
        0,
        n_two_starts + [D] * 4,
        4 * HID + FF - 5 * rows,
        1,
        waits=[grad_tok],
    )
    two = scatter_rest(product_two)
    product_one = product(
        rows_middle,
        n_two_all + dh_all,
        wide,
        n_two_starts + [0] * 4,
        4 * HID - 2 * rows,
        0,
        waits=product_two[:1],
    )
    one = scatter_rest(product_one)
    product_zero = product(
        rows_zero, [vec_all, n_one] + joined_all[1:], 0, None, waits=product_one[:1]
    )
    zero = scatter_rest(product_zero)
    three, _ = lax.optimization_barrier((three, product_two[1]))
    three = links.to_chip(three, {0: 1, 2: 3})
    two = links.to_chip(two, {0: 1, 3: 2})
    three = links.to_chip(three, {1: 3})
    two = links.to_chip(two, {1: 2})
    one = links.to_chip(one, {0: 1, 3: 2})
    one = links.to_chip(one, {2: 1})
    zero = links.to_chip(zero, {0: 1, 1: 0, 2: 3, 3: 2})
    zero = links.to_chip(zero, {0: 2, 2: 0})
    mine = jnp.where(links.chip == 1, one, jnp.where(links.chip == 2, two, three))
    size = mine.shape[0]
    mine = jnp.where(links.chip == 0, zero[:size], mine)
    grad_w = links.gather_positions(mine).astype(f32)
    sums = zero[size:]
    got = links.along(sums, {0: 1, 2: 3})
    sums = jnp.where(links.chip % 2 == 0, sums, got).astype(f32)
    width = vectors.shape[1]
    grad_v = lax.dynamic_slice_in_dim(sums, lax.axis_index("shard") * width, width, 1)
    new = [grad_w] + list(adam_update(*state, grad_w, decay_rate))
    return out, grad_tok, grad_v[: vectors.shape[0]], new


def per_device(
    replicas,
    shards,
    tokens,
    segments,
    cotangent,
    weights,
    vectors,
    first_weights,
    first_vectors,
    second_weights,
    second_vectors,
):
    if Links.fits(replicas, shards, weights.shape[0]):
        output, grad_tokens, grad_v, new = direct_step(
            Links(replicas, shards),
            tokens,
            segments,
            cotangent,
            (weights, first_weights, second_weights),
            vectors,
        )
    else:
        w_full = lax.all_gather(weights.astype(jnp.bfloat16), "shard", axis=0, tiled=True)
        v_full = lax.all_gather(vectors.astype(jnp.bfloat16), "shard", axis=1, tiled=True)
        output, kept_state = forward(tokens, segments, w_full, v_full)
        grad_tokens, grad_vec, row_terms, col_terms = backward(
            kept_state, cotangent, segments, w_full
        )
        local_grad = weight_grads(row_terms, col_terms).astype(jnp.bfloat16)
        own_w = lax.psum_scatter(local_grad, "shard", scatter_dimension=0, tiled=True)
        own_v = lax.psum_scatter(
            grad_vec.astype(jnp.bfloat16), "shard", scatter_dimension=1, tiled=True
        )
        grad_w = lax.psum(own_w, "rep").astype(jnp.float32)
        grad_v = lax.psum(own_v, "rep").astype(jnp.float32)
        new = [grad_w]
        new += adam_update(weights, first_weights, second_weights, grad_w, decay_rate)
    grad_w, new_w, new_fw, new_sw = new
    new_v, new_fv, new_sv = adam_update(vectors, first_vectors, second_vectors, grad_v, 0.0)
    return (output, grad_tokens, grad_w, grad_v, new_w, new_v, new_fw, new_fv, new_sw, new_sv)


def solution(mesh):
    placed = (
        P(("rep", "shard"), None),
        P(("rep", "shard"), None),
        P(("rep", "shard"), None),
        P("shard", None),
        P(None, "shard"),
        P("shard", None),
        P(None, "shard"),
        P("shard", None),
        P(None, "shard"),
    )
    return jax.shard_map(
        functools.partial(per_device, mesh.shape["rep"], mesh.shape["shard"]),
        mesh=mesh,
        in_specs=placed,
        out_specs=(
            P(("rep", "shard"), None),
            P(("rep", "shard"), None),
            P("shard", None),
            P(None, "shard"),
            P("shard", None),
            P(None, "shard"),
            P("shard", None),
            P(None, "shard"),
            P("shard", None),
            P(None, "shard"),
        ),
        check_vma=False,
    )
```

```python
import functools
import math

import jax
import jax.numpy as jnp
from jax import lax
from jax.experimental import pallas as pl
from jax.experimental.pallas import tpu as pltpu
from jax.sharding import PartitionSpec as P

D = 768
HEADS = 12
HEAD = 64
FF = 3072
STEP = 3
HID = 768
R = 9216


norm_eps = 1e-05
beta_one = 0.9
beta_two = 0.999
adam_eps = 1e-08
learn_rate = 0.2
decay_rate = 0.1
masked_score = -1e30


def normalize(values):
    centred = values - jnp.mean(values, axis=-1, keepdims=True)
    return centred * lax.rsqrt(jnp.mean(centred * centred, axis=-1, keepdims=True) + norm_eps)


def affine_norm(values, gain_vec, shift_vec):
    return normalize(values) * gain_vec + shift_vec


def gelu_tanh(values):
    return jax.nn.gelu(values, approximate=True)


def matmul(left_op, right_op):
    return jnp.dot(left_op, right_op, preferred_element_type=jnp.float32)


def matmul_nt(left_op, right_op):
    return lax.dot_general(
        left_op, right_op, (((1,), (1,)), ((), ())), preferred_element_type=jnp.float32
    )


def matmul_tn(left_op, right_op):
    return lax.dot_general(
        left_op, right_op, (((0,), (0,)), ((), ())), preferred_element_type=jnp.float32
    )


def product(pattern, left_op, right_op):
    return jnp.einsum(pattern, left_op, right_op, preferred_element_type=jnp.float32)


def allowed_pairs(segments):
    length = segments.shape[1]
    places = lax.broadcasted_iota(jnp.int32, (length, length), 0)
    others = lax.broadcasted_iota(jnp.int32, (length, length), 1)
    causal = others <= places
    same_doc = segments[:, :, None] == segments[:, None, :]
    return (causal[None] & same_doc)[:, None]


def scores_of(query_rows, key_rows, allowed):
    raw_scores = product("sqhd,skhd->shqk", query_rows, key_rows) * HEAD ** (-0.5)
    return jnp.where(allowed, raw_scores, masked_score)


def forward(tokens, segments, w_bf, v_bf):
    seq_count, length = segments.shape
    tok_count = tokens.shape[0]
    head_shape = (seq_count, length, HEADS, HEAD)
    floats = v_bf.astype(jnp.float32)
    residual = tokens.astype(jnp.float32)
    normed_one = affine_norm(residual, floats[0], floats[1]).astype(jnp.bfloat16)
    projected = matmul_nt(normed_one, w_bf[: 3 * HID])
    query_rows = (projected[:, :HID] + floats[2]).astype(jnp.bfloat16)
    key_rows = projected[:, HID : 2 * HID].astype(jnp.bfloat16)
    value_rows = (projected[:, 2 * HID :] + floats[3]).astype(jnp.bfloat16)
    allowed = allowed_pairs(segments)
    scores = scores_of(query_rows.reshape(head_shape), key_rows.reshape(head_shape), allowed)
    row_max = jnp.max(scores, axis=-1, keepdims=True)
    log_total = row_max + jnp.log(jnp.sum(jnp.exp(scores - row_max), axis=-1, keepdims=True))
    attn_probs = jnp.exp(scores - log_total).astype(jnp.bfloat16)
    mixed_heads = product("shqk,skhd->sqhd", attn_probs, value_rows.reshape(head_shape))
    attended = mixed_heads.reshape(tok_count, HID).astype(jnp.bfloat16)
    hidden_one = residual + matmul(attended, w_bf[3 * HID : 4 * HID]) + floats[4]
    normed_two = affine_norm(hidden_one, floats[5], floats[6]).astype(jnp.bfloat16)
    pre_act = matmul_nt(normed_two, w_bf[4 * HID : 4 * HID + FF]) + floats[7:11].reshape(FF)
    active = gelu_tanh(pre_act).astype(jnp.bfloat16)
    output = (hidden_one + matmul(active, w_bf[4 * HID + FF :]) + floats[11]).astype(jnp.bfloat16)
    kept_state = (
        residual,
        normed_one,
        query_rows,
        key_rows,
        value_rows,
        log_total,
        attended,
        hidden_one,
        normed_two,
        pre_act,
        active,
        floats,
    )
    return (output, kept_state)


def backward(kept_state, cotangent, segments, w_bf):
    (
        residual,
        normed_one,
        query_rows,
        key_rows,
        value_rows,
        log_total,
        attended,
        hidden_one,
        normed_two,
        pre_act,
        active,
        floats,
    ) = kept_state
    seq_count, length = segments.shape
    tok_count = residual.shape[0]
    head_shape = (seq_count, length, HEADS, HEAD)
    grad_out = cotangent.astype(jnp.float32)
    grad_active = matmul_nt(cotangent, w_bf[4 * HID + FF :])
    grad_pre = jax.vjp(gelu_tanh, pre_act)[1](grad_active)[0]
    grad_pre_bf = grad_pre.astype(jnp.bfloat16)
    grad_normed_two = matmul(grad_pre_bf, w_bf[4 * HID : 4 * HID + FF])
    norm_back_two = jax.vjp(affine_norm, hidden_one, floats[5], floats[6])[1]
    grad_h_part, grad_gain_two, grad_shift_two = norm_back_two(grad_normed_two)
    grad_hidden = grad_out + grad_h_part
    grad_hidden_bf = grad_hidden.astype(jnp.bfloat16)
    grad_attended = matmul_nt(grad_hidden_bf, w_bf[3 * HID : 4 * HID]).astype(jnp.bfloat16)
    query_four = query_rows.reshape(head_shape)
    key_four = key_rows.reshape(head_shape)
    value_four = value_rows.reshape(head_shape)
    grad_att_four = grad_attended.reshape(head_shape)
    allowed = allowed_pairs(segments)
    scores = scores_of(query_four, key_four, allowed)
    attn_probs = jnp.exp(scores - log_total)
    probs_bf = attn_probs.astype(jnp.bfloat16)
    grad_probs = product("sqhd,skhd->shqk", grad_att_four, value_four)
    inner_sum = jnp.sum(attn_probs * grad_probs, axis=-1, keepdims=True)
    grad_scores = (attn_probs * (grad_probs - inner_sum) * HEAD ** (-0.5)).astype(jnp.bfloat16)
    grad_query = product("shqk,skhd->sqhd", grad_scores, key_four).reshape(tok_count, HID)
    grad_keys = product("shqk,sqhd->skhd", grad_scores, query_four).reshape(tok_count, HID)
    grad_values = product("shqk,sqhd->skhd", probs_bf, grad_att_four).reshape(tok_count, HID)
    grad_proj = jnp.concatenate([grad_query, grad_keys, grad_values], axis=1)
    grad_proj_bf = grad_proj.astype(jnp.bfloat16)
    grad_normed_one = matmul(grad_proj_bf, w_bf[: 3 * HID])
    norm_back_one = jax.vjp(affine_norm, residual, floats[0], floats[1])[1]
    grad_r_part, grad_gain_one, grad_shift_one = norm_back_one(grad_normed_one)
    grad_tokens = grad_hidden + grad_r_part
    bias_ff = jnp.sum(grad_pre, axis=0).reshape(FF // D, D)
    head_rows = jnp.stack(
        [
            grad_gain_one,
            grad_shift_one,
            jnp.sum(grad_query, axis=0),
            jnp.sum(grad_values, axis=0),
            jnp.sum(grad_hidden, axis=0),
            grad_gain_two,
            grad_shift_two,
        ]
    )
    grad_vec = jnp.concatenate([head_rows, bias_ff, jnp.sum(grad_out, axis=0)[None]], axis=0)
    row_terms = jnp.concatenate([grad_proj_bf, attended, grad_pre_bf, active], axis=1)
    col_terms = jnp.stack([normed_one, grad_hidden_bf, normed_two, cotangent])
    return (grad_tokens, grad_vec, row_terms, col_terms)


def weight_grads(row_terms, col_terms):
    row_bounds = (0, 3 * HID, 4 * HID, 4 * HID + FF, R)
    pieces = [
        matmul_tn(row_terms[:, row_bounds[index] : row_bounds[index + 1]], col_terms[index])
        for index in range(4)
    ]
    return jnp.concatenate(pieces, axis=0)


def adam_update(param, first, second, grad, decay):
    new_first = beta_one * first + (1.0 - beta_one) * grad
    new_second = beta_two * second + (1.0 - beta_two) * grad * grad
    first_hat = new_first / (1.0 - beta_one**STEP)
    second_hat = new_second / (1.0 - beta_two**STEP)
    new_param = param - learn_rate * (first_hat / (jnp.sqrt(second_hat) + adam_eps) + decay * param)
    return (new_param, new_first, new_second)


def bit_reverse(index, bits):
    out = index * 0
    for place in range(bits):
        out = out * 2 + (index >> place) % 2
    return out


class Links:
    def __init__(self, replicas, shards):
        self.replicas = replicas
        self.cores = 2
        self.chips = shards // self.cores
        self.bits = replicas.bit_length() - 1
        self.replica = lax.axis_index("rep")
        shard = lax.axis_index("shard")
        self.chip = shard // self.cores
        self.core = shard % self.cores

    @staticmethod
    def fits(replicas, shards, rows):
        power = replicas > 2 and replicas & (replicas - 1) == 0
        return shards == 8 and power and 2 * rows == 3 * HID

    def send(self, value, target):
        route = []
        for rep in range(self.replicas):
            for chip in range(self.chips):
                for core in range(self.cores):
                    goal = target(rep, chip, core)
                    if goal is None:
                        continue
                    start = (rep * self.chips + chip) * self.cores + core
                    stop = (goal[0] * self.chips + goal[1]) * self.cores + goal[2]
                    route.append((start, stop))
        return lax.ppermute(value, ("rep", "shard"), route)

    def swap_core(self, value):
        return self.send(value, lambda rep, chip, core: (rep, chip, 1 - core))

    def swap_both(self, value, bit):
        return self.send(value, lambda rep, chip, core: (rep ^ (1 << bit), chip, 1 - core))

    def swap_bit(self, value, bit):
        return self.send(value, lambda rep, chip, core: (rep ^ (1 << bit), chip, core))

    def along(self, value, moves):
        table = dict(moves)
        return self.send(
            value, lambda rep, chip, core: (rep, table[chip], core) if chip in table else None
        )

    def bit_of(self, bit):
        return (self.replica >> bit) % 2

    def own_pieces(self, block):
        half = block.shape[0] // 2
        size = half // self.replicas
        first = lax.dynamic_slice_in_dim(block, self.replica * size, size)
        turned = bit_reverse(self.replica, self.bits)
        second = lax.dynamic_slice_in_dim(block, half + turned * size, size)
        return first, second

    def gather_pieces(self, first, second):
        for step in range(self.bits):
            low, high = step, self.bits - 1 - step
            got_first = self.swap_bit(first, low)
            got_second = self.swap_bit(second, high)
            if step == self.bits - 1:
                return [first, got_first, second, got_second]
            first = jnp.where(
                self.bit_of(low) == 0,
                jnp.concatenate([first, got_first]),
                jnp.concatenate([got_first, first]),
            )
            second = jnp.where(
                self.bit_of(high) == 0,
                jnp.concatenate([second, got_second]),
                jnp.concatenate([got_second, second]),
            )

    def gather_positions(self, piece):
        size = piece.shape[0] // 2
        first, second = piece[:size], piece[size:]
        for step in range(self.bits):
            high, low = self.bits - 1 - step, step
            got_first = self.swap_bit(first, high)
            got_second = self.swap_bit(second, low)
            first = jnp.where(
                self.bit_of(high) == 0,
                jnp.concatenate([first, got_first]),
                jnp.concatenate([got_first, first]),
            )
            second = jnp.where(
                self.bit_of(low) == 0,
                jnp.concatenate([second, got_second]),
                jnp.concatenate([got_second, second]),
            )
        parts = []
        for position in range(self.replicas):
            turned = bit_reverse(position, self.bits)
            parts.append(first[position * size : (position + 1) * size])
            parts.append(second[turned * size : (turned + 1) * size])
        return jnp.concatenate(parts)

    def to_chip(self, piece, moves):
        got = self.along(piece, moves)
        return add_bf(piece, got)


def add_bf(left, right):
    return (left.astype(jnp.float32) + right.astype(jnp.float32)).astype(jnp.bfloat16)


vector_pad = 16


def dot(left, right, left_dim, right_dim):
    return lax.dot_general(
        left,
        right,
        (((left_dim,), (right_dim,)), ((), ())),
        preferred_element_type=jnp.float32,
    )


def norm_parts(values):
    centred = values - jnp.mean(values, axis=-1, keepdims=True)
    scale = lax.rsqrt(jnp.mean(centred * centred, axis=-1, keepdims=True) + norm_eps)
    return centred * scale, scale


def norm_back(unit, scale, grad):
    inner = jnp.mean(grad, axis=-1, keepdims=True)
    outer = jnp.mean(grad * unit, axis=-1, keepdims=True)
    return scale * (grad - inner - unit * outer)


def row_sum(values):
    return jnp.sum(values, axis=0, keepdims=True)


def left_lanes(value):
    return lax.broadcasted_iota(jnp.int32, value.shape, 1) < HEAD


def head_parts(pair):
    left = left_lanes(pair)
    none = jnp.zeros_like(pair)
    return jnp.where(left, pair, none), jnp.where(left, none, pair)


def load_blocks(place, blocks, rows, target, sem, first, last):
    quarter = rows // 4
    starts = (
        place[7] * quarter,
        (1 - place[7]) * quarter,
        (2 + place[5]) * quarter,
        (3 - place[5]) * quarter,
    )
    for slot in range(4):
        chip = place[slot]

        @pl.when((chip >= first) & (chip < last))
        def _():
            for side in range(2):
                core = place[4] if side == 0 else 1 - place[4]
                number = (chip - first) * 2 + core
                if slot == 0:
                    parts = [(blocks[side], 0, rows)]
                else:
                    at = 2 + (slot - 1) * 8 + side
                    parts = [
                        (blocks[at + 2 * index], starts[index], quarter) for index in range(4)
                    ]
                for ref, shift, size in parts:
                    start = pl.multiple_of(number * rows + shift, 16)
                    pltpu.make_async_copy(ref, target.at[pl.ds(start, size)], sem.at[number]).start()

    done = set()

    def ready(low, high):
        for number in range(low // rows, -(-high // rows)):
            if number in done:
                continue
            done.add(number)
            index = number - 2 * first
            pltpu.make_async_copy(
                blocks[0], target.at[pl.ds(index * rows, rows)], sem.at[index]
            ).wait()

    return ready


block_count = 26


def spread_terms(place, terms, rows, first, outs, wide, lane=0):
    core, across = place[4], place[5]
    count = terms.shape[0]
    for index, out in enumerate(outs):
        block = core if index % 2 == 0 else 1 - core
        side = across if index < 2 else 1 - across
        start = pl.multiple_of(first + block * rows + side * (rows - wide), 128)
        out[:count, lane : lane + wide] = terms[:, pl.ds(start, wide)]


def query_kernel(rows, place, tok, seg_col, seg_row, vec_all, *rest):
    blocks = rest[:block_count]
    n_out, qkv, probs, att, w_in, load_sem = rest[block_count:]
    ready = load_blocks(place, blocks, rows, w_in, load_sem, 0, 1)
    unit, _ = norm_parts(tok[...].astype(jnp.float32))
    n_one = (unit * vec_all[0:1, :] + vec_all[1:2, :]).astype(jnp.bfloat16)
    n_out[...] = n_one
    for index, bias in enumerate((vec_all[2:3, :], None, vec_all[3:4, :])):
        ready(index * HID, (index + 1) * HID)
        value = dot(n_one, w_in[index * HID : (index + 1) * HID], 1, 1)
        if bias is not None:
            value = value + bias
        qkv[:, index * HID : (index + 1) * HID] = value.astype(jnp.bfloat16)
    length = seg_row.shape[1]
    for seq in range(seg_row.shape[0]):
        span = slice(seq * length, (seq + 1) * length)
        order = lax.broadcasted_iota(jnp.int32, (length, length), 0)
        other = lax.broadcasted_iota(jnp.int32, (length, length), 1)
        allowed = (other <= order) & (seg_col[span, :] == seg_row[seq : seq + 1, :])
        for pair in range(HEADS // 2):
            lanes = slice(pair * 2 * HEAD, (pair + 1) * 2 * HEAD)
            key_pair = qkv[span, HID + lanes.start : HID + lanes.stop]
            value_pair = qkv[span, 2 * HID + lanes.start : 2 * HID + lanes.stop]
            mixed = []
            for half, query in enumerate(head_parts(qkv[span, lanes])):
                raw = dot(query, key_pair, 1, 1) * HEAD ** (-0.5)
                raw = jnp.where(allowed, raw, masked_score)
                top = jnp.max(raw, axis=-1, keepdims=True)
                power = jnp.exp(raw - top)
                prob = power * (1.0 / jnp.sum(power, axis=-1, keepdims=True))
                probs[seq * HEADS + 2 * pair + half] = prob
                mixed.append(dot(prob.astype(jnp.bfloat16), value_pair, 1, 0))
            att[span, lanes] = jnp.where(left_lanes(mixed[0]), mixed[0], mixed[1]).astype(
                jnp.bfloat16
            )


def active_kernel(rows, place, tok, att, vec_all, *rest):
    blocks = rest[:block_count]
    n_out, hidden, act, slope_out = rest[block_count : block_count + 4]
    windows = rest[block_count + 4 : block_count + 8]
    w_mid, load_sem = rest[block_count + 8 :]
    ready = load_blocks(place, blocks, rows, w_mid, load_sem, 1, 3)
    base = 2 * rows

    def weight(first, size):
        ready(first, first + size)
        return w_mid[first - base : first - base + size]

    h_value = tok[...].astype(jnp.float32) + dot(att[...], weight(3 * HID, HID), 1, 0)
    h_value = h_value + vec_all[4:5, :]
    hidden[...] = h_value
    unit, _ = norm_parts(h_value)
    n_two = (unit * vec_all[5:6, :] + vec_all[6:7, :]).astype(jnp.bfloat16)
    n_out[...] = n_two
    root = math.sqrt(2.0 / math.pi)
    for index in range(FF // D):
        span = slice(index * D, (index + 1) * D)
        pre = dot(n_two, weight(4 * HID + index * D, D), 1, 1) + vec_all[7 + index : 8 + index, :]
        squared = pre * pre
        bent = jnp.tanh(root * (pre + 0.044715 * (pre * squared)))
        half = 0.5 * (1.0 + bent)
        act[:, span] = (pre * half).astype(jnp.bfloat16)
        slope_out[:, span] = half + 0.5 * pre * (1.0 - bent * bent) * (
            root * (1.0 + 3 * 0.044715 * squared)
        )
    wide = windows[0].shape[1]
    spread_terms(place, act, rows, 6 * rows - (4 * HID + FF), windows, wide)
    windows[1][:, wide:] = n_two
    windows[2][:, wide:] = n_two
    ready(2 * rows, 6 * rows)


def change_kernel(rows, place, cot, att, act, slope, hidden, vec_all, *rest):
    blocks = rest[:block_count]
    rest = rest[block_count:]
    out, dub, vec_out = rest[:3]
    windows_two, windows_one = rest[3:7], rest[7:11]
    w_top, terms, load_sem = rest[11:]
    ready = load_blocks(place, blocks, rows, w_top, load_sem, 2, 4)
    base = 4 * rows
    terms[:, :HID] = att[...]
    result = hidden[...] + vec_all[11:12, :]
    for index in range(FF // D):
        span = slice(index * D, (index + 1) * D)
        first = 4 * HID + FF + index * D - base
        ready(first + base, first + base + D)
        weight = w_top[first : first + D]
        active = act[:, span]
        change = dot(cot[...], weight, 1, 1) * slope[:, span]
        change_bf = change.astype(jnp.bfloat16)
        dub[:, span] = change_bf
        terms[:, HID + index * D : HID + (index + 1) * D] = change_bf
        terms[:, HID + FF + index * D : HID + FF + (index + 1) * D] = active
        vec_out[index : index + 1, :] = row_sum(change)
        result = result + dot(active, weight, 1, 0)
    wide = windows_one[0].shape[1]
    spread_terms(place, terms, rows, 2 * rows, windows_two, wide)
    spread_terms(place, terms, rows, 0, windows_one, wide)
    out[...] = result.astype(jnp.bfloat16)
    vec_out[4:5, :] = row_sum(cot[...].astype(jnp.float32))
    vec_out[5:8, :] = jnp.zeros((3, D), jnp.float32)
    ready(4 * rows, 8 * rows)


def hidden_kernel(rows, place, dub, hidden, cot, vec_all, *rest):
    blocks = rest[:block_count]
    dh, dh_bf, da, vec_out, w_mid, load_sem = rest[block_count:]
    ready = load_blocks(place, blocks, rows, w_mid, load_sem, 1, 3)
    base = 2 * rows
    unit, scale = norm_parts(hidden[...])
    start = 4 * HID
    back = None
    while start < 4 * HID + FF:
        stop = min((start // rows + 1) * rows, 4 * HID + FF)
        ready(start, stop)
        part = dot(dub[:, start - 4 * HID : stop - 4 * HID], w_mid[start - base : stop - base], 1, 0)
        back = part if back is None else back + part
        start = stop
    vec_out[0:1, :] = row_sum(back * unit)
    vec_out[1:2, :] = row_sum(back)
    value = cot[...].astype(jnp.float32) + norm_back(unit, scale, back * vec_all[5:6, :])
    dh[...] = value
    vec_out[2:3, :] = row_sum(value)
    vec_out[3:8, :] = jnp.zeros((5, D), jnp.float32)
    rounded = value.astype(jnp.bfloat16)
    dh_bf[...] = rounded
    da[...] = dot(rounded, w_mid[3 * HID - base : 4 * HID - base], 1, 1).astype(jnp.bfloat16)


def attention_kernel(rows, place, da, qkv, probs, dh, tok, vec_all, vec_first, vec_second, *rest):
    blocks = rest[:block_count]
    rest = rest[block_count:]
    grad_tok = rest[0]
    windows = rest[1:5]
    w_in, dqkv, vec_out, packed, load_sem = rest[5:]
    ready = load_blocks(place, blocks, rows, w_in, load_sem, 0, 1)
    heads_total = probs.shape[0]
    length = probs.shape[1]
    vec_out[2:4, :] = jnp.zeros((2, D), jnp.float32)
    for seq in range(heads_total // HEADS):
        span = slice(seq * length, (seq + 1) * length)
        for pair in range(HEADS // 2):
            lanes = slice(pair * 2 * HEAD, (pair + 1) * 2 * HEAD)
            query_pair = qkv[span, lanes]
            key_pair = qkv[span, HID + lanes.start : HID + lanes.stop]
            value_pair = qkv[span, 2 * HID + lanes.start : 2 * HID + lanes.stop]
            da_pair = da[span, lanes]
            got = []
            for half, da_head in enumerate(head_parts(da_pair)):
                prob = probs[seq * HEADS + 2 * pair + half]
                grad_prob = dot(da_head, value_pair, 1, 1)
                inner = jnp.sum(prob * grad_prob, axis=-1, keepdims=True)
                grad_score = (prob * (grad_prob - inner) * HEAD ** (-0.5)).astype(jnp.bfloat16)
                got.append(
                    (
                        dot(grad_score, key_pair, 1, 0),
                        dot(grad_score, query_pair, 0, 0),
                        dot(prob.astype(jnp.bfloat16), da_pair, 0, 0),
                    )
                )
            left = left_lanes(got[0][0])
            query_grad, key_grad, value_grad = [
                jnp.where(left, one, two) for one, two in zip(got[0], got[1])
            ]
            dqkv[span, lanes] = query_grad.astype(jnp.bfloat16)
            dqkv[span, HID + lanes.start : HID + lanes.stop] = key_grad.astype(jnp.bfloat16)
            dqkv[span, 2 * HID + lanes.start : 2 * HID + lanes.stop] = value_grad.astype(
                jnp.bfloat16
            )
            vec_out[2:3, lanes] = vec_out[2:3, lanes] + row_sum(query_grad)
            vec_out[3:4, lanes] = vec_out[3:4, lanes] + row_sum(value_grad)
    unit, scale = norm_parts(tok[...].astype(jnp.float32))
    ready(0, 2 * rows)
    back = dot(dqkv[...], w_in[...], 1, 0)
    grad_tok[...] = dh[...] + norm_back(unit, scale, back * vec_all[0:1, :])
    vec_out[0:1, :] = row_sum(back * unit)
    vec_out[1:2, :] = row_sum(back)
    vec_out[4:5, :] = vec_second[2:3, :]
    vec_out[5:7, :] = vec_second[0:2, :]
    vec_out[7:12, :] = vec_first[0:5, :]
    wide = windows[0].shape[1]
    spread_terms(place, dqkv, rows, 0, windows, wide)
    packed[...] = jnp.zeros_like(packed)
    for at, lanes, row, source in vector_tiles(wide):
        packed[at : at + 1, lanes] = vec_out[row : row + 1, source]
    for window in windows:
        window[dqkv.shape[0] :, :] = packed[...].astype(jnp.bfloat16)


def vector_tiles(wide):
    across, packed = D // 128, wide // 128
    for index in range(12 * across):
        at, to = divmod(index, packed)
        row, source = divmod(index, across)
        yield at, slice(to * 128, to * 128 + 128), row, slice(source * 128, source * 128 + 128)


def product_kernel(rows, wide, lane, starts, split, which, place, *rest):
    last = split is None and starts is None
    terms, columns, rest = rest[:4], rest[4:-6], rest[-6:]
    away, mine, left, right, whole, sums = rest
    if last:
        vec_all, columns = columns[0], columns[1:]
    count = columns[0].shape[0]
    for index in range(4):
        left[index * count : (index + 1) * count] = terms[index][:count, lane : lane + wide]
    core, across, high = place[4], place[5], place[6]

    def column(index):
        value = columns[index]
        if last and index > 0:
            unit, _ = norm_parts(value[:, :D].astype(jnp.float32))
            return (unit * vec_all[0:1, :] + vec_all[1:2, :]).astype(jnp.bfloat16)
        start = 0 if last else starts[index]
        return value[:, start : start + D]

    def put(span, other):
        for index in range(4):
            value = column(index)
            if other is not None:
                value = jnp.where(other, column(4 + index), value)
            right[index * count : (index + 1) * count] = value
        whole[span, :] = dot(left[:, span], right[...], 0, 0).astype(jnp.bfloat16)

    if split is None:
        put(slice(0, wide), None)
    else:
        start = rows - wide
        chosen = core == which
        if split <= start:
            put(slice(0, split), chosen & (across == 1))
            put(slice(split, wide), chosen)
        else:
            put(slice(0, split - start), chosen)
            put(slice(split - start, wide), chosen & (across == 0))
    part = rows // 4
    first = across * (wide - rows // 2)
    away[:part] = whole[pl.ds(pl.multiple_of(first + (1 - high) * part, 16), part), :]
    mine[:part] = whole[pl.ds(pl.multiple_of(first + high * part, 16), part), :]
    if last:
        total = terms[0][count:, :].astype(jnp.float32)
        for index in range(1, 4):
            total = total + terms[index][count:, :].astype(jnp.float32)
        sums[...] = jnp.zeros_like(sums)
        for at, lanes, row, source in vector_tiles(wide):
            sums[row : row + 1, source] = total[at : at + 1, lanes]
        away[part:] = sums[...].astype(jnp.bfloat16)
        mine[part:] = sums[...].astype(jnp.bfloat16)


any_spec = pl.BlockSpec(memory_space=pl.ANY)
vmem_spec = pl.BlockSpec(memory_space=pltpu.VMEM)
smem_spec = pl.BlockSpec(memory_space=pltpu.SMEM)
bf16, f32 = jnp.bfloat16, jnp.float32


def grant(inputs, outputs, scratch):
    arrays = [value for value, spec in inputs if spec is vmem_spec]
    arrays += [jax.ShapeDtypeStruct(shape, kind) for shape, kind, spec in outputs]
    need = 2 * sum(value.size * value.dtype.itemsize for value in arrays)
    for item in scratch:
        if hasattr(item, "shape") and item.dtype in (bf16, f32):
            need += math.prod(item.shape) * jnp.dtype(item.dtype).itemsize
    return need + 6 * 1024 * 1024


def call(kernel, inputs, outputs, scratch, flops, moved):
    return pl.pallas_call(
        kernel,
        grid=(1,),
        in_specs=[spec for _, spec in inputs],
        out_specs=[spec for _, _, spec in outputs],
        out_shape=[jax.ShapeDtypeStruct(shape, kind) for shape, kind, _ in outputs],
        scratch_shapes=scratch,
        compiler_params=pltpu.CompilerParams(vmem_limit_bytes=grant(inputs, outputs, scratch)),
        cost_estimate=pl.CostEstimate(flops=flops, bytes_accessed=moved, transcendentals=0),
    )(*[value for value, _ in inputs])


def after(kernel, inputs, waits):
    count, extra = len(inputs), len(waits)

    def body(*refs):
        kernel(*refs[:count], *refs[count + extra :])

    return body, inputs + [(value, any_spec) for value in waits]


def parameter_blocks(links, weights, vectors):
    shards = links.chips * links.cores
    width = vectors.shape[1]
    number = links.chip * links.cores + links.core
    location = lax.broadcasted_iota(jnp.int32, (vectors.shape[0], width * shards), 1) // width
    spread = jnp.where(location == number, jnp.tile(vectors, (1, shards)), 0.0)
    spread = jnp.pad(spread, ((0, vector_pad - vectors.shape[0]), (0, 0))).astype(bf16)
    first, second = links.own_pieces(weights)
    size = first.shape[0]
    mine = jnp.concatenate([first.astype(bf16), second.astype(bf16), spread])
    inner = (links.chip == 1) | (links.chip == 2)
    near = links.along(mine, {0: 1, 1: 0, 2: 3, 3: 2})
    middle = links.along(mine, {1: 2, 2: 1})
    across = links.along(near, {1: 2, 2: 1})
    outward = links.along(middle, {1: 0, 2: 3})
    far = links.along(across, {1: 0, 2: 3})
    block = weights.astype(bf16)
    blocks = [block, links.swap_core(block)]
    slots = (near, jnp.where(inner, middle, outward), jnp.where(inner, across, far))
    total = spread
    for slot in slots:
        total = total + slot[2 * size :]
        for piece in links.gather_pieces(slot[:size], slot[size : 2 * size]):
            blocks += [piece, links.swap_core(piece)]
    total = total + links.swap_core(total)
    return blocks, total.astype(f32)


def direct_step(links, tokens, segments, cotangent, state, vectors):
    count = tokens.shape[0]
    weights = state[0]
    rows = weights.shape[0]
    wide = -(-rows // 256) * 128
    blocks, vec_all = parameter_blocks(links, weights, vectors)
    low = links.chip < links.chips // 2
    place = jnp.stack(
        [
            links.chip,
            links.chip ^ 1,
            jnp.where(low, 2, 1),
            jnp.where(low, 3, 0),
            links.core,
            links.bit_of(0),
            links.bit_of(1),
            links.bit_of(links.bits - 1),
        ]
    ).astype(jnp.int32)
    ends = [(place, smem_spec)]
    pairs = segments.shape[0] * HEADS
    length = segments.shape[1]
    unit_cost = 2 * count * HID * D
    parameters = [(block, any_spec) for block in blocks]

    def full(*arrays):
        return [(array, vmem_spec) for array in arrays]

    def shape(width, kind=bf16, height=count):
        return (height, width), kind, vmem_spec

    def weight_scratch(chips):
        return [pltpu.VMEM((chips * 2 * rows, D), bf16)]

    def weight_sem(chips):
        return [pltpu.SemaphoreType.DMA((chips * 2,))]

    def share_rows(parts):
        own, to_core, to_side, to_both = parts
        side = links.swap_bit(to_side, 0)
        both = links.swap_both(to_both, 0)
        other = links.swap_core(to_core)
        return [own, other, side, both]

    joined = jnp.concatenate([tokens, cotangent], axis=1)
    joined_side = links.swap_bit(joined, 0)
    joined_core = links.swap_core(joined)
    joined_both = links.swap_core(joined_side)
    joined_all = [joined, joined_core, joined_side, joined_both]
    column = segments.reshape(count, 1)
    n_one, qkv, probs, att = call(
        functools.partial(query_kernel, rows),
        ends + full(tokens, column, segments, vec_all) + parameters,
        [
            shape(D),
            shape(3 * HID),
            ((pairs, length, length), f32, vmem_spec),
            shape(HID),
        ],
        weight_scratch(1) + weight_sem(1),
        4 * unit_cost,
        6 * HID * D,
    )
    active_out = call(
        functools.partial(active_kernel, rows),
        ends + full(tokens, att, vec_all) + parameters,
        [shape(D), shape(D, f32), shape(FF), shape(FF, f32)]
        + [shape(wide), shape(wide + D), shape(wide + D), shape(wide)],
        weight_scratch(2) + weight_sem(2),
        5 * unit_cost,
        8 * rows * D,
    )
    n_two, hidden, act, slope = active_out[:4]
    rows_three = share_rows(active_out[4:])
    n_two_both = links.swap_core(rows_three[2])
    n_two_all = [n_two, rows_three[1], rows_three[2], n_two_both]
    n_two_starts = [0, wide, wide, wide]
    change_out = call(
        functools.partial(change_kernel, rows),
        ends + full(cotangent, att, act, slope, hidden, vec_all) + parameters,
        [shape(D), shape(FF), shape(D, f32, 8)] + [shape(wide)] * 8,
        weight_scratch(2) + [pltpu.VMEM((count, HID + 2 * FF), bf16)] + weight_sem(2),
        8 * unit_cost,
        8 * rows * D,
    )
    out, dub, vec_first = change_out[:3]
    rows_two = share_rows(change_out[3:7])
    rows_one = share_rows(change_out[7:])

    def product(parts, columns, lane, starts, split=None, which=0, waits=()):
        extra = 0 if starts is not None else vector_pad
        kernel, inputs = after(
            functools.partial(product_kernel, rows, wide, lane, starts, split, which),
            ends + full(*parts) + full(*columns),
            list(waits),
        )
        return call(
            kernel,
            inputs,
            [shape(D, bf16, rows // 4 + extra)] * 2,
            [
                pltpu.VMEM((4 * count, wide), bf16),
                pltpu.VMEM((4 * count, D), bf16),
                pltpu.VMEM((wide, D), bf16),
                pltpu.VMEM((vector_pad, D), f32),
            ],
            8 * count * wide * D,
            4 * rows * D,
        )

    def scatter_rest(parts):
        away, mine = parts
        got = links.swap_bit(away, 1)
        mine = add_bf(mine, got)
        part = rows // 4
        mine, rest = mine[:part], mine[part:]
        for bit in range(2, links.bits):
            size = mine.shape[0] // 2
            away = lax.dynamic_slice_in_dim(mine, (1 - links.bit_of(bit)) * size, size)
            near = lax.dynamic_slice_in_dim(mine, links.bit_of(bit) * size, size)
            mine = add_bf(near, links.swap_bit(away, bit))
            if rest.shape[0]:
                rest = add_bf(rest, links.swap_bit(rest, bit))
        return jnp.concatenate([mine, rest]) if rest.shape[0] else mine

    product_three = product(rows_three, joined_all, 0, [D] * 4)
    three = scatter_rest(product_three)
    kernel, inputs = after(
        functools.partial(hidden_kernel, rows),
        ends + full(dub, hidden, cotangent, vec_all) + parameters,
        product_three[:1],
    )
    dh, dh_bf, da, vec_second = call(
        kernel,
        inputs,
        [shape(D, f32), shape(D), shape(HID), shape(D, f32, 8)],
        weight_scratch(2) + weight_sem(2),
        5 * unit_cost,
        8 * rows * D,
    )
    dh_side = links.swap_bit(dh_bf, 0)
    dh_core = links.swap_core(dh_bf)
    product_two = product(
        rows_two,
        n_two_all + joined_all,
        0,
        n_two_starts + [D] * 4,
        4 * HID + FF - 5 * rows,
        1,
        waits=[vec_second],
    )
    two = scatter_rest(product_two)
    three, _ = lax.optimization_barrier((three, product_two[1]))
    three = links.to_chip(three, {0: 1, 2: 3})
    kernel, inputs = after(
        functools.partial(attention_kernel, rows),
        ends + full(da, qkv, probs, dh, tokens, vec_all, vec_first, vec_second) + parameters,
        product_two[:1],
    )
    attention_out = call(
        kernel,
        inputs,
        [shape(D, f32)] + [shape(wide, bf16, count + vector_pad)] * 4,
        weight_scratch(1)
        + [
            pltpu.VMEM((count, 3 * HID), bf16),
            pltpu.VMEM((vector_pad, D), f32),
            pltpu.VMEM((vector_pad, wide), f32),
        ]
        + weight_sem(1),
        4 * unit_cost,
        4 * rows * D,
    )
    grad_tok = attention_out[0]
    rows_zero = share_rows(attention_out[1:])
    two, dh_side, _ = lax.optimization_barrier((two, dh_side, grad_tok))
    dh_both = links.swap_core(dh_side)
    dh_all = [dh_bf, dh_core, dh_side, dh_both]
    two = links.to_chip(two, {0: 1, 3: 2})
    product_one = product(
        rows_one,
        n_two_all + dh_all,
        0,
        n_two_starts + [0] * 4,
        4 * HID - 2 * rows,
        0,
        waits=[grad_tok],
    )
    one = scatter_rest(product_one)
    product_zero = product(
        rows_zero, [vec_all, n_one] + joined_all[1:], 0, None, waits=product_one[:1]
    )
    zero = scatter_rest(product_zero)
    three = links.to_chip(three, {1: 3})
    two = links.to_chip(two, {1: 2})
    one = links.to_chip(one, {0: 1, 3: 2})
    one = links.to_chip(one, {2: 1})
    zero = links.to_chip(zero, {0: 1, 1: 0, 2: 3, 3: 2})
    zero = links.to_chip(zero, {0: 2, 2: 0})
    mine = jnp.where(links.chip == 1, one, jnp.where(links.chip == 2, two, three))
    size = mine.shape[0]
    mine = jnp.where(links.chip == 0, zero[:size], mine)
    grad_w = links.gather_positions(mine).astype(f32)
    sums = zero[size:]
    got = links.along(sums, {0: 1, 2: 3})
    sums = jnp.where(links.chip % 2 == 0, sums, got).astype(f32)
    width = vectors.shape[1]
    grad_v = lax.dynamic_slice_in_dim(sums, lax.axis_index("shard") * width, width, 1)
    new = [grad_w] + list(adam_update(*state, grad_w, decay_rate))
    return out, grad_tok, grad_v[: vectors.shape[0]], new


def per_device(
    replicas,
    shards,
    tokens,
    segments,
    cotangent,
    weights,
    vectors,
    first_weights,
    first_vectors,
    second_weights,
    second_vectors,
):
    if Links.fits(replicas, shards, weights.shape[0]):
        output, grad_tokens, grad_v, new = direct_step(
            Links(replicas, shards),
            tokens,
            segments,
            cotangent,
            (weights, first_weights, second_weights),
            vectors,
        )
    else:
        w_full = lax.all_gather(weights.astype(jnp.bfloat16), "shard", axis=0, tiled=True)
        v_full = lax.all_gather(vectors.astype(jnp.bfloat16), "shard", axis=1, tiled=True)
        output, kept_state = forward(tokens, segments, w_full, v_full)
        grad_tokens, grad_vec, row_terms, col_terms = backward(
            kept_state, cotangent, segments, w_full
        )
        local_grad = weight_grads(row_terms, col_terms).astype(jnp.bfloat16)
        own_w = lax.psum_scatter(local_grad, "shard", scatter_dimension=0, tiled=True)
        own_v = lax.psum_scatter(
            grad_vec.astype(jnp.bfloat16), "shard", scatter_dimension=1, tiled=True
        )
        grad_w = lax.psum(own_w, "rep").astype(jnp.float32)
        grad_v = lax.psum(own_v, "rep").astype(jnp.float32)
        new = [grad_w]
        new += adam_update(weights, first_weights, second_weights, grad_w, decay_rate)
    grad_w, new_w, new_fw, new_sw = new
    new_v, new_fv, new_sv = adam_update(vectors, first_vectors, second_vectors, grad_v, 0.0)
    return (output, grad_tokens, grad_w, grad_v, new_w, new_v, new_fw, new_fv, new_sw, new_sv)


def solution(mesh):
    placed = (
        P(("rep", "shard"), None),
        P(("rep", "shard"), None),
        P(("rep", "shard"), None),
        P("shard", None),
        P(None, "shard"),
        P("shard", None),
        P(None, "shard"),
        P("shard", None),
        P(None, "shard"),
    )
    return jax.shard_map(
        functools.partial(per_device, mesh.shape["rep"], mesh.shape["shard"]),
        mesh=mesh,
        in_specs=placed,
        out_specs=(
            P(("rep", "shard"), None),
            P(("rep", "shard"), None),
            P("shard", None),
            P(None, "shard"),
            P("shard", None),
            P(None, "shard"),
            P("shard", None),
            P(None, "shard"),
            P("shard", None),
            P(None, "shard"),
        ),
        check_vma=False,
    )
```

```python
import functools
import math

import jax
import jax.numpy as jnp
from jax import lax
from jax.experimental import pallas as pl
from jax.experimental.pallas import tpu as pltpu
from jax.sharding import PartitionSpec as P

D = 768
HEADS = 12
HEAD = 64
FF = 3072
STEP = 3
HID = 768
R = 9216


norm_eps = 1e-05
beta_one = 0.9
beta_two = 0.999
adam_eps = 1e-08
learn_rate = 0.2
decay_rate = 0.1
masked_score = -1e30


def normalize(values):
    centred = values - jnp.mean(values, axis=-1, keepdims=True)
    return centred * lax.rsqrt(jnp.mean(centred * centred, axis=-1, keepdims=True) + norm_eps)


def affine_norm(values, gain_vec, shift_vec):
    return normalize(values) * gain_vec + shift_vec


def gelu_tanh(values):
    return jax.nn.gelu(values, approximate=True)


def matmul(left_op, right_op):
    return jnp.dot(left_op, right_op, preferred_element_type=jnp.float32)


def matmul_nt(left_op, right_op):
    return lax.dot_general(
        left_op, right_op, (((1,), (1,)), ((), ())), preferred_element_type=jnp.float32
    )


def matmul_tn(left_op, right_op):
    return lax.dot_general(
        left_op, right_op, (((0,), (0,)), ((), ())), preferred_element_type=jnp.float32
    )


def product(pattern, left_op, right_op):
    return jnp.einsum(pattern, left_op, right_op, preferred_element_type=jnp.float32)


def allowed_pairs(segments):
    length = segments.shape[1]
    places = lax.broadcasted_iota(jnp.int32, (length, length), 0)
    others = lax.broadcasted_iota(jnp.int32, (length, length), 1)
    causal = others <= places
    same_doc = segments[:, :, None] == segments[:, None, :]
    return (causal[None] & same_doc)[:, None]


def scores_of(query_rows, key_rows, allowed):
    raw_scores = product("sqhd,skhd->shqk", query_rows, key_rows) * HEAD ** (-0.5)
    return jnp.where(allowed, raw_scores, masked_score)


def forward(tokens, segments, w_bf, v_bf):
    seq_count, length = segments.shape
    tok_count = tokens.shape[0]
    head_shape = (seq_count, length, HEADS, HEAD)
    floats = v_bf.astype(jnp.float32)
    residual = tokens.astype(jnp.float32)
    normed_one = affine_norm(residual, floats[0], floats[1]).astype(jnp.bfloat16)
    projected = matmul_nt(normed_one, w_bf[: 3 * HID])
    query_rows = (projected[:, :HID] + floats[2]).astype(jnp.bfloat16)
    key_rows = projected[:, HID : 2 * HID].astype(jnp.bfloat16)
    value_rows = (projected[:, 2 * HID :] + floats[3]).astype(jnp.bfloat16)
    allowed = allowed_pairs(segments)
    scores = scores_of(query_rows.reshape(head_shape), key_rows.reshape(head_shape), allowed)
    row_max = jnp.max(scores, axis=-1, keepdims=True)
    log_total = row_max + jnp.log(jnp.sum(jnp.exp(scores - row_max), axis=-1, keepdims=True))
    attn_probs = jnp.exp(scores - log_total).astype(jnp.bfloat16)
    mixed_heads = product("shqk,skhd->sqhd", attn_probs, value_rows.reshape(head_shape))
    attended = mixed_heads.reshape(tok_count, HID).astype(jnp.bfloat16)
    hidden_one = residual + matmul(attended, w_bf[3 * HID : 4 * HID]) + floats[4]
    normed_two = affine_norm(hidden_one, floats[5], floats[6]).astype(jnp.bfloat16)
    pre_act = matmul_nt(normed_two, w_bf[4 * HID : 4 * HID + FF]) + floats[7:11].reshape(FF)
    active = gelu_tanh(pre_act).astype(jnp.bfloat16)
    output = (hidden_one + matmul(active, w_bf[4 * HID + FF :]) + floats[11]).astype(jnp.bfloat16)
    kept_state = (
        residual,
        normed_one,
        query_rows,
        key_rows,
        value_rows,
        log_total,
        attended,
        hidden_one,
        normed_two,
        pre_act,
        active,
        floats,
    )
    return (output, kept_state)


def backward(kept_state, cotangent, segments, w_bf):
    (
        residual,
        normed_one,
        query_rows,
        key_rows,
        value_rows,
        log_total,
        attended,
        hidden_one,
        normed_two,
        pre_act,
        active,
        floats,
    ) = kept_state
    seq_count, length = segments.shape
    tok_count = residual.shape[0]
    head_shape = (seq_count, length, HEADS, HEAD)
    grad_out = cotangent.astype(jnp.float32)
    grad_active = matmul_nt(cotangent, w_bf[4 * HID + FF :])
    grad_pre = jax.vjp(gelu_tanh, pre_act)[1](grad_active)[0]
    grad_pre_bf = grad_pre.astype(jnp.bfloat16)
    grad_normed_two = matmul(grad_pre_bf, w_bf[4 * HID : 4 * HID + FF])
    norm_back_two = jax.vjp(affine_norm, hidden_one, floats[5], floats[6])[1]
    grad_h_part, grad_gain_two, grad_shift_two = norm_back_two(grad_normed_two)
    grad_hidden = grad_out + grad_h_part
    grad_hidden_bf = grad_hidden.astype(jnp.bfloat16)
    grad_attended = matmul_nt(grad_hidden_bf, w_bf[3 * HID : 4 * HID]).astype(jnp.bfloat16)
    query_four = query_rows.reshape(head_shape)
    key_four = key_rows.reshape(head_shape)
    value_four = value_rows.reshape(head_shape)
    grad_att_four = grad_attended.reshape(head_shape)
    allowed = allowed_pairs(segments)
    scores = scores_of(query_four, key_four, allowed)
    attn_probs = jnp.exp(scores - log_total)
    probs_bf = attn_probs.astype(jnp.bfloat16)
    grad_probs = product("sqhd,skhd->shqk", grad_att_four, value_four)
    inner_sum = jnp.sum(attn_probs * grad_probs, axis=-1, keepdims=True)
    grad_scores = (attn_probs * (grad_probs - inner_sum) * HEAD ** (-0.5)).astype(jnp.bfloat16)
    grad_query = product("shqk,skhd->sqhd", grad_scores, key_four).reshape(tok_count, HID)
    grad_keys = product("shqk,sqhd->skhd", grad_scores, query_four).reshape(tok_count, HID)
    grad_values = product("shqk,sqhd->skhd", probs_bf, grad_att_four).reshape(tok_count, HID)
    grad_proj = jnp.concatenate([grad_query, grad_keys, grad_values], axis=1)
    grad_proj_bf = grad_proj.astype(jnp.bfloat16)
    grad_normed_one = matmul(grad_proj_bf, w_bf[: 3 * HID])
    norm_back_one = jax.vjp(affine_norm, residual, floats[0], floats[1])[1]
    grad_r_part, grad_gain_one, grad_shift_one = norm_back_one(grad_normed_one)
    grad_tokens = grad_hidden + grad_r_part
    bias_ff = jnp.sum(grad_pre, axis=0).reshape(FF // D, D)
    head_rows = jnp.stack(
        [
            grad_gain_one,
            grad_shift_one,
            jnp.sum(grad_query, axis=0),
            jnp.sum(grad_values, axis=0),
            jnp.sum(grad_hidden, axis=0),
            grad_gain_two,
            grad_shift_two,
        ]
    )
    grad_vec = jnp.concatenate([head_rows, bias_ff, jnp.sum(grad_out, axis=0)[None]], axis=0)
    row_terms = jnp.concatenate([grad_proj_bf, attended, grad_pre_bf, active], axis=1)
    col_terms = jnp.stack([normed_one, grad_hidden_bf, normed_two, cotangent])
    return (grad_tokens, grad_vec, row_terms, col_terms)


def weight_grads(row_terms, col_terms):
    row_bounds = (0, 3 * HID, 4 * HID, 4 * HID + FF, R)
    pieces = [
        matmul_tn(row_terms[:, row_bounds[index] : row_bounds[index + 1]], col_terms[index])
        for index in range(4)
    ]
    return jnp.concatenate(pieces, axis=0)


def adam_update(param, first, second, grad, decay):
    new_first = beta_one * first + (1.0 - beta_one) * grad
    new_second = beta_two * second + (1.0 - beta_two) * grad * grad
    first_hat = new_first / (1.0 - beta_one**STEP)
    second_hat = new_second / (1.0 - beta_two**STEP)
    new_param = param - learn_rate * (first_hat / (jnp.sqrt(second_hat) + adam_eps) + decay * param)
    return (new_param, new_first, new_second)


def bit_reverse(index, bits):
    out = index * 0
    for place in range(bits):
        out = out * 2 + (index >> place) % 2
    return out


class Links:
    def __init__(self, replicas, shards):
        self.replicas = replicas
        self.cores = 2
        self.chips = shards // self.cores
        self.bits = replicas.bit_length() - 1
        self.replica = lax.axis_index("rep")
        shard = lax.axis_index("shard")
        self.chip = shard // self.cores
        self.core = shard % self.cores

    @staticmethod
    def fits(replicas, shards, rows):
        power = replicas > 2 and replicas & (replicas - 1) == 0
        return shards == 8 and power and 2 * rows == 3 * HID

    def send(self, value, target):
        route = []
        for rep in range(self.replicas):
            for chip in range(self.chips):
                for core in range(self.cores):
                    goal = target(rep, chip, core)
                    if goal is None:
                        continue
                    start = (rep * self.chips + chip) * self.cores + core
                    stop = (goal[0] * self.chips + goal[1]) * self.cores + goal[2]
                    route.append((start, stop))
        return lax.ppermute(value, ("rep", "shard"), route)

    def swap_core(self, value):
        return self.send(value, lambda rep, chip, core: (rep, chip, 1 - core))

    def swap_both(self, value, bit):
        return self.send(value, lambda rep, chip, core: (rep ^ (1 << bit), chip, 1 - core))

    def swap_bit(self, value, bit):
        return self.send(value, lambda rep, chip, core: (rep ^ (1 << bit), chip, core))

    def along(self, value, moves):
        table = dict(moves)
        return self.send(
            value, lambda rep, chip, core: (rep, table[chip], core) if chip in table else None
        )

    def bit_of(self, bit):
        return (self.replica >> bit) % 2

    def own_pieces(self, block):
        half = block.shape[0] // 2
        size = half // self.replicas
        first = lax.dynamic_slice_in_dim(block, self.replica * size, size)
        turned = bit_reverse(self.replica, self.bits)
        second = lax.dynamic_slice_in_dim(block, half + turned * size, size)
        return first, second

    def gather_pieces(self, first, second):
        for step in range(self.bits):
            low, high = step, self.bits - 1 - step
            got_first = self.swap_bit(first, low)
            got_second = self.swap_bit(second, high)
            if step == self.bits - 1:
                return [first, got_first, second, got_second]
            first = jnp.where(
                self.bit_of(low) == 0,
                jnp.concatenate([first, got_first]),
                jnp.concatenate([got_first, first]),
            )
            second = jnp.where(
                self.bit_of(high) == 0,
                jnp.concatenate([second, got_second]),
                jnp.concatenate([got_second, second]),
            )

    def gather_positions(self, piece):
        size = piece.shape[0] // 2
        first, second = piece[:size], piece[size:]
        for step in range(self.bits):
            high, low = self.bits - 1 - step, step
            got_first = self.swap_bit(first, high)
            got_second = self.swap_bit(second, low)
            first = jnp.where(
                self.bit_of(high) == 0,
                jnp.concatenate([first, got_first]),
                jnp.concatenate([got_first, first]),
            )
            second = jnp.where(
                self.bit_of(low) == 0,
                jnp.concatenate([second, got_second]),
                jnp.concatenate([got_second, second]),
            )
        parts = []
        for position in range(self.replicas):
            turned = bit_reverse(position, self.bits)
            parts.append(first[position * size : (position + 1) * size])
            parts.append(second[turned * size : (turned + 1) * size])
        return jnp.concatenate(parts)

    def to_chip(self, piece, moves):
        got = self.along(piece, moves)
        return add_bf(piece, got)


def add_bf(left, right):
    return (left.astype(jnp.float32) + right.astype(jnp.float32)).astype(jnp.bfloat16)


vector_pad = 16


def dot(left, right, left_dim, right_dim):
    return lax.dot_general(
        left,
        right,
        (((left_dim,), (right_dim,)), ((), ())),
        preferred_element_type=jnp.float32,
    )


def norm_parts(values):
    centred = values - jnp.mean(values, axis=-1, keepdims=True)
    scale = lax.rsqrt(jnp.mean(centred * centred, axis=-1, keepdims=True) + norm_eps)
    return centred * scale, scale


def norm_back(unit, scale, grad):
    inner = jnp.mean(grad, axis=-1, keepdims=True)
    outer = jnp.mean(grad * unit, axis=-1, keepdims=True)
    return scale * (grad - inner - unit * outer)


def row_sum(values):
    return jnp.sum(values, axis=0, keepdims=True)


def left_lanes(value):
    return lax.broadcasted_iota(jnp.int32, value.shape, 1) < HEAD


def head_parts(pair):
    left = left_lanes(pair)
    none = jnp.zeros_like(pair)
    return jnp.where(left, pair, none), jnp.where(left, none, pair)


def load_blocks(place, blocks, rows, target, sem, first, last):
    quarter = rows // 4
    starts = (
        place[7] * quarter,
        (1 - place[7]) * quarter,
        (2 + place[5]) * quarter,
        (3 - place[5]) * quarter,
    )
    for slot in range(4):
        chip = place[slot]

        @pl.when((chip >= first) & (chip < last))
        def _():
            for side in range(2):
                core = place[4] if side == 0 else 1 - place[4]
                number = (chip - first) * 2 + core
                if slot == 0:
                    parts = [(blocks[side], 0, rows)]
                else:
                    at = 2 + (slot - 1) * 8 + side
                    parts = [
                        (blocks[at + 2 * index], starts[index], quarter) for index in range(4)
                    ]
                for ref, shift, size in parts:
                    start = pl.multiple_of(number * rows + shift, 16)
                    pltpu.make_async_copy(ref, target.at[pl.ds(start, size)], sem.at[number]).start()

    done = set()

    def ready(low, high):
        for number in range(low // rows, -(-high // rows)):
            if number in done:
                continue
            done.add(number)
            index = number - 2 * first
            pltpu.make_async_copy(
                blocks[0], target.at[pl.ds(index * rows, rows)], sem.at[index]
            ).wait()

    return ready


block_count = 26


def spread_terms(place, terms, rows, first, outs, wide, lane=0):
    core, across = place[4], place[5]
    count = terms.shape[0]
    for index, out in enumerate(outs):
        block = core if index % 2 == 0 else 1 - core
        side = across if index < 2 else 1 - across
        start = pl.multiple_of(first + block * rows + side * (rows - wide), 128)
        out[:count, lane : lane + wide] = terms[:, pl.ds(start, wide)]


def query_kernel(rows, place, tok, seg_col, seg_row, vec_all, *rest):
    blocks = rest[:block_count]
    n_out, qkv, probs, att, w_in, load_sem = rest[block_count:]
    ready = load_blocks(place, blocks, rows, w_in, load_sem, 0, 1)
    unit, _ = norm_parts(tok[...].astype(jnp.float32))
    n_one = (unit * vec_all[0:1, :] + vec_all[1:2, :]).astype(jnp.bfloat16)
    n_out[...] = n_one
    for index, bias in enumerate((vec_all[2:3, :], None, vec_all[3:4, :])):
        ready(index * HID, (index + 1) * HID)
        value = dot(n_one, w_in[index * HID : (index + 1) * HID], 1, 1)
        if bias is not None:
            value = value + bias
        qkv[:, index * HID : (index + 1) * HID] = value.astype(jnp.bfloat16)
    length = seg_row.shape[1]
    for seq in range(seg_row.shape[0]):
        span = slice(seq * length, (seq + 1) * length)
        order = lax.broadcasted_iota(jnp.int32, (length, length), 0)
        other = lax.broadcasted_iota(jnp.int32, (length, length), 1)
        allowed = (other <= order) & (seg_col[span, :] == seg_row[seq : seq + 1, :])
        for pair in range(HEADS // 2):
            lanes = slice(pair * 2 * HEAD, (pair + 1) * 2 * HEAD)
            key_pair = qkv[span, HID + lanes.start : HID + lanes.stop]
            value_pair = qkv[span, 2 * HID + lanes.start : 2 * HID + lanes.stop]
            mixed = []
            for half, query in enumerate(head_parts(qkv[span, lanes])):
                raw = dot(query, key_pair, 1, 1) * HEAD ** (-0.5)
                raw = jnp.where(allowed, raw, masked_score)
                top = jnp.max(raw, axis=-1, keepdims=True)
                power = jnp.exp(raw - top)
                prob = power * (1.0 / jnp.sum(power, axis=-1, keepdims=True))
                probs[seq * HEADS + 2 * pair + half] = prob
                mixed.append(dot(prob.astype(jnp.bfloat16), value_pair, 1, 0))
            att[span, lanes] = jnp.where(left_lanes(mixed[0]), mixed[0], mixed[1]).astype(
                jnp.bfloat16
            )


def active_kernel(rows, place, tok, att, vec_all, *rest):
    blocks = rest[:block_count]
    n_out, hidden, act, slope_out = rest[block_count : block_count + 4]
    windows = rest[block_count + 4 : block_count + 8]
    w_mid, load_sem = rest[block_count + 8 :]
    ready = load_blocks(place, blocks, rows, w_mid, load_sem, 1, 3)
    base = 2 * rows

    def weight(first, size):
        ready(first, first + size)
        return w_mid[first - base : first - base + size]

    h_value = tok[...].astype(jnp.float32) + dot(att[...], weight(3 * HID, HID), 1, 0)
    h_value = h_value + vec_all[4:5, :]
    hidden[...] = h_value
    unit, _ = norm_parts(h_value)
    n_two = (unit * vec_all[5:6, :] + vec_all[6:7, :]).astype(jnp.bfloat16)
    n_out[...] = n_two
    root = math.sqrt(2.0 / math.pi)
    for index in range(FF // D):
        span = slice(index * D, (index + 1) * D)
        pre = dot(n_two, weight(4 * HID + index * D, D), 1, 1) + vec_all[7 + index : 8 + index, :]
        squared = pre * pre
        bent = jnp.tanh(root * (pre + 0.044715 * (pre * squared)))
        half = 0.5 * (1.0 + bent)
        act[:, span] = (pre * half).astype(jnp.bfloat16)
        slope_out[:, span] = half + 0.5 * pre * (1.0 - bent * bent) * (
            root * (1.0 + 3 * 0.044715 * squared)
        )
    wide = windows[0].shape[1]
    spread_terms(place, act, rows, 6 * rows - (4 * HID + FF), windows, wide)
    windows[1][:, wide:] = n_two
    windows[2][:, wide:] = n_two
    ready(2 * rows, 6 * rows)


def change_kernel(rows, place, cot, att, act, slope, hidden, vec_all, *rest):
    blocks = rest[:block_count]
    rest = rest[block_count:]
    out, dub, vec_out = rest[:3]
    windows = rest[3:7]
    w_top, terms, load_sem = rest[7:]
    ready = load_blocks(place, blocks, rows, w_top, load_sem, 2, 4)
    base = 4 * rows
    terms[:, :HID] = att[...]
    result = hidden[...] + vec_all[11:12, :]
    for index in range(FF // D):
        span = slice(index * D, (index + 1) * D)
        first = 4 * HID + FF + index * D - base
        ready(first + base, first + base + D)
        weight = w_top[first : first + D]
        active = act[:, span]
        change = dot(cot[...], weight, 1, 1) * slope[:, span]
        change_bf = change.astype(jnp.bfloat16)
        dub[:, span] = change_bf
        terms[:, HID + index * D : HID + (index + 1) * D] = change_bf
        terms[:, HID + FF + index * D : HID + FF + (index + 1) * D] = active
        vec_out[index : index + 1, :] = row_sum(change)
        result = result + dot(active, weight, 1, 0)
    wide = windows[0].shape[1] // 2
    spread_terms(place, terms, rows, 2 * rows, windows, wide)
    spread_terms(place, terms, rows, 0, windows, wide, wide)
    out[...] = result.astype(jnp.bfloat16)
    vec_out[4:5, :] = row_sum(cot[...].astype(jnp.float32))
    vec_out[5:8, :] = jnp.zeros((3, D), jnp.float32)
    ready(4 * rows, 8 * rows)


def hidden_kernel(rows, place, dub, hidden, cot, vec_all, *rest):
    blocks = rest[:block_count]
    dh, dh_bf, da, vec_out, w_mid, load_sem = rest[block_count:]
    ready = load_blocks(place, blocks, rows, w_mid, load_sem, 1, 3)
    base = 2 * rows
    unit, scale = norm_parts(hidden[...])
    start = 4 * HID
    back = None
    while start < 4 * HID + FF:
        stop = min((start // rows + 1) * rows, 4 * HID + FF)
        ready(start, stop)
        part = dot(dub[:, start - 4 * HID : stop - 4 * HID], w_mid[start - base : stop - base], 1, 0)
        back = part if back is None else back + part
        start = stop
    vec_out[0:1, :] = row_sum(back * unit)
    vec_out[1:2, :] = row_sum(back)
    value = cot[...].astype(jnp.float32) + norm_back(unit, scale, back * vec_all[5:6, :])
    dh[...] = value
    vec_out[2:3, :] = row_sum(value)
    vec_out[3:8, :] = jnp.zeros((5, D), jnp.float32)
    rounded = value.astype(jnp.bfloat16)
    dh_bf[...] = rounded
    da[...] = dot(rounded, w_mid[3 * HID - base : 4 * HID - base], 1, 1).astype(jnp.bfloat16)


def attention_kernel(rows, place, da, qkv, probs, dh, tok, vec_all, vec_first, vec_second, *rest):
    blocks = rest[:block_count]
    rest = rest[block_count:]
    grad_tok = rest[0]
    windows = rest[1:5]
    w_in, dqkv, vec_out, packed, load_sem = rest[5:]
    ready = load_blocks(place, blocks, rows, w_in, load_sem, 0, 1)
    heads_total = probs.shape[0]
    length = probs.shape[1]
    vec_out[2:4, :] = jnp.zeros((2, D), jnp.float32)
    for seq in range(heads_total // HEADS):
        span = slice(seq * length, (seq + 1) * length)
        for pair in range(HEADS // 2):
            lanes = slice(pair * 2 * HEAD, (pair + 1) * 2 * HEAD)
            query_pair = qkv[span, lanes]
            key_pair = qkv[span, HID + lanes.start : HID + lanes.stop]
            value_pair = qkv[span, 2 * HID + lanes.start : 2 * HID + lanes.stop]
            da_pair = da[span, lanes]
            got = []
            for half, da_head in enumerate(head_parts(da_pair)):
                prob = probs[seq * HEADS + 2 * pair + half]
                grad_prob = dot(da_head, value_pair, 1, 1)
                inner = jnp.sum(prob * grad_prob, axis=-1, keepdims=True)
                grad_score = (prob * (grad_prob - inner) * HEAD ** (-0.5)).astype(jnp.bfloat16)
                got.append(
                    (
                        dot(grad_score, key_pair, 1, 0),
                        dot(grad_score, query_pair, 0, 0),
                        dot(prob.astype(jnp.bfloat16), da_pair, 0, 0),
                    )
                )
            left = left_lanes(got[0][0])
            query_grad, key_grad, value_grad = [
                jnp.where(left, one, two) for one, two in zip(got[0], got[1])
            ]
            dqkv[span, lanes] = query_grad.astype(jnp.bfloat16)
            dqkv[span, HID + lanes.start : HID + lanes.stop] = key_grad.astype(jnp.bfloat16)
            dqkv[span, 2 * HID + lanes.start : 2 * HID + lanes.stop] = value_grad.astype(
                jnp.bfloat16
            )
            vec_out[2:3, lanes] = vec_out[2:3, lanes] + row_sum(query_grad)
            vec_out[3:4, lanes] = vec_out[3:4, lanes] + row_sum(value_grad)
    unit, scale = norm_parts(tok[...].astype(jnp.float32))
    ready(0, 2 * rows)
    back = dot(dqkv[...], w_in[...], 1, 0)
    grad_tok[...] = dh[...] + norm_back(unit, scale, back * vec_all[0:1, :])
    vec_out[0:1, :] = row_sum(back * unit)
    vec_out[1:2, :] = row_sum(back)
    vec_out[4:5, :] = vec_second[2:3, :]
    vec_out[5:7, :] = vec_second[0:2, :]
    vec_out[7:12, :] = vec_first[0:5, :]
    wide = windows[0].shape[1]
    spread_terms(place, dqkv, rows, 0, windows, wide)
    packed[...] = jnp.zeros_like(packed)
    for at, lanes, row, source in vector_tiles(wide):
        packed[at : at + 1, lanes] = vec_out[row : row + 1, source]
    for window in windows:
        window[dqkv.shape[0] :, :] = packed[...].astype(jnp.bfloat16)


def vector_tiles(wide):
    across, packed = D // 128, wide // 128
    for index in range(12 * across):
        at, to = divmod(index, packed)
        row, source = divmod(index, across)
        yield at, slice(to * 128, to * 128 + 128), row, slice(source * 128, source * 128 + 128)


def product_kernel(rows, wide, lane, starts, split, which, place, *rest):
    last = split is None and starts is None
    terms, columns, rest = rest[:4], rest[4:-6], rest[-6:]
    away, mine, left, right, whole, sums = rest
    if last:
        vec_all, columns = columns[0], columns[1:]
    count = columns[0].shape[0]
    for index in range(4):
        left[index * count : (index + 1) * count] = terms[index][:count, lane : lane + wide]
    core, across, high = place[4], place[5], place[6]

    def column(index):
        value = columns[index]
        if last and index > 0:
            unit, _ = norm_parts(value[:, :D].astype(jnp.float32))
            return (unit * vec_all[0:1, :] + vec_all[1:2, :]).astype(jnp.bfloat16)
        start = 0 if last else starts[index]
        return value[:, start : start + D]

    def put(span, other):
        for index in range(4):
            value = column(index)
            if other is not None:
                value = jnp.where(other, column(4 + index), value)
            right[index * count : (index + 1) * count] = value
        whole[span, :] = dot(left[:, span], right[...], 0, 0).astype(jnp.bfloat16)

    if split is None:
        put(slice(0, wide), None)
    else:
        start = rows - wide
        chosen = core == which
        if split <= start:
            put(slice(0, split), chosen & (across == 1))
            put(slice(split, wide), chosen)
        else:
            put(slice(0, split - start), chosen)
            put(slice(split - start, wide), chosen & (across == 0))
    part = rows // 4
    first = across * (wide - rows // 2)
    away[:part] = whole[pl.ds(pl.multiple_of(first + (1 - high) * part, 16), part), :]
    mine[:part] = whole[pl.ds(pl.multiple_of(first + high * part, 16), part), :]
    if last:
        total = terms[0][count:, :].astype(jnp.float32)
        for index in range(1, 4):
            total = total + terms[index][count:, :].astype(jnp.float32)
        sums[...] = jnp.zeros_like(sums)
        for at, lanes, row, source in vector_tiles(wide):
            sums[row : row + 1, source] = total[at : at + 1, lanes]
        away[part:] = sums[...].astype(jnp.bfloat16)
        mine[part:] = sums[...].astype(jnp.bfloat16)


any_spec = pl.BlockSpec(memory_space=pl.ANY)
vmem_spec = pl.BlockSpec(memory_space=pltpu.VMEM)
smem_spec = pl.BlockSpec(memory_space=pltpu.SMEM)
bf16, f32 = jnp.bfloat16, jnp.float32


def grant(inputs, outputs, scratch):
    arrays = [value for value, spec in inputs if spec is vmem_spec]
    arrays += [jax.ShapeDtypeStruct(shape, kind) for shape, kind, spec in outputs]
    need = 2 * sum(value.size * value.dtype.itemsize for value in arrays)
    for item in scratch:
        if hasattr(item, "shape") and item.dtype in (bf16, f32):
            need += math.prod(item.shape) * jnp.dtype(item.dtype).itemsize
    return need + 6 * 1024 * 1024


def call(kernel, inputs, outputs, scratch, flops, moved):
    return pl.pallas_call(
        kernel,
        grid=(1,),
        in_specs=[spec for _, spec in inputs],
        out_specs=[spec for _, _, spec in outputs],
        out_shape=[jax.ShapeDtypeStruct(shape, kind) for shape, kind, _ in outputs],
        scratch_shapes=scratch,
        compiler_params=pltpu.CompilerParams(vmem_limit_bytes=grant(inputs, outputs, scratch)),
        cost_estimate=pl.CostEstimate(flops=flops, bytes_accessed=moved, transcendentals=0),
    )(*[value for value, _ in inputs])


def after(kernel, inputs, waits):
    count, extra = len(inputs), len(waits)

    def body(*refs):
        kernel(*refs[:count], *refs[count + extra :])

    return body, inputs + [(value, any_spec) for value in waits]


def parameter_blocks(links, weights, vectors):
    shards = links.chips * links.cores
    width = vectors.shape[1]
    number = links.chip * links.cores + links.core
    location = lax.broadcasted_iota(jnp.int32, (vectors.shape[0], width * shards), 1) // width
    spread = jnp.where(location == number, jnp.tile(vectors, (1, shards)), 0.0)
    spread = jnp.pad(spread, ((0, vector_pad - vectors.shape[0]), (0, 0))).astype(bf16)
    first, second = links.own_pieces(weights)
    size = first.shape[0]
    mine = jnp.concatenate([first.astype(bf16), second.astype(bf16), spread])
    inner = (links.chip == 1) | (links.chip == 2)
    near = links.along(mine, {0: 1, 1: 0, 2: 3, 3: 2})
    middle = links.along(mine, {1: 2, 2: 1})
    across = links.along(near, {1: 2, 2: 1})
    outward = links.along(middle, {1: 0, 2: 3})
    far = links.along(across, {1: 0, 2: 3})
    block = weights.astype(bf16)
    blocks = [block, links.swap_core(block)]
    slots = (near, jnp.where(inner, middle, outward), jnp.where(inner, across, far))
    total = spread
    for slot in slots:
        total = total + slot[2 * size :]
        for piece in links.gather_pieces(slot[:size], slot[size : 2 * size]):
            blocks += [piece, links.swap_core(piece)]
    total = total + links.swap_core(total)
    return blocks, total.astype(f32)


def direct_step(links, tokens, segments, cotangent, state, vectors):
    count = tokens.shape[0]
    weights = state[0]
    rows = weights.shape[0]
    wide = -(-rows // 256) * 128
    blocks, vec_all = parameter_blocks(links, weights, vectors)
    low = links.chip < links.chips // 2
    place = jnp.stack(
        [
            links.chip,
            links.chip ^ 1,
            jnp.where(low, 2, 1),
            jnp.where(low, 3, 0),
            links.core,
            links.bit_of(0),
            links.bit_of(1),
            links.bit_of(links.bits - 1),
        ]
    ).astype(jnp.int32)
    ends = [(place, smem_spec)]
    pairs = segments.shape[0] * HEADS
    length = segments.shape[1]
    unit_cost = 2 * count * HID * D
    parameters = [(block, any_spec) for block in blocks]

    def full(*arrays):
        return [(array, vmem_spec) for array in arrays]

    def shape(width, kind=bf16, height=count):
        return (height, width), kind, vmem_spec

    def weight_scratch(chips):
        return [pltpu.VMEM((chips * 2 * rows, D), bf16)]

    def weight_sem(chips):
        return [pltpu.SemaphoreType.DMA((chips * 2,))]

    def share_rows(parts):
        own, to_core, to_side, to_both = parts
        side = links.swap_bit(to_side, 0)
        both = links.swap_both(to_both, 0)
        other = links.swap_core(to_core)
        return [own, other, side, both]

    joined = jnp.concatenate([tokens, cotangent], axis=1)
    joined_side = links.swap_bit(joined, 0)
    joined_core = links.swap_core(joined)
    joined_both = links.swap_core(joined_side)
    joined_all = [joined, joined_core, joined_side, joined_both]
    column = segments.reshape(count, 1)
    n_one, qkv, probs, att = call(
        functools.partial(query_kernel, rows),
        ends + full(tokens, column, segments, vec_all) + parameters,
        [
            shape(D),
            shape(3 * HID),
            ((pairs, length, length), f32, vmem_spec),
            shape(HID),
        ],
        weight_scratch(1) + weight_sem(1),
        4 * unit_cost,
        6 * HID * D,
    )
    active_out = call(
        functools.partial(active_kernel, rows),
        ends + full(tokens, att, vec_all) + parameters,
        [shape(D), shape(D, f32), shape(FF), shape(FF, f32)]
        + [shape(wide), shape(wide + D), shape(wide + D), shape(wide)],
        weight_scratch(2) + weight_sem(2),
        5 * unit_cost,
        8 * rows * D,
    )
    n_two, hidden, act, slope = active_out[:4]
    rows_three = share_rows(active_out[4:])
    n_two_both = links.swap_core(rows_three[2])
    n_two_all = [n_two, rows_three[1], rows_three[2], n_two_both]
    n_two_starts = [0, wide, wide, wide]
    change_out = call(
        functools.partial(change_kernel, rows),
        ends + full(cotangent, att, act, slope, hidden, vec_all) + parameters,
        [shape(D), shape(FF), shape(D, f32, 8)] + [shape(2 * wide)] * 4,
        weight_scratch(2) + [pltpu.VMEM((count, HID + 2 * FF), bf16)] + weight_sem(2),
        8 * unit_cost,
        8 * rows * D,
    )
    out, dub, vec_first = change_out[:3]
    rows_middle = share_rows(change_out[3:])

    def product(parts, columns, lane, starts, split=None, which=0, waits=()):
        extra = 0 if starts is not None else vector_pad
        kernel, inputs = after(
            functools.partial(product_kernel, rows, wide, lane, starts, split, which),
            ends + full(*parts) + full(*columns),
            list(waits),
        )
        return call(
            kernel,
            inputs,
            [shape(D, bf16, rows // 4 + extra)] * 2,
            [
                pltpu.VMEM((4 * count, wide), bf16),
                pltpu.VMEM((4 * count, D), bf16),
                pltpu.VMEM((wide, D), bf16),
                pltpu.VMEM((vector_pad, D), f32),
            ],
            8 * count * wide * D,
            4 * rows * D,
        )

    def scatter_rest(parts):
        away, mine = parts
        got = links.swap_bit(away, 1)
        mine = add_bf(mine, got)
        part = rows // 4
        mine, rest = mine[:part], mine[part:]
        for bit in range(2, links.bits):
            size = mine.shape[0] // 2
            away = lax.dynamic_slice_in_dim(mine, (1 - links.bit_of(bit)) * size, size)
            near = lax.dynamic_slice_in_dim(mine, links.bit_of(bit) * size, size)
            mine = add_bf(near, links.swap_bit(away, bit))
            if rest.shape[0]:
                rest = add_bf(rest, links.swap_bit(rest, bit))
        return jnp.concatenate([mine, rest]) if rest.shape[0] else mine

    product_three = product(rows_three, joined_all, 0, [D] * 4)
    three = scatter_rest(product_three)
    kernel, inputs = after(
        functools.partial(hidden_kernel, rows),
        ends + full(dub, hidden, cotangent, vec_all) + parameters,
        product_three[:1],
    )
    dh, dh_bf, da, vec_second = call(
        kernel,
        inputs,
        [shape(D, f32), shape(D), shape(HID), shape(D, f32, 8)],
        weight_scratch(2) + weight_sem(2),
        5 * unit_cost,
        8 * rows * D,
    )
    dh_side = links.swap_bit(dh_bf, 0)
    dh_core = links.swap_core(dh_bf)
    kernel, inputs = after(
        functools.partial(attention_kernel, rows),
        ends + full(da, qkv, probs, dh, tokens, vec_all, vec_first, vec_second) + parameters,
        [vec_second],
    )
    attention_out = call(
        kernel,
        inputs,
        [shape(D, f32)] + [shape(wide, bf16, count + vector_pad)] * 4,
        weight_scratch(1)
        + [
            pltpu.VMEM((count, 3 * HID), bf16),
            pltpu.VMEM((vector_pad, D), f32),
            pltpu.VMEM((vector_pad, wide), f32),
        ]
        + weight_sem(1),
        4 * unit_cost,
        4 * rows * D,
    )
    grad_tok = attention_out[0]
    rows_zero = share_rows(attention_out[1:])
    product_two = product(
        rows_middle,
        n_two_all + joined_all,
        0,
        n_two_starts + [D] * 4,
        4 * HID + FF - 5 * rows,
        1,
        waits=[grad_tok],
    )
    two = scatter_rest(product_two)
    dh_side, _ = lax.optimization_barrier((dh_side, product_two[1]))
    dh_both = links.swap_core(dh_side)
    dh_all = [dh_bf, dh_core, dh_side, dh_both]
    product_zero = product(
        rows_zero, [vec_all, n_one] + joined_all[1:], 0, None, waits=product_two[:1]
    )
    zero = scatter_rest(product_zero)
    product_one = product(
        rows_middle,
        n_two_all + dh_all,
        wide,
        n_two_starts + [0] * 4,
        4 * HID - 2 * rows,
        0,
        waits=product_zero[:1],
    )
    one = scatter_rest(product_one)
    three, _ = lax.optimization_barrier((three, product_two[1]))
    three = links.to_chip(three, {0: 1, 2: 3})
    two = links.to_chip(two, {0: 1, 3: 2})
    three = links.to_chip(three, {1: 3})
    two = links.to_chip(two, {1: 2})
    one = links.to_chip(one, {0: 1, 3: 2})
    one = links.to_chip(one, {2: 1})
    zero = links.to_chip(zero, {0: 1, 1: 0, 2: 3, 3: 2})
    zero = links.to_chip(zero, {0: 2, 2: 0})
    mine = jnp.where(links.chip == 1, one, jnp.where(links.chip == 2, two, three))
    size = mine.shape[0]
    mine = jnp.where(links.chip == 0, zero[:size], mine)
    grad_w = links.gather_positions(mine).astype(f32)
    sums = zero[size:]
    got = links.along(sums, {0: 1, 2: 3})
    sums = jnp.where(links.chip % 2 == 0, sums, got).astype(f32)
    width = vectors.shape[1]
    grad_v = lax.dynamic_slice_in_dim(sums, lax.axis_index("shard") * width, width, 1)
    new = [grad_w] + list(adam_update(*state, grad_w, decay_rate))
    return out, grad_tok, grad_v[: vectors.shape[0]], new


def per_device(
    replicas,
    shards,
    tokens,
    segments,
    cotangent,
    weights,
    vectors,
    first_weights,
    first_vectors,
    second_weights,
    second_vectors,
):
    if Links.fits(replicas, shards, weights.shape[0]):
        output, grad_tokens, grad_v, new = direct_step(
            Links(replicas, shards),
            tokens,
            segments,
            cotangent,
            (weights, first_weights, second_weights),
            vectors,
        )
    else:
        w_full = lax.all_gather(weights.astype(jnp.bfloat16), "shard", axis=0, tiled=True)
        v_full = lax.all_gather(vectors.astype(jnp.bfloat16), "shard", axis=1, tiled=True)
        output, kept_state = forward(tokens, segments, w_full, v_full)
        grad_tokens, grad_vec, row_terms, col_terms = backward(
            kept_state, cotangent, segments, w_full
        )
        local_grad = weight_grads(row_terms, col_terms).astype(jnp.bfloat16)
        own_w = lax.psum_scatter(local_grad, "shard", scatter_dimension=0, tiled=True)
        own_v = lax.psum_scatter(
            grad_vec.astype(jnp.bfloat16), "shard", scatter_dimension=1, tiled=True
        )
        grad_w = lax.psum(own_w, "rep").astype(jnp.float32)
        grad_v = lax.psum(own_v, "rep").astype(jnp.float32)
        new = [grad_w]
        new += adam_update(weights, first_weights, second_weights, grad_w, decay_rate)
    grad_w, new_w, new_fw, new_sw = new
    new_v, new_fv, new_sv = adam_update(vectors, first_vectors, second_vectors, grad_v, 0.0)
    return (output, grad_tokens, grad_w, grad_v, new_w, new_v, new_fw, new_fv, new_sw, new_sv)


def solution(mesh):
    placed = (
        P(("rep", "shard"), None),
        P(("rep", "shard"), None),
        P(("rep", "shard"), None),
        P("shard", None),
        P(None, "shard"),
        P("shard", None),
        P(None, "shard"),
        P("shard", None),
        P(None, "shard"),
    )
    return jax.shard_map(
        functools.partial(per_device, mesh.shape["rep"], mesh.shape["shard"]),
        mesh=mesh,
        in_specs=placed,
        out_specs=(
            P(("rep", "shard"), None),
            P(("rep", "shard"), None),
            P("shard", None),
            P(None, "shard"),
            P("shard", None),
            P(None, "shard"),
            P("shard", None),
            P(None, "shard"),
            P("shard", None),
            P(None, "shard"),
        ),
        check_vma=False,
    )
```

```python
import functools
import math

import jax
import jax.numpy as jnp
from jax import lax
from jax.experimental import pallas as pl
from jax.experimental.pallas import tpu as pltpu
from jax.sharding import PartitionSpec as P

D = 768
HEADS = 12
HEAD = 64
FF = 3072
STEP = 3
HID = 768
R = 9216


norm_eps = 1e-05
beta_one = 0.9
beta_two = 0.999
adam_eps = 1e-08
learn_rate = 0.2
decay_rate = 0.1
masked_score = -1e30


def normalize(values):
    centred = values - jnp.mean(values, axis=-1, keepdims=True)
    return centred * lax.rsqrt(jnp.mean(centred * centred, axis=-1, keepdims=True) + norm_eps)


def affine_norm(values, gain_vec, shift_vec):
    return normalize(values) * gain_vec + shift_vec


def gelu_tanh(values):
    return jax.nn.gelu(values, approximate=True)


def matmul(left_op, right_op):
    return jnp.dot(left_op, right_op, preferred_element_type=jnp.float32)


def matmul_nt(left_op, right_op):
    return lax.dot_general(
        left_op, right_op, (((1,), (1,)), ((), ())), preferred_element_type=jnp.float32
    )


def matmul_tn(left_op, right_op):
    return lax.dot_general(
        left_op, right_op, (((0,), (0,)), ((), ())), preferred_element_type=jnp.float32
    )


def product(pattern, left_op, right_op):
    return jnp.einsum(pattern, left_op, right_op, preferred_element_type=jnp.float32)


def allowed_pairs(segments):
    length = segments.shape[1]
    places = lax.broadcasted_iota(jnp.int32, (length, length), 0)
    others = lax.broadcasted_iota(jnp.int32, (length, length), 1)
    causal = others <= places
    same_doc = segments[:, :, None] == segments[:, None, :]
    return (causal[None] & same_doc)[:, None]


def scores_of(query_rows, key_rows, allowed):
    raw_scores = product("sqhd,skhd->shqk", query_rows, key_rows) * HEAD ** (-0.5)
    return jnp.where(allowed, raw_scores, masked_score)


def forward(tokens, segments, w_bf, v_bf):
    seq_count, length = segments.shape
    tok_count = tokens.shape[0]
    head_shape = (seq_count, length, HEADS, HEAD)
    floats = v_bf.astype(jnp.float32)
    residual = tokens.astype(jnp.float32)
    normed_one = affine_norm(residual, floats[0], floats[1]).astype(jnp.bfloat16)
    projected = matmul_nt(normed_one, w_bf[: 3 * HID])
    query_rows = (projected[:, :HID] + floats[2]).astype(jnp.bfloat16)
    key_rows = projected[:, HID : 2 * HID].astype(jnp.bfloat16)
    value_rows = (projected[:, 2 * HID :] + floats[3]).astype(jnp.bfloat16)
    allowed = allowed_pairs(segments)
    scores = scores_of(query_rows.reshape(head_shape), key_rows.reshape(head_shape), allowed)
    row_max = jnp.max(scores, axis=-1, keepdims=True)
    log_total = row_max + jnp.log(jnp.sum(jnp.exp(scores - row_max), axis=-1, keepdims=True))
    attn_probs = jnp.exp(scores - log_total).astype(jnp.bfloat16)
    mixed_heads = product("shqk,skhd->sqhd", attn_probs, value_rows.reshape(head_shape))
    attended = mixed_heads.reshape(tok_count, HID).astype(jnp.bfloat16)
    hidden_one = residual + matmul(attended, w_bf[3 * HID : 4 * HID]) + floats[4]
    normed_two = affine_norm(hidden_one, floats[5], floats[6]).astype(jnp.bfloat16)
    pre_act = matmul_nt(normed_two, w_bf[4 * HID : 4 * HID + FF]) + floats[7:11].reshape(FF)
    active = gelu_tanh(pre_act).astype(jnp.bfloat16)
    output = (hidden_one + matmul(active, w_bf[4 * HID + FF :]) + floats[11]).astype(jnp.bfloat16)
    kept_state = (
        residual,
        normed_one,
        query_rows,
        key_rows,
        value_rows,
        log_total,
        attended,
        hidden_one,
        normed_two,
        pre_act,
        active,
        floats,
    )
    return (output, kept_state)


def backward(kept_state, cotangent, segments, w_bf):
    (
        residual,
        normed_one,
        query_rows,
        key_rows,
        value_rows,
        log_total,
        attended,
        hidden_one,
        normed_two,
        pre_act,
        active,
        floats,
    ) = kept_state
    seq_count, length = segments.shape
    tok_count = residual.shape[0]
    head_shape = (seq_count, length, HEADS, HEAD)
    grad_out = cotangent.astype(jnp.float32)
    grad_active = matmul_nt(cotangent, w_bf[4 * HID + FF :])
    grad_pre = jax.vjp(gelu_tanh, pre_act)[1](grad_active)[0]
    grad_pre_bf = grad_pre.astype(jnp.bfloat16)
    grad_normed_two = matmul(grad_pre_bf, w_bf[4 * HID : 4 * HID + FF])
    norm_back_two = jax.vjp(affine_norm, hidden_one, floats[5], floats[6])[1]
    grad_h_part, grad_gain_two, grad_shift_two = norm_back_two(grad_normed_two)
    grad_hidden = grad_out + grad_h_part
    grad_hidden_bf = grad_hidden.astype(jnp.bfloat16)
    grad_attended = matmul_nt(grad_hidden_bf, w_bf[3 * HID : 4 * HID]).astype(jnp.bfloat16)
    query_four = query_rows.reshape(head_shape)
    key_four = key_rows.reshape(head_shape)
    value_four = value_rows.reshape(head_shape)
    grad_att_four = grad_attended.reshape(head_shape)
    allowed = allowed_pairs(segments)
    scores = scores_of(query_four, key_four, allowed)
    attn_probs = jnp.exp(scores - log_total)
    probs_bf = attn_probs.astype(jnp.bfloat16)
    grad_probs = product("sqhd,skhd->shqk", grad_att_four, value_four)
    inner_sum = jnp.sum(attn_probs * grad_probs, axis=-1, keepdims=True)
    grad_scores = (attn_probs * (grad_probs - inner_sum) * HEAD ** (-0.5)).astype(jnp.bfloat16)
    grad_query = product("shqk,skhd->sqhd", grad_scores, key_four).reshape(tok_count, HID)
    grad_keys = product("shqk,sqhd->skhd", grad_scores, query_four).reshape(tok_count, HID)
    grad_values = product("shqk,sqhd->skhd", probs_bf, grad_att_four).reshape(tok_count, HID)
    grad_proj = jnp.concatenate([grad_query, grad_keys, grad_values], axis=1)
    grad_proj_bf = grad_proj.astype(jnp.bfloat16)
    grad_normed_one = matmul(grad_proj_bf, w_bf[: 3 * HID])
    norm_back_one = jax.vjp(affine_norm, residual, floats[0], floats[1])[1]
    grad_r_part, grad_gain_one, grad_shift_one = norm_back_one(grad_normed_one)
    grad_tokens = grad_hidden + grad_r_part
    bias_ff = jnp.sum(grad_pre, axis=0).reshape(FF // D, D)
    head_rows = jnp.stack(
        [
            grad_gain_one,
            grad_shift_one,
            jnp.sum(grad_query, axis=0),
            jnp.sum(grad_values, axis=0),
            jnp.sum(grad_hidden, axis=0),
            grad_gain_two,
            grad_shift_two,
        ]
    )
    grad_vec = jnp.concatenate([head_rows, bias_ff, jnp.sum(grad_out, axis=0)[None]], axis=0)
    row_terms = jnp.concatenate([grad_proj_bf, attended, grad_pre_bf, active], axis=1)
    col_terms = jnp.stack([normed_one, grad_hidden_bf, normed_two, cotangent])
    return (grad_tokens, grad_vec, row_terms, col_terms)


def weight_grads(row_terms, col_terms):
    row_bounds = (0, 3 * HID, 4 * HID, 4 * HID + FF, R)
    pieces = [
        matmul_tn(row_terms[:, row_bounds[index] : row_bounds[index + 1]], col_terms[index])
        for index in range(4)
    ]
    return jnp.concatenate(pieces, axis=0)


def adam_update(param, first, second, grad, decay):
    new_first = beta_one * first + (1.0 - beta_one) * grad
    new_second = beta_two * second + (1.0 - beta_two) * grad * grad
    first_hat = new_first / (1.0 - beta_one**STEP)
    second_hat = new_second / (1.0 - beta_two**STEP)
    new_param = param - learn_rate * (first_hat / (jnp.sqrt(second_hat) + adam_eps) + decay * param)
    return (new_param, new_first, new_second)


def bit_reverse(index, bits):
    out = index * 0
    for place in range(bits):
        out = out * 2 + (index >> place) % 2
    return out


class Links:
    def __init__(self, replicas, shards):
        self.replicas = replicas
        self.cores = 2
        self.chips = shards // self.cores
        self.bits = replicas.bit_length() - 1
        self.replica = lax.axis_index("rep")
        shard = lax.axis_index("shard")
        self.chip = shard // self.cores
        self.core = shard % self.cores

    @staticmethod
    def fits(replicas, shards, rows):
        power = replicas > 2 and replicas & (replicas - 1) == 0
        return shards == 8 and power and 2 * rows == 3 * HID

    def send(self, value, target):
        route = []
        for rep in range(self.replicas):
            for chip in range(self.chips):
                for core in range(self.cores):
                    goal = target(rep, chip, core)
                    if goal is None:
                        continue
                    start = (rep * self.chips + chip) * self.cores + core
                    stop = (goal[0] * self.chips + goal[1]) * self.cores + goal[2]
                    route.append((start, stop))
        return lax.ppermute(value, ("rep", "shard"), route)

    def swap_core(self, value):
        return self.send(value, lambda rep, chip, core: (rep, chip, 1 - core))

    def swap_both(self, value, bit):
        return self.send(value, lambda rep, chip, core: (rep ^ (1 << bit), chip, 1 - core))

    def swap_bit(self, value, bit):
        return self.send(value, lambda rep, chip, core: (rep ^ (1 << bit), chip, core))

    def along(self, value, moves):
        table = dict(moves)
        return self.send(
            value, lambda rep, chip, core: (rep, table[chip], core) if chip in table else None
        )

    def bit_of(self, bit):
        return (self.replica >> bit) % 2

    def own_pieces(self, block):
        half = block.shape[0] // 2
        size = half // self.replicas
        first = lax.dynamic_slice_in_dim(block, self.replica * size, size)
        turned = bit_reverse(self.replica, self.bits)
        second = lax.dynamic_slice_in_dim(block, half + turned * size, size)
        return first, second

    def gather_pieces(self, first, second):
        for step in range(self.bits):
            low, high = step, self.bits - 1 - step
            got_first = self.swap_bit(first, low)
            got_second = self.swap_bit(second, high)
            if step == self.bits - 1:
                return [first, got_first, second, got_second]
            first = jnp.where(
                self.bit_of(low) == 0,
                jnp.concatenate([first, got_first]),
                jnp.concatenate([got_first, first]),
            )
            second = jnp.where(
                self.bit_of(high) == 0,
                jnp.concatenate([second, got_second]),
                jnp.concatenate([got_second, second]),
            )

    def gather_positions(self, piece):
        size = piece.shape[0] // 2
        first, second = piece[:size], piece[size:]
        for step in range(self.bits):
            high, low = self.bits - 1 - step, step
            got_first = self.swap_bit(first, high)
            got_second = self.swap_bit(second, low)
            first = jnp.where(
                self.bit_of(high) == 0,
                jnp.concatenate([first, got_first]),
                jnp.concatenate([got_first, first]),
            )
            second = jnp.where(
                self.bit_of(low) == 0,
                jnp.concatenate([second, got_second]),
                jnp.concatenate([got_second, second]),
            )
        parts = []
        for position in range(self.replicas):
            turned = bit_reverse(position, self.bits)
            parts.append(first[position * size : (position + 1) * size])
            parts.append(second[turned * size : (turned + 1) * size])
        return jnp.concatenate(parts)

    def to_chip(self, piece, moves):
        got = self.along(piece, moves)
        return add_bf(piece, got)


def add_bf(left, right):
    return (left.astype(jnp.float32) + right.astype(jnp.float32)).astype(jnp.bfloat16)


vector_pad = 16


def dot(left, right, left_dim, right_dim):
    return lax.dot_general(
        left,
        right,
        (((left_dim,), (right_dim,)), ((), ())),
        preferred_element_type=jnp.float32,
    )


def norm_parts(values):
    centred = values - jnp.mean(values, axis=-1, keepdims=True)
    scale = lax.rsqrt(jnp.mean(centred * centred, axis=-1, keepdims=True) + norm_eps)
    return centred * scale, scale


def norm_back(unit, scale, grad):
    inner = jnp.mean(grad, axis=-1, keepdims=True)
    outer = jnp.mean(grad * unit, axis=-1, keepdims=True)
    return scale * (grad - inner - unit * outer)


def row_sum(values):
    return jnp.sum(values, axis=0, keepdims=True)


def left_lanes(value):
    return lax.broadcasted_iota(jnp.int32, value.shape, 1) < HEAD


def head_parts(pair):
    left = left_lanes(pair)
    none = jnp.zeros_like(pair)
    return jnp.where(left, pair, none), jnp.where(left, none, pair)


def load_blocks(place, blocks, rows, target, sem, first, last):
    quarter = rows // 4
    starts = (
        place[7] * quarter,
        (1 - place[7]) * quarter,
        (2 + place[5]) * quarter,
        (3 - place[5]) * quarter,
    )
    for slot in range(4):
        chip = place[slot]

        @pl.when((chip >= first) & (chip < last))
        def _():
            for side in range(2):
                core = place[4] if side == 0 else 1 - place[4]
                number = (chip - first) * 2 + core
                if slot == 0:
                    parts = [(blocks[side], 0, rows)]
                else:
                    at = 2 + (slot - 1) * 8 + side
                    parts = [
                        (blocks[at + 2 * index], starts[index], quarter) for index in range(4)
                    ]
                for ref, shift, size in parts:
                    start = pl.multiple_of(number * rows + shift, 16)
                    pltpu.make_async_copy(ref, target.at[pl.ds(start, size)], sem.at[number]).start()

    done = set()

    def ready(low, high):
        for number in range(low // rows, -(-high // rows)):
            if number in done:
                continue
            done.add(number)
            index = number - 2 * first
            pltpu.make_async_copy(
                blocks[0], target.at[pl.ds(index * rows, rows)], sem.at[index]
            ).wait()

    return ready


block_count = 26


def spread_terms(place, terms, rows, first, outs, wide, lane=0):
    core, across = place[4], place[5]
    count = terms.shape[0]
    for index, out in enumerate(outs):
        block = core if index % 2 == 0 else 1 - core
        side = across if index < 2 else 1 - across
        start = pl.multiple_of(first + block * rows + side * (rows - wide), 128)
        out[:count, lane : lane + wide] = terms[:, pl.ds(start, wide)]


def query_kernel(rows, place, tok, seg_col, seg_row, vec_all, *rest):
    blocks = rest[:block_count]
    n_out, qkv, probs, att, w_in, load_sem = rest[block_count:]
    ready = load_blocks(place, blocks, rows, w_in, load_sem, 0, 1)
    unit, _ = norm_parts(tok[...].astype(jnp.float32))
    n_one = (unit * vec_all[0:1, :] + vec_all[1:2, :]).astype(jnp.bfloat16)
    n_out[...] = n_one
    for index, bias in enumerate((vec_all[2:3, :], None, vec_all[3:4, :])):
        ready(index * HID, (index + 1) * HID)
        value = dot(n_one, w_in[index * HID : (index + 1) * HID], 1, 1)
        if bias is not None:
            value = value + bias
        qkv[:, index * HID : (index + 1) * HID] = value.astype(jnp.bfloat16)
    length = seg_row.shape[1]
    for seq in range(seg_row.shape[0]):
        span = slice(seq * length, (seq + 1) * length)
        order = lax.broadcasted_iota(jnp.int32, (length, length), 0)
        other = lax.broadcasted_iota(jnp.int32, (length, length), 1)
        allowed = (other <= order) & (seg_col[span, :] == seg_row[seq : seq + 1, :])
        for pair in range(HEADS // 2):
            lanes = slice(pair * 2 * HEAD, (pair + 1) * 2 * HEAD)
            key_pair = qkv[span, HID + lanes.start : HID + lanes.stop]
            value_pair = qkv[span, 2 * HID + lanes.start : 2 * HID + lanes.stop]
            mixed = []
            for half, query in enumerate(head_parts(qkv[span, lanes])):
                raw = dot(query, key_pair, 1, 1) * HEAD ** (-0.5)
                raw = jnp.where(allowed, raw, masked_score)
                top = jnp.max(raw, axis=-1, keepdims=True)
                power = jnp.exp(raw - top)
                prob = power * (1.0 / jnp.sum(power, axis=-1, keepdims=True))
                probs[seq * HEADS + 2 * pair + half] = prob
                mixed.append(dot(prob.astype(jnp.bfloat16), value_pair, 1, 0))
            att[span, lanes] = jnp.where(left_lanes(mixed[0]), mixed[0], mixed[1]).astype(
                jnp.bfloat16
            )


def active_kernel(rows, place, tok, att, vec_all, *rest):
    blocks = rest[:block_count]
    n_out, hidden, act, slope_out = rest[block_count : block_count + 4]
    windows = rest[block_count + 4 : block_count + 8]
    w_mid, load_sem = rest[block_count + 8 :]
    ready = load_blocks(place, blocks, rows, w_mid, load_sem, 1, 3)
    base = 2 * rows

    def weight(first, size):
        ready(first, first + size)
        return w_mid[first - base : first - base + size]

    h_value = tok[...].astype(jnp.float32) + dot(att[...], weight(3 * HID, HID), 1, 0)
    h_value = h_value + vec_all[4:5, :]
    hidden[...] = h_value
    unit, _ = norm_parts(h_value)
    n_two = (unit * vec_all[5:6, :] + vec_all[6:7, :]).astype(jnp.bfloat16)
    n_out[...] = n_two
    root = math.sqrt(2.0 / math.pi)
    for index in range(FF // D):
        span = slice(index * D, (index + 1) * D)
        pre = dot(n_two, weight(4 * HID + index * D, D), 1, 1) + vec_all[7 + index : 8 + index, :]
        squared = pre * pre
        bent = jnp.tanh(root * (pre + 0.044715 * (pre * squared)))
        half = 0.5 * (1.0 + bent)
        act[:, span] = (pre * half).astype(jnp.bfloat16)
        slope_out[:, span] = half + 0.5 * pre * (1.0 - bent * bent) * (
            root * (1.0 + 3 * 0.044715 * squared)
        )
    wide = windows[0].shape[1]
    spread_terms(place, act, rows, 6 * rows - (4 * HID + FF), windows, wide)
    windows[1][:, wide:] = n_two
    windows[2][:, wide:] = n_two
    ready(2 * rows, 6 * rows)


def change_kernel(rows, place, cot, att, act, slope, hidden, vec_all, *rest):
    blocks = rest[:block_count]
    rest = rest[block_count:]
    out, dub, vec_out = rest[:3]
    windows_two, windows_one = rest[3:7], rest[7:11]
    w_top, terms, load_sem = rest[11:]
    ready = load_blocks(place, blocks, rows, w_top, load_sem, 2, 4)
    base = 4 * rows
    terms[:, :HID] = att[...]
    result = hidden[...] + vec_all[11:12, :]
    for index in range(FF // D):
        span = slice(index * D, (index + 1) * D)
        first = 4 * HID + FF + index * D - base
        ready(first + base, first + base + D)
        weight = w_top[first : first + D]
        active = act[:, span]
        change = dot(cot[...], weight, 1, 1) * slope[:, span]
        change_bf = change.astype(jnp.bfloat16)
        dub[:, span] = change_bf
        terms[:, HID + index * D : HID + (index + 1) * D] = change_bf
        terms[:, HID + FF + index * D : HID + FF + (index + 1) * D] = active
        vec_out[index : index + 1, :] = row_sum(change)
        result = result + dot(active, weight, 1, 0)
    wide = windows_one[0].shape[1]
    spread_terms(place, terms, rows, 2 * rows, windows_two, wide)
    spread_terms(place, terms, rows, 0, windows_one, wide)
    out[...] = result.astype(jnp.bfloat16)
    vec_out[4:5, :] = row_sum(cot[...].astype(jnp.float32))
    vec_out[5:8, :] = jnp.zeros((3, D), jnp.float32)
    ready(4 * rows, 8 * rows)


def hidden_kernel(rows, place, dub, hidden, cot, vec_all, *rest):
    blocks = rest[:block_count]
    dh, dh_bf, da, vec_out, w_mid, load_sem = rest[block_count:]
    ready = load_blocks(place, blocks, rows, w_mid, load_sem, 1, 3)
    base = 2 * rows
    unit, scale = norm_parts(hidden[...])
    start = 4 * HID
    back = None
    while start < 4 * HID + FF:
        stop = min((start // rows + 1) * rows, 4 * HID + FF)
        ready(start, stop)
        part = dot(dub[:, start - 4 * HID : stop - 4 * HID], w_mid[start - base : stop - base], 1, 0)
        back = part if back is None else back + part
        start = stop
    vec_out[0:1, :] = row_sum(back * unit)
    vec_out[1:2, :] = row_sum(back)
    value = cot[...].astype(jnp.float32) + norm_back(unit, scale, back * vec_all[5:6, :])
    dh[...] = value
    vec_out[2:3, :] = row_sum(value)
    vec_out[3:8, :] = jnp.zeros((5, D), jnp.float32)
    rounded = value.astype(jnp.bfloat16)
    dh_bf[...] = rounded
    da[...] = dot(rounded, w_mid[3 * HID - base : 4 * HID - base], 1, 1).astype(jnp.bfloat16)


def attention_kernel(rows, place, da, qkv, probs, dh, tok, vec_all, vec_first, vec_second, *rest):
    blocks = rest[:block_count]
    rest = rest[block_count:]
    grad_tok = rest[0]
    windows = rest[1:5]
    w_in, dqkv, vec_out, packed, load_sem = rest[5:]
    ready = load_blocks(place, blocks, rows, w_in, load_sem, 0, 1)
    heads_total = probs.shape[0]
    length = probs.shape[1]
    vec_out[2:4, :] = jnp.zeros((2, D), jnp.float32)
    for seq in range(heads_total // HEADS):
        span = slice(seq * length, (seq + 1) * length)
        for pair in range(HEADS // 2):
            lanes = slice(pair * 2 * HEAD, (pair + 1) * 2 * HEAD)
            query_pair = qkv[span, lanes]
            key_pair = qkv[span, HID + lanes.start : HID + lanes.stop]
            value_pair = qkv[span, 2 * HID + lanes.start : 2 * HID + lanes.stop]
            da_pair = da[span, lanes]
            got = []
            for half, da_head in enumerate(head_parts(da_pair)):
                prob = probs[seq * HEADS + 2 * pair + half]
                grad_prob = dot(da_head, value_pair, 1, 1)
                inner = jnp.sum(prob * grad_prob, axis=-1, keepdims=True)
                grad_score = (prob * (grad_prob - inner) * HEAD ** (-0.5)).astype(jnp.bfloat16)
                got.append(
                    (
                        dot(grad_score, key_pair, 1, 0),
                        dot(grad_score, query_pair, 0, 0),
                        dot(prob.astype(jnp.bfloat16), da_pair, 0, 0),
                    )
                )
            left = left_lanes(got[0][0])
            query_grad, key_grad, value_grad = [
                jnp.where(left, one, two) for one, two in zip(got[0], got[1])
            ]
            dqkv[span, lanes] = query_grad.astype(jnp.bfloat16)
            dqkv[span, HID + lanes.start : HID + lanes.stop] = key_grad.astype(jnp.bfloat16)
            dqkv[span, 2 * HID + lanes.start : 2 * HID + lanes.stop] = value_grad.astype(
                jnp.bfloat16
            )
            vec_out[2:3, lanes] = vec_out[2:3, lanes] + row_sum(query_grad)
            vec_out[3:4, lanes] = vec_out[3:4, lanes] + row_sum(value_grad)
    unit, scale = norm_parts(tok[...].astype(jnp.float32))
    ready(0, 2 * rows)
    back = dot(dqkv[...], w_in[...], 1, 0)
    grad_tok[...] = dh[...] + norm_back(unit, scale, back * vec_all[0:1, :])
    vec_out[0:1, :] = row_sum(back * unit)
    vec_out[1:2, :] = row_sum(back)
    vec_out[4:5, :] = vec_second[2:3, :]
    vec_out[5:7, :] = vec_second[0:2, :]
    vec_out[7:12, :] = vec_first[0:5, :]
    wide = windows[0].shape[1]
    spread_terms(place, dqkv, rows, 0, windows, wide)
    packed[...] = jnp.zeros_like(packed)
    for at, lanes, row, source in vector_tiles(wide):
        packed[at : at + 1, lanes] = vec_out[row : row + 1, source]
    for window in windows:
        window[dqkv.shape[0] :, :] = packed[...].astype(jnp.bfloat16)


def vector_tiles(wide):
    across, packed = D // 128, wide // 128
    for index in range(12 * across):
        at, to = divmod(index, packed)
        row, source = divmod(index, across)
        yield at, slice(to * 128, to * 128 + 128), row, slice(source * 128, source * 128 + 128)


def product_kernel(rows, wide, lane, starts, split, which, place, *rest):
    last = split is None and starts is None
    terms, columns, rest = rest[:4], rest[4:-6], rest[-6:]
    away, mine, left, right, whole, sums = rest
    if last:
        vec_all, columns = columns[0], columns[1:]
    count = columns[0].shape[0]
    for index in range(4):
        left[index * count : (index + 1) * count] = terms[index][:count, lane : lane + wide]
    core, across, high = place[4], place[5], place[6]

    def column(index):
        value = columns[index]
        if last and index > 0:
            unit, _ = norm_parts(value[:, :D].astype(jnp.float32))
            return (unit * vec_all[0:1, :] + vec_all[1:2, :]).astype(jnp.bfloat16)
        start = 0 if last else starts[index]
        return value[:, start : start + D]

    def put(span, other):
        for index in range(4):
            value = column(index)
            if other is not None:
                value = jnp.where(other, column(4 + index), value)
            right[index * count : (index + 1) * count] = value
        whole[span, :] = dot(left[:, span], right[...], 0, 0).astype(jnp.bfloat16)

    if split is None:
        put(slice(0, wide), None)
    else:
        start = rows - wide
        chosen = core == which
        if split <= start:
            put(slice(0, split), chosen & (across == 1))
            put(slice(split, wide), chosen)
        else:
            put(slice(0, split - start), chosen)
            put(slice(split - start, wide), chosen & (across == 0))
    part = rows // 4
    first = across * (wide - rows // 2)
    away[:part] = whole[pl.ds(pl.multiple_of(first + (1 - high) * part, 16), part), :]
    mine[:part] = whole[pl.ds(pl.multiple_of(first + high * part, 16), part), :]
    if last:
        total = terms[0][count:, :].astype(jnp.float32)
        for index in range(1, 4):
            total = total + terms[index][count:, :].astype(jnp.float32)
        sums[...] = jnp.zeros_like(sums)
        for at, lanes, row, source in vector_tiles(wide):
            sums[row : row + 1, source] = total[at : at + 1, lanes]
        away[part:] = sums[...].astype(jnp.bfloat16)
        mine[part:] = sums[...].astype(jnp.bfloat16)


any_spec = pl.BlockSpec(memory_space=pl.ANY)
vmem_spec = pl.BlockSpec(memory_space=pltpu.VMEM)
smem_spec = pl.BlockSpec(memory_space=pltpu.SMEM)
bf16, f32 = jnp.bfloat16, jnp.float32


def grant(inputs, outputs, scratch):
    arrays = [value for value, spec in inputs if spec is vmem_spec]
    arrays += [jax.ShapeDtypeStruct(shape, kind) for shape, kind, spec in outputs]
    need = 2 * sum(value.size * value.dtype.itemsize for value in arrays)
    for item in scratch:
        if hasattr(item, "shape") and item.dtype in (bf16, f32):
            need += math.prod(item.shape) * jnp.dtype(item.dtype).itemsize
    return need + 6 * 1024 * 1024


def call(kernel, inputs, outputs, scratch, flops, moved):
    return pl.pallas_call(
        kernel,
        grid=(1,),
        in_specs=[spec for _, spec in inputs],
        out_specs=[spec for _, _, spec in outputs],
        out_shape=[jax.ShapeDtypeStruct(shape, kind) for shape, kind, _ in outputs],
        scratch_shapes=scratch,
        compiler_params=pltpu.CompilerParams(vmem_limit_bytes=grant(inputs, outputs, scratch)),
        cost_estimate=pl.CostEstimate(flops=flops, bytes_accessed=moved, transcendentals=0),
    )(*[value for value, _ in inputs])


def after(kernel, inputs, waits):
    count, extra = len(inputs), len(waits)

    def body(*refs):
        kernel(*refs[:count], *refs[count + extra :])

    return body, inputs + [(value, any_spec) for value in waits]


def parameter_blocks(links, weights, vectors):
    shards = links.chips * links.cores
    width = vectors.shape[1]
    number = links.chip * links.cores + links.core
    location = lax.broadcasted_iota(jnp.int32, (vectors.shape[0], width * shards), 1) // width
    spread = jnp.where(location == number, jnp.tile(vectors, (1, shards)), 0.0)
    spread = jnp.pad(spread, ((0, vector_pad - vectors.shape[0]), (0, 0))).astype(bf16)
    first, second = links.own_pieces(weights)
    size = first.shape[0]
    mine = jnp.concatenate([first.astype(bf16), second.astype(bf16), spread])
    inner = (links.chip == 1) | (links.chip == 2)
    near = links.along(mine, {0: 1, 1: 0, 2: 3, 3: 2})
    middle = links.along(mine, {1: 2, 2: 1})
    across = links.along(near, {1: 2, 2: 1})
    outward = links.along(middle, {1: 0, 2: 3})
    far = links.along(across, {1: 0, 2: 3})
    block = weights.astype(bf16)
    blocks = [block, links.swap_core(block)]
    slots = (near, jnp.where(inner, middle, outward), jnp.where(inner, across, far))
    total = spread
    for slot in slots:
        total = total + slot[2 * size :]
        for piece in links.gather_pieces(slot[:size], slot[size : 2 * size]):
            blocks += [piece, links.swap_core(piece)]
    total = total + links.swap_core(total)
    return blocks, total.astype(f32)


def direct_step(links, tokens, segments, cotangent, state, vectors):
    count = tokens.shape[0]
    weights = state[0]
    rows = weights.shape[0]
    wide = -(-rows // 256) * 128
    blocks, vec_all = parameter_blocks(links, weights, vectors)
    low = links.chip < links.chips // 2
    place = jnp.stack(
        [
            links.chip,
            links.chip ^ 1,
            jnp.where(low, 2, 1),
            jnp.where(low, 3, 0),
            links.core,
            links.bit_of(0),
            links.bit_of(1),
            links.bit_of(links.bits - 1),
        ]
    ).astype(jnp.int32)
    ends = [(place, smem_spec)]
    pairs = segments.shape[0] * HEADS
    length = segments.shape[1]
    unit_cost = 2 * count * HID * D
    parameters = [(block, any_spec) for block in blocks]

    def full(*arrays):
        return [(array, vmem_spec) for array in arrays]

    def shape(width, kind=bf16, height=count):
        return (height, width), kind, vmem_spec

    def weight_scratch(chips):
        return [pltpu.VMEM((chips * 2 * rows, D), bf16)]

    def weight_sem(chips):
        return [pltpu.SemaphoreType.DMA((chips * 2,))]

    def share_rows(parts):
        own, to_core, to_side, to_both = parts
        side = links.swap_bit(to_side, 0)
        both = links.swap_both(to_both, 0)
        other = links.swap_core(to_core)
        return [own, other, side, both]

    joined = jnp.concatenate([tokens, cotangent], axis=1)
    joined_side = links.swap_bit(joined, 0)
    joined_core = links.swap_core(joined)
    joined_both = links.swap_core(joined_side)
    joined_all = [joined, joined_core, joined_side, joined_both]
    column = segments.reshape(count, 1)
    n_one, qkv, probs, att = call(
        functools.partial(query_kernel, rows),
        ends + full(tokens, column, segments, vec_all) + parameters,
        [
            shape(D),
            shape(3 * HID),
            ((pairs, length, length), f32, vmem_spec),
            shape(HID),
        ],
        weight_scratch(1) + weight_sem(1),
        4 * unit_cost,
        6 * HID * D,
    )
    active_out = call(
        functools.partial(active_kernel, rows),
        ends + full(tokens, att, vec_all) + parameters,
        [shape(D), shape(D, f32), shape(FF), shape(FF, f32)]
        + [shape(wide), shape(wide + D), shape(wide + D), shape(wide)],
        weight_scratch(2) + weight_sem(2),
        5 * unit_cost,
        8 * rows * D,
    )
    n_two, hidden, act, slope = active_out[:4]
    rows_three = share_rows(active_out[4:])
    n_two_both = links.swap_core(rows_three[2])
    n_two_all = [n_two, rows_three[1], rows_three[2], n_two_both]
    n_two_starts = [0, wide, wide, wide]
    change_out = call(
        functools.partial(change_kernel, rows),
        ends + full(cotangent, att, act, slope, hidden, vec_all) + parameters,
        [shape(D), shape(FF), shape(D, f32, 8)] + [shape(wide)] * 8,
        weight_scratch(2) + [pltpu.VMEM((count, HID + 2 * FF), bf16)] + weight_sem(2),
        8 * unit_cost,
        8 * rows * D,
    )
    out, dub, vec_first = change_out[:3]
    rows_two = share_rows(change_out[3:7])
    rows_one = share_rows(change_out[7:])

    def product(parts, columns, lane, starts, split=None, which=0, waits=()):
        extra = 0 if starts is not None else vector_pad
        kernel, inputs = after(
            functools.partial(product_kernel, rows, wide, lane, starts, split, which),
            ends + full(*parts) + full(*columns),
            list(waits),
        )
        return call(
            kernel,
            inputs,
            [shape(D, bf16, rows // 4 + extra)] * 2,
            [
                pltpu.VMEM((4 * count, wide), bf16),
                pltpu.VMEM((4 * count, D), bf16),
                pltpu.VMEM((wide, D), bf16),
                pltpu.VMEM((vector_pad, D), f32),
            ],
            8 * count * wide * D,
            4 * rows * D,
        )

    def scatter_rest(parts):
        away, mine = parts
        got = links.swap_bit(away, 1)
        mine = add_bf(mine, got)
        part = rows // 4
        mine, rest = mine[:part], mine[part:]
        for bit in range(2, links.bits):
            size = mine.shape[0] // 2
            away = lax.dynamic_slice_in_dim(mine, (1 - links.bit_of(bit)) * size, size)
            near = lax.dynamic_slice_in_dim(mine, links.bit_of(bit) * size, size)
            mine = add_bf(near, links.swap_bit(away, bit))
            if rest.shape[0]:
                rest = add_bf(rest, links.swap_bit(rest, bit))
        return jnp.concatenate([mine, rest]) if rest.shape[0] else mine

    product_three = product(rows_three, joined_all, 0, [D] * 4)
    three = scatter_rest(product_three)
    kernel, inputs = after(
        functools.partial(hidden_kernel, rows),
        ends + full(dub, hidden, cotangent, vec_all) + parameters,
        product_three[:1],
    )
    dh, dh_bf, da, vec_second = call(
        kernel,
        inputs,
        [shape(D, f32), shape(D), shape(HID), shape(D, f32, 8)],
        weight_scratch(2) + weight_sem(2),
        5 * unit_cost,
        8 * rows * D,
    )
    dh_side = links.swap_bit(dh_bf, 0)
    dh_core = links.swap_core(dh_bf)
    product_two = product(
        rows_two,
        n_two_all + joined_all,
        0,
        n_two_starts + [D] * 4,
        4 * HID + FF - 5 * rows,
        1,
        waits=[vec_second],
    )
    two = scatter_rest(product_two)
    kernel, inputs = after(
        functools.partial(attention_kernel, rows),
        ends + full(da, qkv, probs, dh, tokens, vec_all, vec_first, vec_second) + parameters,
        product_two[:1],
    )
    attention_out = call(
        kernel,
        inputs,
        [shape(D, f32)] + [shape(wide, bf16, count + vector_pad)] * 4,
        weight_scratch(1)
        + [
            pltpu.VMEM((count, 3 * HID), bf16),
            pltpu.VMEM((vector_pad, D), f32),
            pltpu.VMEM((vector_pad, wide), f32),
        ]
        + weight_sem(1),
        4 * unit_cost,
        4 * rows * D,
    )
    grad_tok = attention_out[0]
    rows_zero = share_rows(attention_out[1:])
    three, _ = lax.optimization_barrier((three, grad_tok))
    three = links.to_chip(three, {0: 1, 2: 3})
    dh_side, _ = lax.optimization_barrier((dh_side, grad_tok))
    dh_both = links.swap_core(dh_side)
    dh_all = [dh_bf, dh_core, dh_side, dh_both]
    two, _ = lax.optimization_barrier((two, grad_tok))
    two = links.to_chip(two, {0: 1, 3: 2})
    product_one = product(
        rows_one,
        n_two_all + dh_all,
        0,
        n_two_starts + [0] * 4,
        4 * HID - 2 * rows,
        0,
        waits=[grad_tok],
    )
    one = scatter_rest(product_one)
    product_zero = product(
        rows_zero, [vec_all, n_one] + joined_all[1:], 0, None, waits=product_one[:1]
    )
    zero = scatter_rest(product_zero)
    three = links.to_chip(three, {1: 3})
    two = links.to_chip(two, {1: 2})
    one = links.to_chip(one, {0: 1, 3: 2})
    one = links.to_chip(one, {2: 1})
    zero = links.to_chip(zero, {0: 1, 1: 0, 2: 3, 3: 2})
    zero = links.to_chip(zero, {0: 2, 2: 0})
    mine = jnp.where(links.chip == 1, one, jnp.where(links.chip == 2, two, three))
    size = mine.shape[0]
    mine = jnp.where(links.chip == 0, zero[:size], mine)
    grad_w = links.gather_positions(mine).astype(f32)
    sums = zero[size:]
    got = links.along(sums, {0: 1, 2: 3})
    sums = jnp.where(links.chip % 2 == 0, sums, got).astype(f32)
    width = vectors.shape[1]
    grad_v = lax.dynamic_slice_in_dim(sums, lax.axis_index("shard") * width, width, 1)
    new = [grad_w] + list(adam_update(*state, grad_w, decay_rate))
    return out, grad_tok, grad_v[: vectors.shape[0]], new


def per_device(
    replicas,
    shards,
    tokens,
    segments,
    cotangent,
    weights,
    vectors,
    first_weights,
    first_vectors,
    second_weights,
    second_vectors,
):
    if Links.fits(replicas, shards, weights.shape[0]):
        output, grad_tokens, grad_v, new = direct_step(
            Links(replicas, shards),
            tokens,
            segments,
            cotangent,
            (weights, first_weights, second_weights),
            vectors,
        )
    else:
        w_full = lax.all_gather(weights.astype(jnp.bfloat16), "shard", axis=0, tiled=True)
        v_full = lax.all_gather(vectors.astype(jnp.bfloat16), "shard", axis=1, tiled=True)
        output, kept_state = forward(tokens, segments, w_full, v_full)
        grad_tokens, grad_vec, row_terms, col_terms = backward(
            kept_state, cotangent, segments, w_full
        )
        local_grad = weight_grads(row_terms, col_terms).astype(jnp.bfloat16)
        own_w = lax.psum_scatter(local_grad, "shard", scatter_dimension=0, tiled=True)
        own_v = lax.psum_scatter(
            grad_vec.astype(jnp.bfloat16), "shard", scatter_dimension=1, tiled=True
        )
        grad_w = lax.psum(own_w, "rep").astype(jnp.float32)
        grad_v = lax.psum(own_v, "rep").astype(jnp.float32)
        new = [grad_w]
        new += adam_update(weights, first_weights, second_weights, grad_w, decay_rate)
    grad_w, new_w, new_fw, new_sw = new
    new_v, new_fv, new_sv = adam_update(vectors, first_vectors, second_vectors, grad_v, 0.0)
    return (output, grad_tokens, grad_w, grad_v, new_w, new_v, new_fw, new_fv, new_sw, new_sv)


def solution(mesh):
    placed = (
        P(("rep", "shard"), None),
        P(("rep", "shard"), None),
        P(("rep", "shard"), None),
        P("shard", None),
        P(None, "shard"),
        P("shard", None),
        P(None, "shard"),
        P("shard", None),
        P(None, "shard"),
    )
    return jax.shard_map(
        functools.partial(per_device, mesh.shape["rep"], mesh.shape["shard"]),
        mesh=mesh,
        in_specs=placed,
        out_specs=(
            P(("rep", "shard"), None),
            P(("rep", "shard"), None),
            P("shard", None),
            P(None, "shard"),
            P("shard", None),
            P(None, "shard"),
            P("shard", None),
            P(None, "shard"),
            P("shard", None),
            P(None, "shard"),
        ),
        check_vma=False,
    )
```
